256 devices in a mesh: seq: 32 (over y, z), chan: 8 (over x, core).
Axes of the slice: x: 4, y: 4, z: 8, core: 2. Of those that a mesh axis runs over, the one named last changes fastest.
Arguments:
- targets: int32 [32768], P('seq'), may hold values from 0 to 4
- resid: bfloat16 [32768, 2560], P('seq', 'chan'), may hold values from -6 to 6
- w_gate_in: bfloat16 [2560, 2560], P('seq', 'chan'), may hold values from -0.125 to 0.125
- w_x_in: bfloat16 [2560, 2560], P('seq', 'chan'), may hold values from -0.125 to 0.125
- conv_weight: float32 [4, 2560], P(None, 'chan'), may hold values from -3 to 3
- conv_bias: float32 [2560], P('chan'), may hold values from -3 to 3
- skip_d: float32 [40], P('chan'), may hold values from 0.5 to 2
- norm_gain: float32 [2560], P('chan'), may hold values from 0.1 to 1.9
- w_out: bfloat16 [2560, 2560], P('seq', 'chan'), may hold values from -0.125 to 0.125
- w_head: bfloat16 [2560, 16], P('chan'), may hold values from -0.375 to 0.375
Outputs:
- new_resid: bfloat16 [32768, 2560], P('seq', 'chan')
- grad_gate_in: float32 [2560, 2560], P('seq', 'chan')
- grad_x_in: float32 [2560, 2560], P('seq', 'chan')
- grad_out: float32 [2560, 2560], P('seq', 'chan')
- grad_head: float32 [2560, 16], P('chan')
- grad_conv_weight: float32 [4, 2560], P(None, 'chan')
- grad_conv_bias: float32 [2560], P('chan')
- grad_skip: float32 [40], P('chan')
- grad_gain: float32 [2560], P('chan')
The draws below stay inside these ranges and needn't reach their ends.
All inputs are finite; a program needn't handle non-finite values.
Results may differ from the reference program's by a relative error of at most 0.035.
Values may be sent and summed in bfloat16 or wider, within the bound.
A program may use at most 128 MiB of HBM per device.

```python
import math
import jax
import jax.numpy as jnp
import numpy as np
from jax import lax

DMODEL = 2560
HEADS = 40
HEADDIM = 64
KERNEL = 4
VOCAB = 16
INNER = 2560
TOKENS = 32768
N_CHAN = 8


def with_ends(array, stream_key, smallest, high):
    place = [jax.random.randint(jax.random.fold_in(stream_key, axis), (), 0, length) for axis, length in enumerate(array.shape)]
    longest = array.shape.index(max(array.shape))
    neighbour = place[:longest] + [(place[longest] + 1) % array.shape[longest]] + place[longest + 1:]
    return array.at[tuple(place)].set(smallest).at[tuple(neighbour)].set(high)


def levels(rng, extent, split, least, top_value):
    factor_of, own = 1.0, jax.random.fold_in(rng, 6)
    for position, blocks in split:
        heights = jnp.exp(jax.random.uniform(jax.random.fold_in(own, position), (blocks,), jnp.float32, least / len(split), top_value / len(split)))
        factor_of = factor_of * jnp.repeat(heights, extent[position] // blocks).reshape([-1 if axis == position else 1 for axis in range(len(extent))])
    return factor_of


def cumulative_ranks(count, skew):
    portions = [(1 << 20) // math.isqrt(standing ** skew) + 1 for standing in range(1, count + 1)]
    deviation = 1 + sum(portions) // (1 << 30)
    return np.cumsum(np.array([max(1, weight // deviation) for weight in portions]))


def ranked_ids(rng, dims, count, skew):
    table = cumulative_ranks(count, skew)
    pick = jax.random.randint(jax.random.fold_in(rng, 1), dims, 0, int(table[count - 1]))
    rank = jnp.searchsorted(jnp.asarray(table, jnp.int32), pick, side="right")
    return jax.random.permutation(jax.random.fold_in(rng, 2), count)[rank].astype(jnp.int32)


def scatter_about(rng, extent, spread, reach, shards=(), held_as=jnp.bfloat16):
    result = spread * jax.random.normal(rng, extent, jnp.float32)
    if shards:
        result = result * levels(rng, extent, shards, -0.22, 0.18)
    return jnp.clip(result, -reach, reach).astype(held_as)


def setup_inputs(seed: int = 0) -> dict:
    key_of = jax.random.split(jax.random.key(seed), 11)
    targets = with_ends(ranked_ids(key_of[0], (TOKENS,), 5, 1), jax.random.fold_in(key_of[0], 3), 0, 4).astype(jnp.int32)
    resid = scatter_about(key_of[1], (TOKENS, DMODEL), 1.0, 6.0, ((0, 32), (1, 8)))
    w_gate_in = scatter_about(key_of[2], (DMODEL, INNER), DMODEL ** -0.5, 0.125, ((0, 32), (1, 8)))
    w_x_in = scatter_about(key_of[3], (DMODEL, INNER), DMODEL ** -0.5, 0.125, ((0, 32), (1, 8)))
    conv_weight = scatter_about(key_of[4], (KERNEL, INNER), 0.5, 3.0, ((1, 8),), jnp.float32)
    conv_bias = scatter_about(key_of[5], (INNER,), 0.5, 3.0, ((0, 8),), jnp.float32)
    skip_d = jnp.clip(jnp.exp(math.log(2.0) - 1.3862944 * jax.random.uniform(key_of[6], (HEADS,), jnp.float32) ** levels(key_of[6], (HEADS,), ((0, 8),), -0.2, 0.2)), 0.5, 2.0)
    norm_gain = jnp.clip(1.0 + 0.18 * jax.random.normal(key_of[7], (INNER,), jnp.float32), 0.1, 1.9)
    w_out = scatter_about(key_of[8], (INNER, DMODEL), INNER ** -0.5, 0.125, ((0, 32), (1, 8)))
    w_head = scatter_about(key_of[9], (DMODEL, VOCAB), (DMODEL // 9) ** -0.5, 0.375, ((0, 8),))
    return {"targets": targets, "resid": resid, "w_gate_in": w_gate_in, "w_x_in": w_x_in, "conv_weight": conv_weight, "conv_bias": conv_bias, "skip_d": skip_d, "norm_gain": norm_gain, "w_out": w_out, "w_head": w_head}


def slope(value, sig):
    return sig * (1.0 + value * (1.0 - sig))

def reference(targets, resid, w_gate_in, w_x_in, conv_weight, conv_bias, skip_d, norm_gain, w_out, w_head):
    f32 = jnp.float32
    bf16 = jnp.bfloat16
    halo_rows = KERNEL - 1
    gate_pre = jnp.dot(resid, w_gate_in, preferred_element_type=f32).astype(bf16)
    x_pre = jnp.dot(resid, w_x_in, preferred_element_type=f32).astype(bf16)
    padded = jnp.concatenate([jnp.zeros((halo_rows, INNER), bf16), x_pre], axis=0).astype(f32)
    conv_out = jnp.zeros((TOKENS, INNER), f32) + conv_bias
    for offset in range(KERNEL):
        conv_out = conv_out + conv_weight[offset] * padded[offset:offset + TOKENS]
    sig_conv = jax.nn.sigmoid(conv_out)
    active = conv_out * sig_conv
    gate_f32 = gate_pre.astype(f32)
    sig_gate = jax.nn.sigmoid(gate_f32)
    silu_gate = gate_f32 * sig_gate
    head_scale = jnp.repeat(skip_d, HEADDIM)
    gated = active * head_scale * silu_gate
    inverse = lax.rsqrt(lax.optimization_barrier(jnp.sum(gated * gated, axis=1)) / INNER + 1e-05)
    normed = (gated * inverse[:, None] * norm_gain).astype(bf16)
    new_resid = (resid.astype(f32) + jnp.dot(normed, w_out, preferred_element_type=f32)).astype(bf16)
    logits = jnp.dot(new_resid, w_head, preferred_element_type=f32)
    raised = jnp.exp(logits)
    probs = raised / lax.optimization_barrier(jnp.sum(raised, axis=1, keepdims=True))
    onehot = (targets[:, None] == jnp.arange(VOCAB, dtype=jnp.int32)[None, :]).astype(f32)
    dlogit = (probs - onehot) * (4.0 / jnp.sqrt(jnp.asarray(TOKENS, f32)))
    grad_head = jnp.dot(new_resid.astype(f32).T, dlogit, precision=lax.Precision.HIGHEST)
    dresid = jnp.dot(dlogit, w_head.astype(f32).T, precision=lax.Precision.HIGHEST).astype(bf16)
    grad_out = jnp.dot(normed.T, dresid, preferred_element_type=f32)
    block = DMODEL // N_CHAN
    dnormed = jnp.zeros((TOKENS, INNER), f32)
    for part in range(N_CHAN):
        term = jnp.dot(dresid[:, part * block:(part + 1) * block], w_out[:, part * block:(part + 1) * block].T, preferred_element_type=f32)
        rounded = lax.optimization_barrier(term.astype(bf16))
        dnormed = dnormed + rounded.astype(f32)
    dot_gn = lax.optimization_barrier(jnp.sum(gated * norm_gain * dnormed, axis=1))
    dgated = inverse[:, None] * norm_gain * dnormed - gated * (inverse ** 3 * dot_gn / INNER)[:, None]
    grad_gain = lax.optimization_barrier(jnp.sum(dnormed * gated * inverse[:, None], axis=0))
    grad_skip = lax.optimization_barrier(jnp.sum(dgated * active * silu_gate, axis=0)).reshape(HEADS, HEADDIM).sum(axis=1)
    dgate = (dgated * active * head_scale * slope(gate_f32, sig_gate)).astype(bf16)
    dconv = dgated * head_scale * silu_gate * slope(conv_out, sig_conv)
    grad_conv_bias = lax.optimization_barrier(jnp.sum(dconv, axis=0))
    grad_conv_weight = jnp.stack([lax.optimization_barrier(jnp.sum(dconv * padded[offset:offset + TOKENS], axis=0)) for offset in range(KERNEL)])
    dpadded = jnp.concatenate([dconv, jnp.zeros((halo_rows, INNER), f32)], axis=0)
    dx_sum = jnp.zeros((TOKENS, INNER), f32)
    for offset in range(KERNEL):
        dx_sum = dx_sum + conv_weight[offset] * dpadded[halo_rows - offset:halo_rows - offset + TOKENS]
    dx_pre = dx_sum.astype(bf16)
    grad_gate_in = jnp.dot(resid.T, dgate, preferred_element_type=f32)
    grad_x_in = jnp.dot(resid.T, dx_pre, preferred_element_type=f32)
    return (new_resid, grad_gate_in, grad_x_in, grad_out, grad_head, grad_conv_weight, grad_conv_bias, grad_skip, grad_gain)
```

```python
import jax
import jax.numpy as jnp
from jax import lax
from jax.sharding import PartitionSpec as P

HEADDIM = 64
KERNEL = 4
VOCAB = 16
INNER = 2560


def shifted(array, axis, by):
    length = lax.axis_size(axis)
    pairs = [(i, i + by) for i in range(length) if 0 <= i + by < length]
    return lax.ppermute(array, axis, pairs)


def slope(value, sig):
    return sig * (1.0 + value * (1.0 - sig))


def inner_rows(left, right, precision=None):
    return lax.dot_general(
        left,
        right,
        (((0,), (0,)), ((), ())),
        preferred_element_type=jnp.float32,
        precision=precision,
    )


def per_device(
    targets, resid, w_gate_in, w_x_in, conv_weight, conv_bias, skip_d, norm_gain, w_out, w_head
):
    f32 = jnp.float32
    bf16 = jnp.bfloat16
    exact = lax.Precision.HIGHEST
    tok_rows = resid.shape[0]
    seq_count = lax.axis_size("seq")
    local_inner = w_gate_in.shape[1]
    row_count = w_out.shape[0]
    halo_rows = KERNEL - 1
    mix_part = jnp.dot(w_out, w_head, preferred_element_type=f32)
    mix_rows = lax.psum(mix_part, "chan")
    mix_all = lax.all_gather(mix_rows, "seq", axis=0, tiled=True)
    mix = lax.dynamic_slice_in_dim(
        mix_all, lax.axis_index("chan") * local_inner, local_inner, 0
    )
    features = lax.all_gather(resid, "chan", axis=1, tiled=True)
    w_both = lax.all_gather(
        jnp.concatenate([w_gate_in, w_x_in], axis=1), "seq", axis=0, tiled=True
    )
    both_sum = jnp.dot(features, w_both, preferred_element_type=f32)
    gate_pre = both_sum[:, :local_inner].astype(bf16)
    x_pre = both_sum[:, local_inner:].astype(bf16)
    before = shifted(x_pre[tok_rows - halo_rows :], "seq", 1)
    padded = jnp.concatenate([before, x_pre], axis=0).astype(f32)
    conv_out = jnp.zeros((tok_rows, local_inner), f32) + conv_bias
    for offset in range(KERNEL):
        conv_out = conv_out + conv_weight[offset] * padded[offset : offset + tok_rows]
    sig_conv = jax.nn.sigmoid(conv_out)
    active = conv_out * sig_conv
    gate_f32 = gate_pre.astype(f32)
    sig_gate = jax.nn.sigmoid(gate_f32)
    silu_gate = gate_f32 * sig_gate
    head_scale = jnp.repeat(skip_d, HEADDIM)
    gated = active * head_scale * silu_gate
    gained = gated * norm_gain
    sq_part = jnp.sum(gated * gated, axis=1, keepdims=True)
    head_part = jnp.dot(resid, w_head, preferred_element_type=f32)
    gained_part = jnp.dot(gained, mix, precision=exact)
    stats = lax.psum(jnp.concatenate([head_part, gained_part, sq_part], axis=1), "chan")
    inverse = lax.rsqrt(stats[:, 2 * VOCAB :] / INNER + 1e-05)
    gained_head = stats[:, VOCAB : 2 * VOCAB]
    logits = stats[:, :VOCAB] + inverse * gained_head
    raised = jnp.exp(logits)
    probs = raised / jnp.sum(raised, axis=1, keepdims=True)
    onehot = (targets[:, None] == jnp.arange(VOCAB, dtype=jnp.int32)[None, :]).astype(f32)
    loss_weight = 4.0 / jnp.sqrt(jnp.asarray(tok_rows * seq_count, f32))
    dlogit = (probs - onehot) * loss_weight
    dnormed = jnp.dot(dlogit, mix.T, precision=exact)
    dot_gn = jnp.sum(dlogit * gained_head, axis=1, keepdims=True)
    dgated = inverse * norm_gain * dnormed - gated * (inverse**3 * dot_gn / INNER)
    gain_local = jnp.sum(dnormed * gated * inverse, axis=0)
    skip_local = jnp.sum(dgated * active * silu_gate, axis=0).reshape(-1, HEADDIM).sum(axis=1)
    dgate = (dgated * active * head_scale * slope(gate_f32, sig_gate)).astype(bf16)
    dconv = dgated * head_scale * silu_gate * slope(conv_out, sig_conv)
    bias_local = jnp.sum(dconv, axis=0)
    taps_local = jnp.stack(
        [jnp.sum(dconv * padded[offset : offset + tok_rows], axis=0) for offset in range(KERNEL)]
    )
    future = shifted(dconv[:halo_rows], "seq", -1)
    dpadded = jnp.concatenate([dconv, future], axis=0)
    dx_sum = jnp.zeros((tok_rows, local_inner), f32)
    for offset in range(KERNEL):
        dx_sum = (
            dx_sum
            + conv_weight[offset] * dpadded[halo_rows - offset : halo_rows - offset + tok_rows]
        )
    dx_pre = dx_sum.astype(bf16)
    normed = (gained * inverse).astype(bf16)
    full_normed = lax.all_gather(normed, "chan", axis=1, tiled=True)
    out_cols = lax.all_gather(w_out, "seq", axis=0, tiled=True)
    new_resid = (
        resid.astype(f32) + jnp.dot(full_normed, out_cols, preferred_element_type=f32)
    ).astype(bf16)
    head_local = inner_rows(new_resid.astype(f32), dlogit, exact)
    normed_local = inner_rows(gained * inverse, dlogit, exact)
    both_grads = jnp.concatenate([dgate, dx_pre], axis=1)
    grad_both = lax.psum_scatter(
        inner_rows(features, both_grads).astype(bf16), "seq", scatter_dimension=0, tiled=True
    ).astype(f32)
    grad_gate_in = grad_both[:, :local_inner]
    grad_x_in = grad_both[:, local_inner:]
    grad_head, grad_mix, grad_conv_weight, grad_conv_bias, grad_skip, grad_gain = lax.psum(
        (head_local, normed_local, taps_local, bias_local, skip_local, gain_local), "seq"
    )
    mix_grads = lax.all_gather(grad_mix, "chan", axis=0, tiled=True)
    mix_grad_rows = lax.dynamic_slice_in_dim(
        mix_grads, lax.axis_index("seq") * row_count, row_count, 0
    )
    grad_out = jnp.dot(mix_grad_rows, w_head.astype(f32).T, precision=exact)
    return (
        new_resid,
        grad_gate_in,
        grad_x_in,
        grad_out,
        grad_head,
        grad_conv_weight,
        grad_conv_bias,
        grad_skip,
        grad_gain,
    )


def solution(mesh):
    return jax.shard_map(
        per_device,
        mesh=mesh,
        in_specs=(
            P("seq"),
            P("seq", "chan"),
            P("seq", "chan"),
            P("seq", "chan"),
            P(None, "chan"),
            P("chan"),
            P("chan"),
            P("chan"),
            P("seq", "chan"),
            P("chan", None),
        ),
        out_specs=(
            P("seq", "chan"),
            P("seq", "chan"),
            P("seq", "chan"),
            P("seq", "chan"),
            P("chan", None),
            P(None, "chan"),
            P("chan"),
            P("chan"),
            P("chan"),
        ),
        check_vma=False,
    )
```

```python
import functools

import jax
import jax.numpy as jnp
from jax import lax
from jax.experimental import pallas as pl
from jax.experimental.pallas import tpu as pltpu
from jax.sharding import PartitionSpec as P

HEADDIM = 64
KERNEL = 4
VOCAB = 16
INNER = 2560
NX, NY, NZ = 4, 4, 8
NCHAN = 2 * NX
MESH = pl.DeviceIdType.MESH
VMEM_BYTES = 56 * 1024 * 1024


class Wire:
    def __init__(self, send, recv):
        self.send, self.recv, self.copies = send, recv, []

    def put(self, source, target, **where):
        place = len(self.copies)
        copy = pltpu.make_async_remote_copy(
            src_ref=source,
            dst_ref=target,
            send_sem=self.send.at[place],
            recv_sem=self.recv.at[place],
            device_id=where,
            device_id_type=MESH,
        )
        copy.start()
        self.copies.append(copy)
        return copy

    def finish(self):
        for copy in self.copies:
            copy.wait_send()


def greet(peers):
    barrier = pltpu.get_barrier_semaphore()
    for peer in peers:
        pl.semaphore_signal(barrier, inc=1, device_id=peer, device_id_type=MESH)
    pl.semaphore_wait(barrier, len(peers))


def take_turns(*streams):
    streams = list(streams)
    while streams:
        for stream in list(streams):
            try:
                next(stream)
            except StopIteration:
                streams.remove(stream)


def place():
    s, c = lax.axis_index("seq"), lax.axis_index("chan")
    return s // NZ, s % NZ, c


def gather_chan(wire, shard, full, c, rows):
    x, core = c // 2, c % 2
    mate = c + 1 - 2 * core
    right = lax.rem(x + 1, NX) * 2 + core
    left = lax.rem(x + NX - 1, NX) * 2 + core
    across = lax.rem(x + 2, NX) * 2 + core
    lo, hi = pl.ds(0, rows // 2), pl.ds(rows // 2, rows // 2)
    to_right_lo = wire.put(shard.at[lo], full.at[c, lo], chan=right)
    to_left_hi = wire.put(shard.at[hi], full.at[c, hi], chan=left)
    to_right_hi = wire.put(shard.at[hi], full.at[c, hi], chan=right)
    to_left_lo = wire.put(shard.at[lo], full.at[c, lo], chan=left)
    to_mate = [wire.put(shard, full.at[c], chan=mate)]
    yield
    to_right_lo.wait_recv()
    on_right = wire.put(full.at[left, lo], full.at[left, lo], chan=right)
    to_left_hi.wait_recv()
    on_left = wire.put(full.at[right, hi], full.at[right, hi], chan=left)
    yield
    to_right_hi.wait_recv()
    to_mate.append(wire.put(full.at[left], full.at[left], chan=mate))
    to_left_lo.wait_recv()
    to_mate.append(wire.put(full.at[right], full.at[right], chan=mate))
    yield
    on_right.wait_recv()
    to_mate.append(wire.put(full.at[across, lo], full.at[across, lo], chan=mate))
    on_left.wait_recv()
    to_mate.append(wire.put(full.at[across, hi], full.at[across, hi], chan=mate))
    yield
    for copy in to_mate:
        copy.wait_recv()


def ring_z(wire, first, block, halves, y, z):
    up, down = y * NZ + lax.rem(z + 1, NZ), y * NZ + lax.rem(z + NZ - 1, NZ)
    plus = wire.put(first, block(z), seq=up)
    minus = wire.put(first, block(z), seq=down)
    for step in range(1, NZ // 2):
        last = step == NZ // 2 - 1
        yield
        behind, ahead = lax.rem(z + NZ - step, NZ), lax.rem(z + step, NZ)
        plus.wait_recv()
        moved = halves(behind)[0] if last else block(behind)
        plus = wire.put(moved, moved, seq=up)
        minus.wait_recv()
        moved = halves(ahead)[1] if last else block(ahead)
        minus = wire.put(moved, moved, seq=down)
    yield
    plus.wait_recv()
    minus.wait_recv()


def gather_y_first(wire, shard, full, own, y, z, rows):
    puts = [
        wire.put(shard.at[rows], full.at[y, z, rows], seq=lax.rem(y + d, NY) * NZ + z)
        for d in (1, 3, 2)
    ]
    yield
    own.wait()
    for copy in puts:
        copy.wait_recv()
    yield from ring_z(
        wire,
        full.at[:, z, rows],
        lambda at: full.at[:, at, rows],
        lambda at: (full.at[pl.ds(0, 2), at, rows], full.at[pl.ds(2, 2), at, rows]),
        y,
        z,
    )


def gather_z_first(wire, shard, full, y, z, start, count):
    rows = pl.ds(start, count)
    cut = (count // 32) * 16
    yield from ring_z(
        wire,
        shard.at[rows],
        lambda at: full.at[y, at, rows],
        lambda at: (
            full.at[y, at, pl.ds(start, cut)],
            full.at[y, at, pl.ds(start + cut, count - cut)],
        ),
        y,
        z,
    )
    above, below = lax.rem(y + 1, NY), lax.rem(y + NY - 1, NY)
    up, down = above * NZ + z, below * NZ + z
    lo, hi = pl.ds(0, NZ // 2), pl.ds(NZ // 2, NZ // 2)
    up_lo = wire.put(full.at[y, lo, rows], full.at[y, lo, rows], seq=up)
    down_hi = wire.put(full.at[y, hi, rows], full.at[y, hi, rows], seq=down)
    up_hi = wire.put(full.at[y, hi, rows], full.at[y, hi, rows], seq=up)
    down_lo = wire.put(full.at[y, lo, rows], full.at[y, lo, rows], seq=down)
    yield
    up_lo.wait_recv()
    on_up = wire.put(full.at[below, lo, rows], full.at[below, lo, rows], seq=up)
    down_hi.wait_recv()
    on_down = wire.put(full.at[above, hi, rows], full.at[above, hi, rows], seq=down)
    yield
    for copy in (up_hi, down_lo, on_up, on_down):
        copy.wait_recv()


def gather_kernel(resid, weights, full_resid, full_weights, send, recv, local):
    y, z, c = place()
    x, core = c // 2, c % 2
    greet(
        [{"chan": c + 1 - 2 * core}]
        + [{"chan": lax.rem(x + d, NX) * 2 + core} for d in (1, NX - 1)]
        + [{"seq": lax.rem(y + d, NY) * NZ + z} for d in range(1, NY)]
        + [{"seq": y * NZ + lax.rem(z + d, NZ)} for d in (1, NZ - 1)]
    )
    wire = Wire(send, recv)
    own_weights = pltpu.make_async_copy(weights, full_weights.at[y, z], local.at[0])
    own_resid = pltpu.make_async_copy(resid, full_resid.at[c], local.at[1])
    own_weights.start()
    own_resid.start()
    rows = weights.shape[0]
    take_turns(
        gather_y_first(wire, weights, full_weights, own_weights, y, z, pl.ds(0, 32)),
        gather_z_first(wire, weights, full_weights, y, z, 32, rows - 32),
        gather_chan(wire, resid, full_resid, c, resid.shape[0]),
    )
    own_resid.wait()
    wire.finish()


def gather_all(resid, weights):
    anywhere = pl.BlockSpec(memory_space=pl.ANY)
    copies = 48
    return pl.pallas_call(
        gather_kernel,
        name="gather_all",
        out_shape=(
            jax.ShapeDtypeStruct((NCHAN, *resid.shape), resid.dtype),
            jax.ShapeDtypeStruct((NY, NZ, *weights.shape), weights.dtype),
        ),
        in_specs=[anywhere] * 2,
        out_specs=(anywhere,) * 2,
        scratch_shapes=[
            pltpu.SemaphoreType.DMA((copies,)),
            pltpu.SemaphoreType.DMA((copies,)),
            pltpu.SemaphoreType.DMA((2,)),
        ],
        compiler_params=pltpu.CompilerParams(collective_id=0, has_side_effects=True),
    )(resid, weights)


def stats_kernel(stats, out, parts, total, send, recv):
    c = lax.axis_index("chan")
    greet([{"chan": lax.rem(c + d, NCHAN)} for d in range(1, NCHAN)])
    wire = Wire(send, recv)
    width = total.shape[1]

    def lanes(chan):
        return pl.ds(pl.multiple_of(chan * width, width), width)

    puts = []
    for d in range(1, NCHAN):
        peer = lax.rem(c + d, NCHAN)
        puts.append(wire.put(stats.at[:, lanes(peer)], parts.at[d - 1], chan=peer))
    acc = stats[:, lanes(c)]
    for d in range(1, NCHAN):
        puts[d - 1].wait_recv()
        acc = acc + parts[d - 1]
    total[...] = acc
    out[:, lanes(c)] = acc
    puts = []
    for d in range(1, NCHAN):
        puts.append(wire.put(total, out.at[:, lanes(c)], chan=lax.rem(c + d, NCHAN)))
    for copy in puts:
        copy.wait_recv()
    wire.finish()


def sum_stats(stats):
    rows, tokens = stats.shape
    vmem = pl.BlockSpec(memory_space=pltpu.VMEM)
    copies = 2 * (NCHAN - 1)
    return pl.pallas_call(
        stats_kernel,
        name="sum_stats",
        out_shape=jax.ShapeDtypeStruct(stats.shape, stats.dtype),
        in_specs=[vmem],
        out_specs=vmem,
        scratch_shapes=[
            pltpu.VMEM((NCHAN - 1, rows, tokens // NCHAN), stats.dtype),
            pltpu.VMEM((rows, tokens // NCHAN), stats.dtype),
            pltpu.SemaphoreType.DMA((copies,)),
            pltpu.SemaphoreType.DMA((copies,)),
        ],
        compiler_params=pltpu.CompilerParams(collective_id=1, has_side_effects=True),
    )(stats)


def scatter_seq(wire, grads, bufs, out, y, z, start, count):
    f32, bf16 = jnp.float32, jnp.bfloat16
    from_below, from_above, via_up, via_down, got_below, got_above, lines, got_z = bufs
    rows = pl.ds(start, count)
    lo, hi = pl.ds(0, NZ // 2), pl.ds(NZ // 2, NZ // 2)
    above, below, across = lax.rem(y + 1, NY), lax.rem(y + 3, NY), lax.rem(y + 2, NY)
    up, down = above * NZ + z, below * NZ + z
    half_up = wire.put(grads.at[across, lo, rows], from_below.at[:, rows], seq=up)
    half_down = wire.put(grads.at[across, hi, rows], from_above.at[:, rows], seq=down)
    moves = [
        wire.put(grads.at[above, hi, rows], got_below.at[hi, rows], seq=up),
        wire.put(grads.at[below, lo, rows], got_above.at[lo, rows], seq=down),
    ]
    yield
    half_up.wait_recv()
    via_up[:, rows] = (
        grads[above, lo, rows].astype(f32) + from_below[:, rows].astype(f32)
    ).astype(bf16)
    moves.append(wire.put(via_up.at[:, rows], got_below.at[lo, rows], seq=up))
    half_down.wait_recv()
    via_down[:, rows] = (
        grads[below, hi, rows].astype(f32) + from_above[:, rows].astype(f32)
    ).astype(bf16)
    moves.append(wire.put(via_down.at[:, rows], got_above.at[hi, rows], seq=down))
    yield
    for copy in moves:
        copy.wait_recv()
    lines[:, rows] = (
        grads[y, :, rows].astype(f32)
        + got_below[:, rows].astype(f32)
        + got_above[:, rows].astype(f32)
    ).astype(bf16)
    puts = []
    for d in range(1, NZ):
        peer = lax.rem(z + d, NZ)
        puts.append(wire.put(lines.at[peer, rows], got_z.at[d - 1, rows], seq=y * NZ + peer))
    yield
    acc = (
        grads[y, z, rows].astype(f32)
        + got_below[z, rows].astype(f32)
        + got_above[z, rows].astype(f32)
    )
    for d in range(1, NZ):
        puts[d - 1].wait_recv()
        acc = acc + got_z[d - 1, rows].astype(f32)
    out[rows] = acc


def sum_small(wire, small, got_y, part, got_z, total, heads, y, z, c):
    puts = [
        wire.put(small, got_y.at[y], seq=lax.rem(y + d, NY) * NZ + z) for d in range(1, NY)
    ]
    got_y[y] = small[...]
    yield
    for copy in puts:
        copy.wait_recv()
    acc = got_y[0]
    for at in range(1, NY):
        acc = acc + got_y[at]
    part[...] = acc
    puts = [
        wire.put(part, got_z.at[z], seq=y * NZ + lax.rem(z + d, NZ)) for d in range(1, NZ)
    ]
    got_z[z] = acc
    yield
    for copy in puts:
        copy.wait_recv()
    acc = got_z[0]
    for at in range(1, NZ):
        acc = acc + got_z[at]
    total[...] = acc
    first = pl.ds(0, VOCAB)
    puts = [
        wire.put(total.at[first], heads.at[c], chan=lax.rem(c + d, NCHAN))
        for d in range(1, NCHAN)
    ]
    heads[c] = total[first]
    yield
    for copy in puts:
        copy.wait_recv()


def grads_kernel(
    grads, small, gained, out, total, heads, full_gained, *scratch
):
    *bufs, small_y, small_part, small_z, send, recv, local = scratch
    y, z, c = place()
    greet(
        [{"chan": lax.rem(c + d, NCHAN)} for d in range(1, NCHAN)]
        + [{"seq": lax.rem(y + d, NY) * NZ + z} for d in range(1, NY)]
        + [{"seq": y * NZ + lax.rem(z + d, NZ)} for d in range(1, NZ)]
    )
    wire = Wire(send, recv)
    own = pltpu.make_async_copy(gained, full_gained.at[c], local.at[0])
    own.start()
    rows = out.shape[0]
    take_turns(
        sum_small(wire, small, small_y, small_part, small_z, total, heads, y, z, c),
        scatter_seq(wire, grads, bufs, out, y, z, 0, 48),
        scatter_seq(wire, grads, bufs, out, y, z, 48, rows - 48),
        gather_chan(wire, gained, full_gained, c, gained.shape[0]),
    )
    own.wait()
    wire.finish()


def finish_grads(grads, small, gained):
    f32, bf16 = jnp.float32, jnp.bfloat16
    anywhere = pl.BlockSpec(memory_space=pl.ANY)
    vmem = pl.BlockSpec(memory_space=pltpu.VMEM)
    _, _, rows, cols = grads.shape
    copies = 64
    half = (NZ // 2, rows, cols)
    line = (NZ, rows, cols)
    return pl.pallas_call(
        grads_kernel,
        name="finish_grads",
        out_shape=(
            jax.ShapeDtypeStruct((rows, cols), f32),
            jax.ShapeDtypeStruct(small.shape, f32),
            jax.ShapeDtypeStruct((NCHAN, VOCAB, small.shape[1]), f32),
            jax.ShapeDtypeStruct((NCHAN, *gained.shape), bf16),
        ),
        in_specs=[vmem, vmem, anywhere],
        out_specs=(vmem, vmem, vmem, anywhere),
        scratch_shapes=[pltpu.VMEM(half, bf16)] * 4
        + [pltpu.VMEM(line, bf16)] * 3
        + [
            pltpu.VMEM((NZ - 1, rows, cols), bf16),
            pltpu.VMEM((NY, *small.shape), f32),
            pltpu.VMEM(small.shape, f32),
            pltpu.VMEM((NZ, *small.shape), f32),
            pltpu.SemaphoreType.DMA((copies,)),
            pltpu.SemaphoreType.DMA((copies,)),
            pltpu.SemaphoreType.DMA((1,)),
        ],
        compiler_params=pltpu.CompilerParams(
            collective_id=2, has_side_effects=True, vmem_limit_bytes=VMEM_BYTES
        ),
    )(grads, small, gained)


def stacked_kernel(first, left, right, out):
    depth, width = left.shape[2], out.shape[1]
    acc = jnp.zeros(out.shape, jnp.float32)
    for at in range(left.shape[0]):
        acc = acc + jnp.dot(
            left[at],
            right[pl.ds(at * depth, depth), pl.ds(first, width)],
            preferred_element_type=jnp.float32,
        )
    out[...] = acc.astype(out.dtype)


def stacked_dot(left, right, first, width, dtype):
    parts, tokens, depth = left.shape
    tile = 256
    return pl.pallas_call(
        functools.partial(stacked_kernel, first),
        name="stacked_dot",
        grid=(tokens // tile,),
        out_shape=jax.ShapeDtypeStruct((tokens, width), dtype),
        in_specs=[
            pl.BlockSpec((parts, tile, depth), lambda i: (0, i, 0)),
            pl.BlockSpec(right.shape, lambda i: (0, 0), pipeline_mode=pl.Buffered(1)),
        ],
        out_specs=pl.BlockSpec((tile, width), lambda i: (i, 0)),
        compiler_params=pltpu.CompilerParams(vmem_limit_bytes=VMEM_BYTES),
    )(left, right)


def outer_kernel(left, right, out):
    out[0] = lax.dot_general(
        left[0], right[...], (((0,), (0,)), ((), ())), preferred_element_type=jnp.float32
    ).astype(out.dtype)


def stacked_outer(left, right):
    parts, tokens, depth = left.shape
    width = right.shape[1]
    return pl.pallas_call(
        outer_kernel,
        name="stacked_outer",
        grid=(parts,),
        out_shape=jax.ShapeDtypeStruct((parts, depth, width), jnp.bfloat16),
        in_specs=[
            pl.BlockSpec((1, tokens, depth), lambda i: (i, 0, 0)),
            pl.BlockSpec(right.shape, lambda i: (0, 0), pipeline_mode=pl.Buffered(1)),
        ],
        out_specs=pl.BlockSpec((1, depth, width), lambda i: (i, 0, 0)),
        compiler_params=pltpu.CompilerParams(vmem_limit_bytes=VMEM_BYTES),
    )(left, right)


def shifted(array, axis, by):
    length = lax.axis_size(axis)
    pairs = [(i, i + by) for i in range(length) if 0 <= i + by < length]
    return lax.ppermute(array, axis, pairs)


def slope(value, sig):
    return sig * (1.0 + value * (1.0 - sig))


def inner_rows(left, right, precision=None):
    return lax.dot_general(
        left,
        right,
        (((0,), (0,)), ((), ())),
        preferred_element_type=jnp.float32,
        precision=precision,
    )


def per_device(
    targets, resid, w_gate_in, w_x_in, conv_weight, conv_bias, skip_d, norm_gain, w_out, w_head
):
    f32 = jnp.float32
    bf16 = jnp.bfloat16
    exact = lax.Precision.HIGHEST
    tok_rows = resid.shape[0]
    seq_count = lax.axis_size("seq")
    local_inner = w_gate_in.shape[1]
    row_count = w_out.shape[0]
    halo_rows = KERNEL - 1
    mix_part = lax.psum(jnp.dot(w_out, w_head, preferred_element_type=f32), "chan")
    mix_hi = mix_part.astype(bf16)
    mix_lo = (mix_part - mix_hi.astype(f32)).astype(bf16)
    spare = jnp.zeros((row_count, 2 * VOCAB), bf16)
    shard = jnp.concatenate([w_gate_in, w_x_in, w_out, mix_hi, mix_lo, spare], axis=1)
    features, full = gather_all(resid, shard)
    full = full.reshape(INNER, shard.shape[1])
    mix_at = 3 * local_inner
    mix_rows = lax.dynamic_slice(
        full, (lax.axis_index("chan") * local_inner, mix_at), (local_inner, 2 * VOCAB)
    ).astype(f32)
    mix = mix_rows[:, :VOCAB] + mix_rows[:, VOCAB:]
    both_pre = stacked_dot(features, full, 0, 2 * local_inner, bf16)
    gate_pre = both_pre[:, :local_inner]
    x_pre = both_pre[:, local_inner:]
    before = shifted(x_pre[tok_rows - halo_rows :], "seq", 1)
    padded = jnp.concatenate([before, x_pre], axis=0).astype(f32)
    conv_out = jnp.zeros((tok_rows, local_inner), f32) + conv_bias
    for offset in range(KERNEL):
        conv_out = conv_out + conv_weight[offset] * padded[offset : offset + tok_rows]
    sig_conv = jax.nn.sigmoid(conv_out)
    active = conv_out * sig_conv
    gate_f32 = gate_pre.astype(f32)
    sig_gate = jax.nn.sigmoid(gate_f32)
    silu_gate = gate_f32 * sig_gate
    head_scale = jnp.repeat(skip_d, HEADDIM)
    gated = active * head_scale * silu_gate
    gained = gated * norm_gain
    sq_part = jnp.sum(gated * gated, axis=1)[None, :]
    head_part = lax.dot_general(
        w_head, resid, (((0,), (1,)), ((), ())), preferred_element_type=f32
    )
    gained_part = lax.dot_general(
        mix, gained, (((0,), (1,)), ((), ())), precision=exact, preferred_element_type=f32
    )
    stats = sum_stats(
        jnp.concatenate([head_part, gained_part, sq_part, jnp.zeros((7, tok_rows), f32)], axis=0)
    )
    inverse_row = lax.rsqrt(stats[2 * VOCAB : 2 * VOCAB + 1] / INNER + 1e-05)
    gained_head = stats[VOCAB : 2 * VOCAB]
    logits = stats[:VOCAB] + inverse_row * gained_head
    raised = jnp.exp(logits)
    probs = raised / jnp.sum(raised, axis=0, keepdims=True)
    onehot = (targets[None, :] == jnp.arange(VOCAB, dtype=jnp.int32)[:, None]).astype(f32)
    loss_weight = 4.0 / jnp.sqrt(jnp.asarray(tok_rows * seq_count, f32))
    dlogit_t = (probs - onehot) * loss_weight
    dot_row = jnp.sum(dlogit_t * gained_head, axis=0, keepdims=True)
    per_token = jnp.concatenate(
        [dlogit_t, inverse_row, inverse_row**3 * dot_row / INNER], axis=0
    ).T
    dlogit = per_token[:, :VOCAB]
    inverse = per_token[:, VOCAB : VOCAB + 1]
    pull = per_token[:, VOCAB + 1 :]
    dnormed = jnp.dot(dlogit, mix.T, precision=exact)
    dgated = inverse * norm_gain * dnormed - gated * pull
    gain_local = jnp.sum(dnormed * gated * inverse, axis=0)
    skip_local = jnp.sum(dgated * active * silu_gate, axis=0)
    dgate = (dgated * active * head_scale * slope(gate_f32, sig_gate)).astype(bf16)
    dconv = dgated * head_scale * silu_gate * slope(conv_out, sig_conv)
    bias_local = jnp.sum(dconv, axis=0)
    taps_local = jnp.stack(
        [jnp.sum(dconv * padded[offset : offset + tok_rows], axis=0) for offset in range(KERNEL)]
    )
    future = shifted(dconv[:halo_rows], "seq", -1)
    dpadded = jnp.concatenate([dconv, future], axis=0)
    dx_sum = jnp.zeros((tok_rows, local_inner), f32)
    for offset in range(KERNEL):
        dx_sum = (
            dx_sum
            + conv_weight[offset] * dpadded[halo_rows - offset : halo_rows - offset + tok_rows]
        )
    dx_pre = dx_sum.astype(bf16)
    head_local = jnp.dot(dlogit_t, resid.astype(f32), precision=exact)
    normed_local = jnp.dot(dlogit_t * inverse_row, gained, precision=exact)
    small = jnp.concatenate(
        [
            normed_local,
            head_local,
            taps_local,
            bias_local[None],
            gain_local[None],
            skip_local[None],
            jnp.zeros((1, local_inner), f32),
        ],
        axis=0,
    )
    both_grads = jnp.concatenate([dgate, dx_pre], axis=1)
    grads = stacked_outer(features, both_grads).reshape(NY, NZ, row_count, 2 * local_inner)
    grad_both, total, mix_grads, full_gained = finish_grads(grads, small, gained.astype(bf16))
    grad_gate_in = grad_both[:, :local_inner]
    grad_x_in = grad_both[:, local_inner:]
    at = 2 * VOCAB
    grad_conv_weight = total[at : at + KERNEL]
    grad_conv_bias = total[at + KERNEL]
    grad_gain = total[at + KERNEL + 1]
    grad_skip = total[at + KERNEL + 2].reshape(-1, HEADDIM).sum(axis=1)
    out_sum = stacked_dot(full_gained, full, 2 * local_inner, local_inner, f32)
    new_resid = (resid.astype(f32) + inverse * out_sum).astype(bf16)
    mix_grads = mix_grads.transpose(1, 0, 2).reshape(VOCAB, INNER)
    out_cols = full[:, 2 * local_inner : 3 * local_inner]
    grad_head = total[VOCAB : 2 * VOCAB].T + inner_rows(
        out_cols.astype(f32), mix_grads.T, exact
    )
    mix_grad_rows = lax.dynamic_slice_in_dim(
        mix_grads, lax.axis_index("seq") * row_count, row_count, 1
    )
    grad_out = inner_rows(mix_grad_rows, w_head.astype(f32).T, exact)
    return (
        new_resid,
        grad_gate_in,
        grad_x_in,
        grad_out,
        grad_head,
        grad_conv_weight,
        grad_conv_bias,
        grad_skip,
        grad_gain,
    )


def solution(mesh):
    return jax.shard_map(
        per_device,
        mesh=mesh,
        in_specs=(
            P("seq"),
            P("seq", "chan"),
            P("seq", "chan"),
            P("seq", "chan"),
            P(None, "chan"),
            P("chan"),
            P("chan"),
            P("chan"),
            P("seq", "chan"),
            P("chan", None),
        ),
        out_specs=(
            P("seq", "chan"),
            P("seq", "chan"),
            P("seq", "chan"),
            P("seq", "chan"),
            P("chan", None),
            P(None, "chan"),
            P("chan"),
            P("chan"),
            P("chan"),
        ),
        check_vma=False,
    )
```

```python
import functools

import jax
import jax.numpy as jnp
from jax import lax
from jax.experimental import pallas as pl
from jax.experimental.pallas import tpu as pltpu
from jax.sharding import PartitionSpec as P

HEADDIM = 64
KERNEL = 4
VOCAB = 16
INNER = 2560
NX, NY, NZ = 4, 4, 8
NCHAN = 2 * NX
MESH = pl.DeviceIdType.MESH
VMEM_BYTES = 56 * 1024 * 1024


class Wire:
    def __init__(self, send, recv):
        self.send, self.recv, self.copies = send, recv, []

    def put(self, source, target, **where):
        place = len(self.copies)
        copy = pltpu.make_async_remote_copy(
            src_ref=source,
            dst_ref=target,
            send_sem=self.send.at[place],
            recv_sem=self.recv.at[place],
            device_id=where,
            device_id_type=MESH,
        )
        copy.start()
        self.copies.append(copy)
        return copy

    def finish(self):
        for copy in self.copies:
            copy.wait_send()


def greet(peers):
    barrier = pltpu.get_barrier_semaphore()
    for peer in peers:
        pl.semaphore_signal(barrier, inc=1, device_id=peer, device_id_type=MESH)
    pl.semaphore_wait(barrier, len(peers))


def in_order(*streams):
    for stream in streams:
        next(stream, None)


def place():
    s, c = lax.axis_index("seq"), lax.axis_index("chan")
    return s // NZ, s % NZ, c


def gather_chan(wire, shard, full, c, rows):
    x, core = c // 2, c % 2
    mate = c + 1 - 2 * core
    right = lax.rem(x + 1, NX) * 2 + core
    left = lax.rem(x + NX - 1, NX) * 2 + core
    across = lax.rem(x + 2, NX) * 2 + core
    lo, hi = pl.ds(0, rows // 2), pl.ds(rows // 2, rows // 2)
    to_right_lo = wire.put(shard.at[lo], full.at[c, lo], chan=right)
    to_left_hi = wire.put(shard.at[hi], full.at[c, hi], chan=left)
    to_right_hi = wire.put(shard.at[hi], full.at[c, hi], chan=right)
    to_left_lo = wire.put(shard.at[lo], full.at[c, lo], chan=left)
    to_mate = [wire.put(shard, full.at[c], chan=mate)]
    yield
    to_right_lo.wait_recv()
    on_right = wire.put(full.at[left, lo], full.at[left, lo], chan=right)
    to_left_hi.wait_recv()
    on_left = wire.put(full.at[right, hi], full.at[right, hi], chan=left)
    yield
    to_right_hi.wait_recv()
    to_mate.append(wire.put(full.at[left], full.at[left], chan=mate))
    to_left_lo.wait_recv()
    to_mate.append(wire.put(full.at[right], full.at[right], chan=mate))
    yield
    on_right.wait_recv()
    to_mate.append(wire.put(full.at[across, lo], full.at[across, lo], chan=mate))
    on_left.wait_recv()
    to_mate.append(wire.put(full.at[across, hi], full.at[across, hi], chan=mate))
    yield
    for copy in to_mate:
        copy.wait_recv()


def ring_z(wire, first, block, halves, y, z):
    up, down = y * NZ + lax.rem(z + 1, NZ), y * NZ + lax.rem(z + NZ - 1, NZ)
    plus = wire.put(first, block(z), seq=up)
    minus = wire.put(first, block(z), seq=down)
    for step in range(1, NZ // 2):
        last = step == NZ // 2 - 1
        yield
        behind, ahead = lax.rem(z + NZ - step, NZ), lax.rem(z + step, NZ)
        plus.wait_recv()
        moved = halves(behind)[0] if last else block(behind)
        plus = wire.put(moved, moved, seq=up)
        minus.wait_recv()
        moved = halves(ahead)[1] if last else block(ahead)
        minus = wire.put(moved, moved, seq=down)
    yield
    plus.wait_recv()
    minus.wait_recv()


def exchange_y(wire, shard, full, y, z, rows):
    puts = [
        wire.put(shard.at[rows], full.at[y, z, rows], seq=lax.rem(y + d, NY) * NZ + z)
        for d in (1, 3, 2)
    ]
    yield
    for copy in puts:
        copy.wait_recv()


def ring_z_columns(wire, full, y, z, rows):
    yield from ring_z(
        wire,
        full.at[:, z, rows],
        lambda at: full.at[:, at, rows],
        lambda at: (full.at[pl.ds(0, 2), at, rows], full.at[pl.ds(2, 2), at, rows]),
        y,
        z,
    )


def ring_z_own(wire, shard, full, y, z, start, count):
    cut = (count // 32) * 16
    yield from ring_z(
        wire,
        shard.at[pl.ds(start, count)],
        lambda at: full.at[y, at, pl.ds(start, count)],
        lambda at: (
            full.at[y, at, pl.ds(start, cut)],
            full.at[y, at, pl.ds(start + cut, count - cut)],
        ),
        y,
        z,
    )


def exchange_y_lines(wire, full, y, z, rows):
    above, below = lax.rem(y + 1, NY), lax.rem(y + NY - 1, NY)
    up, down = above * NZ + z, below * NZ + z
    lo, hi = pl.ds(0, NZ // 2), pl.ds(NZ // 2, NZ // 2)
    up_lo = wire.put(full.at[y, lo, rows], full.at[y, lo, rows], seq=up)
    down_hi = wire.put(full.at[y, hi, rows], full.at[y, hi, rows], seq=down)
    up_hi = wire.put(full.at[y, hi, rows], full.at[y, hi, rows], seq=up)
    down_lo = wire.put(full.at[y, lo, rows], full.at[y, lo, rows], seq=down)
    yield
    up_lo.wait_recv()
    on_up = wire.put(full.at[below, lo, rows], full.at[below, lo, rows], seq=up)
    down_hi.wait_recv()
    on_down = wire.put(full.at[above, hi, rows], full.at[above, hi, rows], seq=down)
    yield
    for copy in (up_hi, down_lo, on_up, on_down):
        copy.wait_recv()


def gather_mix(wire, w_out, w_head, out, bufs, y, z, c):
    part, got_c, mine, line, picked = bufs
    rows = w_out.shape[0]
    part[...] = jnp.zeros_like(part)
    part[:, pl.ds(0, rows)] = lax.dot_general(
        w_head[...],
        w_out[...],
        (((1,), (1,)), ((), ())),
        preferred_element_type=jnp.float32,
    )
    puts = [
        wire.put(part, got_c.at[d - 1], chan=lax.rem(c + d, NCHAN)) for d in range(1, NCHAN)
    ]
    yield
    acc = part[...]
    for d in range(1, NCHAN):
        puts[d - 1].wait_recv()
        acc = acc + got_c[d - 1]
    mine[...] = acc
    line[z] = acc
    puts = [
        wire.put(mine, line.at[z], seq=y * NZ + lax.rem(z + d, NZ)) for d in range(1, NZ)
    ]
    yield
    for copy in puts:
        copy.wait_recv()
    kept = pl.ds((c % 2) * (NZ // 2), NZ // 2)
    puts = [
        wire.put(line.at[kept], picked.at[y], seq=lax.rem(y + d, NY) * NZ + z)
        for d in range(1, NY)
    ]
    picked[y] = line[kept]
    yield
    for copy in puts:
        copy.wait_recv()
    for at in range(NZ // 2):
        out[:, pl.ds(at * rows, rows)] = picked[c // 2, at][:, :rows]


def gather_kernel(
    resid, weights, w_out, w_head, full_resid, full_weights, mix, *scratch
):
    *mix_bufs, send, recv, local = scratch
    y, z, c = place()
    greet(
        [{"chan": lax.rem(c + d, NCHAN)} for d in range(1, NCHAN)]
        + [{"seq": lax.rem(y + d, NY) * NZ + z} for d in range(1, NY)]
        + [{"seq": y * NZ + lax.rem(z + d, NZ)} for d in range(1, NZ)]
    )
    wire = Wire(send, recv)
    own_weights = pltpu.make_async_copy(weights, full_weights.at[y, z], local.at[0])
    own_resid = pltpu.make_async_copy(resid, full_resid.at[c], local.at[1])
    own_weights.start()
    own_resid.start()
    rows, first = weights.shape[0], 32
    one, rest = pl.ds(0, first), pl.ds(first, rows - first)
    b_ring = ring_z_own(wire, weights, full_weights, y, z, first, rows - first)
    b_lines = exchange_y_lines(wire, full_weights, y, z, rest)
    a_own = exchange_y(wire, weights, full_weights, y, z, one)
    a_ring = ring_z_columns(wire, full_weights, y, z, one)
    chans = gather_chan(wire, resid, full_resid, c, resid.shape[0])
    mixes = gather_mix(wire, w_out, w_head, mix, mix_bufs, y, z, c)
    in_order(b_ring, a_own, chans, mixes, b_ring, a_own, mixes, b_ring, mixes, b_ring)
    own_weights.wait()
    in_order(b_ring, b_lines, a_ring, mixes, chans, a_ring, chans, a_ring, b_lines)
    in_order(a_ring, chans, a_ring, b_lines, chans)
    own_resid.wait()
    wire.finish()


def gather_all(resid, weights, w_out, w_head):
    anywhere = pl.BlockSpec(memory_space=pl.ANY)
    vmem = pl.BlockSpec(memory_space=pltpu.VMEM)
    f32 = jnp.float32
    copies = 64
    block = (VOCAB, 128)
    return pl.pallas_call(
        gather_kernel,
        name="gather_all",
        out_shape=(
            jax.ShapeDtypeStruct((NCHAN, *resid.shape), resid.dtype),
            jax.ShapeDtypeStruct((NY, NZ, *weights.shape), weights.dtype),
            jax.ShapeDtypeStruct((VOCAB, resid.shape[1]), f32),
        ),
        in_specs=[anywhere] * 2 + [vmem] * 2,
        out_specs=(anywhere, anywhere, vmem),
        scratch_shapes=[
            pltpu.VMEM(block, f32),
            pltpu.VMEM((NCHAN - 1, *block), f32),
            pltpu.VMEM(block, f32),
            pltpu.VMEM((NZ, *block), f32),
            pltpu.VMEM((NY, NZ // 2, *block), f32),
            pltpu.SemaphoreType.DMA((copies,)),
            pltpu.SemaphoreType.DMA((copies,)),
            pltpu.SemaphoreType.DMA((2,)),
        ],
        compiler_params=pltpu.CompilerParams(collective_id=0, has_side_effects=True),
        cost_estimate=pl.CostEstimate(flops=10**10, bytes_accessed=10**8, transcendentals=0),
    )(resid, weights, w_out, w_head)


EXACT = lax.Precision.HIGHEST
LANES = 128
EDGE = 16
SUMS = 40
FACTS = 24


def middle_kernel(
    gate,
    xs,
    resid,
    head_t,
    mix_t,
    params,
    targets,
    dgate,
    dx,
    small,
    gained,
    facts,
    padded,
    prods,
    to_gate,
    to_conv,
    sums,
    parts,
    mine,
    before,
    after,
    acc_rows,
    acc_heads,
    send,
    recv,
):
    f32, bf16 = jnp.float32, jnp.bfloat16
    tokens = gate.shape[0]
    y, z, c = place()
    s = y * NZ + z
    last_seq = NY * NZ - 1
    later, sooner = lax.rem(s + 1, NY * NZ), lax.rem(s + last_seq, NY * NZ)
    greet(
        [{"chan": lax.rem(c + d, NCHAN)} for d in range(1, NCHAN)]
        + [{"seq": later}, {"seq": sooner}]
    )

    def copy_of(source, target, at, where):
        return pltpu.make_async_remote_copy(
            src_ref=source,
            dst_ref=target,
            send_sem=send.at[at],
            recv_sem=recv.at[at],
            device_id=where,
            device_id_type=MESH,
        )

    edge = copy_of(xs.at[pl.ds(tokens - EDGE, EDGE)], before, 2 * NCHAN, {"seq": later})
    edge.start()
    taps = [params[k : k + 1, :] for k in range(KERNEL)]
    bias, skip, gain = params[4:5, :], params[5:6, :], params[6:7, :]
    mix = mix_t[...]
    padded[pl.ds(EDGE, tokens), :] = xs[...].astype(f32)

    def window(tile):
        start = pl.multiple_of(tile * LANES, LANES)
        return pl.ds(start, LANES), padded[pl.ds(start, LANES + EDGE), :]

    def shifted(win, k):
        first = EDGE - (KERNEL - 1) + k
        return win[first : first + LANES]

    def share(step):
        peer = lax.rem(c + 1 + step, NCHAN)
        return copy_of(sums.at[peer], parts.at[step], step, {"chan": peer})

    def forward(tile):
        rows, win = window(tile)
        conv = bias + taps[0] * shifted(win, 0)
        for k in range(1, KERNEL):
            conv = conv + taps[k] * shifted(win, k)
        sig_conv = jax.nn.sigmoid(conv)
        active = conv * sig_conv
        gate_pre = gate[rows, :].astype(f32)
        sig_gate = jax.nn.sigmoid(gate_pre)
        silu_gate = gate_pre * sig_gate
        prod = active * silu_gate
        prods[rows, :] = prod
        to_gate[rows, :] = skip * active * slope(gate_pre, sig_gate)
        to_conv[rows, :] = skip * silu_gate * slope(conv, sig_conv)
        gated = prod * skip
        with_gain = gated * gain
        gained[rows, :] = with_gain.astype(bf16)
        by_lanes = (((1,), (1,)), ((), ()))
        sums[tile, pl.ds(0, VOCAB)] = lax.dot_general(
            head_t[...], resid[rows, :], by_lanes, preferred_element_type=f32
        )
        sums[tile, pl.ds(VOCAB, VOCAB)] = lax.dot_general(
            mix, with_gain, by_lanes, precision=EXACT, preferred_element_type=f32
        )
        sums[tile, pl.ds(2 * VOCAB, 8)] = lax.dot_general(
            jnp.ones((8, gated.shape[1]), f32),
            gated * gated,
            by_lanes,
            precision=EXACT,
            preferred_element_type=f32,
        )

    edge.wait_recv()
    padded[pl.ds(0, EDGE), :] = before[...].astype(f32) * (s > 0).astype(f32)

    def forward_step(step, carry):
        forward(lax.rem(c + 1 + step, NCHAN))
        share(step).start()
        return carry

    lax.fori_loop(0, NCHAN - 1, forward_step, 0)
    forward(c)
    total = sums[c]
    for step in range(NCHAN - 1):
        share(step).wait_recv()
        total = total + parts[step]
    inverse = lax.rsqrt(total[2 * VOCAB : 2 * VOCAB + 1] / INNER + 1e-05)
    gained_head = total[VOCAB : 2 * VOCAB]
    raised = jnp.exp(total[:VOCAB] + inverse * gained_head)
    probs = raised / jnp.sum(raised, axis=0, keepdims=True)
    words = lax.broadcasted_iota(jnp.int32, (VOCAB, LANES), 0)
    onehot = (words == targets[c]).astype(f32)
    weight = 4.0 / float(tokens * NY * NZ) ** 0.5
    dlogit = (probs - onehot) * weight
    dot_gn = jnp.sum(dlogit * gained_head, axis=0, keepdims=True)
    mine[pl.ds(0, VOCAB), :] = dlogit
    mine[pl.ds(VOCAB, 8), :] = jnp.concatenate(
        [inverse, inverse * inverse * inverse * dot_gn / INNER, jnp.zeros((6, LANES), f32)],
        axis=0,
    )
    facts[c] = mine[...]

    def tell(d):
        return copy_of(
            mine, facts.at[c], NCHAN - 1 + d, {"chan": lax.rem(c + d, NCHAN)}
        )

    for d in range(1, NCHAN):
        tell(d).start()
    acc_rows[...] = jnp.zeros_like(acc_rows)
    acc_heads[...] = jnp.zeros_like(acc_heads)
    for d in range(1, NCHAN):
        tell(d).wait_recv()
    second = (
        lax.broadcasted_iota(jnp.int32, (8, mix.shape[1]), 0) == 1
    ).astype(f32)

    def fold(value):
        return jnp.sum(value.reshape(LANES // 8, 8, value.shape[1]), axis=0)

    def backward(tile):
        rows, win = window(tile)
        fact = facts[tile]
        dlogit = fact[:VOCAB]
        scaled = dlogit * fact[VOCAB : VOCAB + 1]
        by_rows = (((0,), (0,)), ((), ()))
        dnormed = lax.dot_general(
            scaled, mix, by_rows, precision=EXACT, preferred_element_type=f32
        )
        pull = lax.dot_general(
            fact[VOCAB : VOCAB + 8], second, by_rows, precision=EXACT, preferred_element_type=f32
        )
        prod = prods[rows, :]
        dgated = gain * dnormed - skip * prod * pull
        dgate[rows, :] = (dgated * to_gate[rows, :]).astype(bf16)
        dconv = dgated * to_conv[rows, :]
        to_conv[rows, :] = dconv
        for k in range(KERNEL):
            acc_rows[k] += fold(dconv * shifted(win, k))
        acc_rows[KERNEL] += fold(dconv)
        acc_rows[KERNEL + 1] += fold(dgated * prod)
        acc_heads[0] += jnp.dot(scaled, prod, precision=EXACT, preferred_element_type=f32)
        acc_heads[1] += jnp.dot(
            dlogit, resid[rows, :].astype(f32), precision=EXACT, preferred_element_type=f32
        )

    backward(0)
    first_rows = copy_of(to_conv.at[pl.ds(0, 8)], after, 2 * NCHAN + 1, {"seq": sooner})
    first_rows.start()

    def backward_step(tile, carry):
        backward(tile)
        return carry

    lax.fori_loop(1, tokens // LANES, backward_step, 0)
    by_channel = acc_heads[0]
    small[pl.ds(0, VOCAB), :] = by_channel * skip * gain
    small[pl.ds(VOCAB, VOCAB), :] = acc_heads[1]
    lines = [jnp.sum(acc_rows[k], axis=0, keepdims=True) for k in range(KERNEL + 2)]
    lines.insert(KERNEL + 1, skip * jnp.sum(mix * by_channel, axis=0, keepdims=True))
    lines.append(jnp.zeros_like(skip))
    small[pl.ds(2 * VOCAB, 8), :] = jnp.concatenate(lines, axis=0)
    first_rows.wait_recv()
    to_conv[pl.ds(tokens, 8), :] = after[...] * (s < last_seq).astype(f32)

    def spread_step(tile, carry):
        start = pl.multiple_of(tile * LANES, LANES)
        win = to_conv[pl.ds(start, LANES + 8), :]
        acc = taps[KERNEL - 1] * win[0:LANES]
        for k in range(KERNEL - 1):
            acc = acc + taps[k] * win[KERNEL - 1 - k : KERNEL - 1 - k + LANES]
        dx[pl.ds(start, LANES), :] = acc.astype(bf16)
        return carry

    lax.fori_loop(0, tokens // LANES, spread_step, 0)
    edge.wait_send()
    first_rows.wait_send()
    for d in range(1, NCHAN):
        share(d - 1).wait_send()
        tell(d).wait_send()


def middle(gate, xs, resid, head_t, mix_t, params, targets):
    f32, bf16 = jnp.float32, jnp.bfloat16
    vmem = pl.BlockSpec(memory_space=pltpu.VMEM)
    tokens, width = gate.shape
    copies = 2 * NCHAN + 2
    return pl.pallas_call(
        middle_kernel,
        name="middle",
        out_shape=(
            jax.ShapeDtypeStruct((tokens, width), bf16),
            jax.ShapeDtypeStruct((tokens, width), bf16),
            jax.ShapeDtypeStruct((SUMS, width), f32),
            jax.ShapeDtypeStruct((tokens, width), bf16),
            jax.ShapeDtypeStruct((NCHAN, FACTS, LANES), f32),
        ),
        in_specs=[vmem] * 7,
        out_specs=(vmem,) * 5,
        scratch_shapes=[
            pltpu.VMEM((tokens + EDGE, width), f32),
            pltpu.VMEM((tokens, width), f32),
            pltpu.VMEM((tokens, width), f32),
            pltpu.VMEM((tokens + 8, width), f32),
            pltpu.VMEM((NCHAN, SUMS, LANES), f32),
            pltpu.VMEM((NCHAN - 1, SUMS, LANES), f32),
            pltpu.VMEM((FACTS, LANES), f32),
            pltpu.VMEM((EDGE, width), bf16),
            pltpu.VMEM((8, width), f32),
            pltpu.VMEM((KERNEL + 2, 8, width), f32),
            pltpu.VMEM((2, VOCAB, width), f32),
            pltpu.SemaphoreType.DMA((copies,)),
            pltpu.SemaphoreType.DMA((copies,)),
        ],
        compiler_params=pltpu.CompilerParams(
            collective_id=1, has_side_effects=True, vmem_limit_bytes=VMEM_BYTES
        ),
        cost_estimate=pl.CostEstimate(flops=10**10, bytes_accessed=10**7, transcendentals=0),
    )(gate, xs, resid, head_t, mix_t, params, targets)


def scatter_seq(wire, grads, bufs, out, y, z, start, count):
    f32, bf16 = jnp.float32, jnp.bfloat16
    from_below, from_above, via_up, via_down, got_below, got_above, lines, got_z = bufs
    rows = pl.ds(start, count)
    lo, hi = pl.ds(0, NZ // 2), pl.ds(NZ // 2, NZ // 2)
    above, below, across = lax.rem(y + 1, NY), lax.rem(y + 3, NY), lax.rem(y + 2, NY)
    up, down = above * NZ + z, below * NZ + z
    half_up = wire.put(grads.at[across, lo, rows], from_below.at[:, rows], seq=up)
    half_down = wire.put(grads.at[across, hi, rows], from_above.at[:, rows], seq=down)
    moves = [
        wire.put(grads.at[above, hi, rows], got_below.at[hi, rows], seq=up),
        wire.put(grads.at[below, lo, rows], got_above.at[lo, rows], seq=down),
    ]
    yield
    half_up.wait_recv()
    via_up[:, rows] = (
        grads[above, lo, rows].astype(f32) + from_below[:, rows].astype(f32)
    ).astype(bf16)
    moves.append(wire.put(via_up.at[:, rows], got_below.at[lo, rows], seq=up))
    half_down.wait_recv()
    via_down[:, rows] = (
        grads[below, hi, rows].astype(f32) + from_above[:, rows].astype(f32)
    ).astype(bf16)
    moves.append(wire.put(via_down.at[:, rows], got_above.at[hi, rows], seq=down))
    yield
    for copy in moves[:2]:
        copy.wait_recv()
    yield
    for copy in moves[2:]:
        copy.wait_recv()
    lines[:, rows] = (
        grads[y, :, rows].astype(f32)
        + got_below[:, rows].astype(f32)
        + got_above[:, rows].astype(f32)
    ).astype(bf16)
    puts = []
    for d in range(1, NZ):
        peer = lax.rem(z + d, NZ)
        puts.append(wire.put(lines.at[peer, rows], got_z.at[d - 1, rows], seq=y * NZ + peer))
    yield
    acc = (
        grads[y, z, rows].astype(f32)
        + got_below[z, rows].astype(f32)
        + got_above[z, rows].astype(f32)
    )
    for d in range(1, NZ):
        puts[d - 1].wait_recv()
        acc = acc + got_z[d - 1, rows].astype(f32)
    out[rows] = acc


def sum_small(wire, small, got_y, part, got_z, total, heads, y, z, c):
    puts = [
        wire.put(small, got_y.at[y], seq=lax.rem(y + d, NY) * NZ + z) for d in range(1, NY)
    ]
    got_y[y] = small[...]
    yield
    for copy in puts:
        copy.wait_recv()
    acc = got_y[0]
    for at in range(1, NY):
        acc = acc + got_y[at]
    part[...] = acc
    puts = [
        wire.put(part, got_z.at[z], seq=y * NZ + lax.rem(z + d, NZ)) for d in range(1, NZ)
    ]
    got_z[z] = acc
    yield
    for copy in puts:
        copy.wait_recv()
    acc = got_z[0]
    for at in range(1, NZ):
        acc = acc + got_z[at]
    total[...] = acc
    first = pl.ds(0, VOCAB)
    puts = [
        wire.put(total.at[first], heads.at[c], chan=lax.rem(c + d, NCHAN))
        for d in range(1, NCHAN)
    ]
    heads[c] = total[first]
    yield
    for copy in puts:
        copy.wait_recv()


def grads_kernel(
    grads, small, gained, out, total, heads, full_gained, *scratch
):
    *bufs, small_y, small_part, small_z, send, recv, local = scratch
    y, z, c = place()
    greet(
        [{"chan": lax.rem(c + d, NCHAN)} for d in range(1, NCHAN)]
        + [{"seq": lax.rem(y + d, NY) * NZ + z} for d in range(1, NY)]
        + [{"seq": y * NZ + lax.rem(z + d, NZ)} for d in range(1, NZ)]
    )
    wire = Wire(send, recv)
    own = pltpu.make_async_copy(gained, full_gained.at[c], local.at[0])
    own.start()
    rows = out.shape[0]
    smalls = sum_small(wire, small, small_y, small_part, small_z, total, heads, y, z, c)
    one = scatter_seq(wire, grads, bufs, out, y, z, 0, 48)
    two = scatter_seq(wire, grads, bufs, out, y, z, 48, rows - 48)
    chans = gather_chan(wire, gained, full_gained, c, gained.shape[0])
    in_order(smalls, one, chans, smalls, one, chans, one, two, one)
    in_order(smalls, chans, two, two, two, chans, smalls, one, two, chans)
    own.wait()
    wire.finish()


def finish_grads(grads, small, gained):
    f32, bf16 = jnp.float32, jnp.bfloat16
    anywhere = pl.BlockSpec(memory_space=pl.ANY)
    vmem = pl.BlockSpec(memory_space=pltpu.VMEM)
    _, _, rows, cols = grads.shape
    copies = 64
    half = (NZ // 2, rows, cols)
    line = (NZ, rows, cols)
    return pl.pallas_call(
        grads_kernel,
        name="finish_grads",
        out_shape=(
            jax.ShapeDtypeStruct((rows, cols), f32),
            jax.ShapeDtypeStruct(small.shape, f32),
            jax.ShapeDtypeStruct((NCHAN, VOCAB, small.shape[1]), f32),
            jax.ShapeDtypeStruct((NCHAN, *gained.shape), bf16),
        ),
        in_specs=[vmem, vmem, anywhere],
        out_specs=(vmem, vmem, vmem, anywhere),
        scratch_shapes=[pltpu.VMEM(half, bf16)] * 4
        + [pltpu.VMEM(line, bf16)] * 3
        + [
            pltpu.VMEM((NZ - 1, rows, cols), bf16),
            pltpu.VMEM((NY, *small.shape), f32),
            pltpu.VMEM(small.shape, f32),
            pltpu.VMEM((NZ, *small.shape), f32),
            pltpu.SemaphoreType.DMA((copies,)),
            pltpu.SemaphoreType.DMA((copies,)),
            pltpu.SemaphoreType.DMA((1,)),
        ],
        compiler_params=pltpu.CompilerParams(
            collective_id=2, has_side_effects=True, vmem_limit_bytes=VMEM_BYTES
        ),
        cost_estimate=pl.CostEstimate(flops=10**10, bytes_accessed=10**8, transcendentals=0),
    )(grads, small, gained)


def sum_of_dots(left, right):
    depth = left.shape[2]
    acc = jnp.dot(left[0], right[pl.ds(0, depth), :], preferred_element_type=jnp.float32)
    for at in range(1, left.shape[0]):
        acc = acc + jnp.dot(
            left[at], right[pl.ds(at * depth, depth), :], preferred_element_type=jnp.float32
        )
    return acc


def project_kernel(left, right, gate, xs):
    acc = sum_of_dots(left, right)
    width = gate.shape[1]
    gate[...] = acc[:, :width].astype(gate.dtype)
    xs[...] = acc[:, width:].astype(xs.dtype)


def project(left, right):
    parts, tokens, depth = left.shape
    tile, width = 256, right.shape[1] // 2
    half = pl.BlockSpec((tile, width), lambda i: (i, 0))
    return pl.pallas_call(
        project_kernel,
        name="project",
        grid=(tokens // tile,),
        out_shape=(jax.ShapeDtypeStruct((tokens, width), jnp.bfloat16),) * 2,
        in_specs=[
            pl.BlockSpec((parts, tile, depth), lambda i: (0, i, 0)),
            pl.BlockSpec(right.shape, lambda i: (0, 0), pipeline_mode=pl.Buffered(1)),
        ],
        out_specs=(half, half),
        compiler_params=pltpu.CompilerParams(vmem_limit_bytes=VMEM_BYTES),
    )(left, right)


def residual_kernel(left, right, resid, facts, out):
    acc = sum_of_dots(left, right)
    inverse = (
        lax.broadcasted_iota(jnp.int32, (8, out.shape[1]), 0) == 0
    ).astype(jnp.float32)
    for at in range(facts.shape[0]):
        rows = pl.ds(at * LANES, LANES)
        scale = lax.dot_general(
            facts[at, pl.ds(VOCAB, 8)],
            inverse,
            (((0,), (0,)), ((), ())),
            precision=EXACT,
            preferred_element_type=jnp.float32,
        )
        summed = resid[rows, :].astype(jnp.float32) + scale * acc[at * LANES : at * LANES + LANES]
        out[rows, :] = summed.astype(out.dtype)


def add_projected(left, right, resid, facts):
    parts, tokens, depth = left.shape
    tile, width = 256, right.shape[1]
    rows = pl.BlockSpec((tile, width), lambda i: (i, 0))
    return pl.pallas_call(
        residual_kernel,
        name="add_projected",
        grid=(tokens // tile,),
        out_shape=jax.ShapeDtypeStruct((tokens, width), jnp.bfloat16),
        in_specs=[
            pl.BlockSpec((parts, tile, depth), lambda i: (0, i, 0)),
            pl.BlockSpec(right.shape, lambda i: (0, 0), pipeline_mode=pl.Buffered(1)),
            rows,
            pl.BlockSpec((tile // LANES, FACTS, LANES), lambda i: (i, 0, 0)),
        ],
        out_specs=rows,
        compiler_params=pltpu.CompilerParams(vmem_limit_bytes=VMEM_BYTES),
    )(left, right, resid, facts)


def outer_kernel(left, dgate, dx, out, both):
    width = dgate.shape[1]

    @pl.when(pl.program_id(0) == 0)
    def _():
        both[:, pl.ds(0, width)] = dgate[...]
        both[:, pl.ds(width, width)] = dx[...]

    out[0] = lax.dot_general(
        left[0], both[...], (((0,), (0,)), ((), ())), preferred_element_type=jnp.float32
    ).astype(out.dtype)


def stacked_outer(left, dgate, dx):
    parts, tokens, depth = left.shape
    width = 2 * dgate.shape[1]
    whole = pl.BlockSpec(dgate.shape, lambda i: (0, 0), pipeline_mode=pl.Buffered(1))
    return pl.pallas_call(
        outer_kernel,
        name="stacked_outer",
        grid=(parts,),
        out_shape=jax.ShapeDtypeStruct((parts, depth, width), jnp.bfloat16),
        in_specs=[pl.BlockSpec((1, tokens, depth), lambda i: (i, 0, 0)), whole, whole],
        out_specs=pl.BlockSpec((1, depth, width), lambda i: (i, 0, 0)),
        scratch_shapes=[pltpu.VMEM((tokens, width), jnp.bfloat16)],
        compiler_params=pltpu.CompilerParams(vmem_limit_bytes=VMEM_BYTES),
    )(left, dgate, dx)


def slope(value, sig):
    return sig * (1.0 + value * (1.0 - sig))


def inner_rows(left, right, precision=None):
    return lax.dot_general(
        left,
        right,
        (((0,), (0,)), ((), ())),
        preferred_element_type=jnp.float32,
        precision=precision,
    )


def per_device(
    targets, resid, w_gate_in, w_x_in, conv_weight, conv_bias, skip_d, norm_gain, w_out, w_head
):
    f32 = jnp.float32
    local_inner = w_gate_in.shape[1]
    row_count = w_out.shape[0]
    out_cols = lax.all_gather(w_out, "seq", axis=0, tiled=True)
    head_t = w_head.T
    features, full, mix_t = gather_all(
        resid, jnp.concatenate([w_gate_in, w_x_in], axis=1), w_out, head_t
    )
    gate_pre, x_pre = project(features, full.reshape(INNER, 2 * local_inner))
    params = jnp.concatenate(
        [
            conv_weight,
            conv_bias[None],
            jnp.repeat(skip_d, HEADDIM)[None],
            norm_gain[None],
            jnp.zeros((1, local_inner), f32),
        ],
        axis=0,
    )
    dgate, dx_pre, small, gained, facts = middle(
        gate_pre, x_pre, resid, head_t, mix_t, params, targets.reshape(NCHAN, 1, LANES)
    )
    grads = stacked_outer(features, dgate, dx_pre).reshape(NY, NZ, row_count, 2 * local_inner)
    grad_both, total, mix_grads, full_gained = finish_grads(grads, small, gained)
    grad_gate_in = grad_both[:, :local_inner]
    grad_x_in = grad_both[:, local_inner:]
    at = 2 * VOCAB
    grad_conv_weight = total[at : at + KERNEL]
    grad_conv_bias = total[at + KERNEL]
    grad_gain = total[at + KERNEL + 1]
    grad_skip = total[at + KERNEL + 2].reshape(-1, HEADDIM).sum(axis=1)
    new_resid = add_projected(full_gained, out_cols, resid, facts)
    mix_grads = mix_grads.transpose(1, 0, 2).reshape(VOCAB, INNER)
    grad_head = total[VOCAB : 2 * VOCAB].T + inner_rows(
        out_cols.astype(f32), mix_grads.T, EXACT
    )
    mix_grad_rows = lax.dynamic_slice_in_dim(
        mix_grads, lax.axis_index("seq") * row_count, row_count, 1
    )
    grad_out = inner_rows(mix_grad_rows, w_head.astype(f32).T, EXACT)
    return (
        new_resid,
        grad_gate_in,
        grad_x_in,
        grad_out,
        grad_head,
        grad_conv_weight,
        grad_conv_bias,
        grad_skip,
        grad_gain,
    )


def solution(mesh):
    return jax.shard_map(
        per_device,
        mesh=mesh,
        in_specs=(
            P("seq"),
            P("seq", "chan"),
            P("seq", "chan"),
            P("seq", "chan"),
            P(None, "chan"),
            P("chan"),
            P("chan"),
            P("chan"),
            P("seq", "chan"),
            P("chan", None),
        ),
        out_specs=(
            P("seq", "chan"),
            P("seq", "chan"),
            P("seq", "chan"),
            P("seq", "chan"),
            P("chan", None),
            P(None, "chan"),
            P("chan"),
            P("chan"),
            P("chan"),
        ),
        check_vma=False,
    )
```

```python
import functools

import jax
import jax.numpy as jnp
from jax import lax
from jax.experimental import pallas as pl
from jax.experimental.pallas import tpu as pltpu
from jax.sharding import PartitionSpec as P

HEADDIM = 64
KERNEL = 4
VOCAB = 16
INNER = 2560
NX, NY, NZ = 4, 4, 8
NCHAN = 2 * NX
MESH = pl.DeviceIdType.MESH
VMEM_BYTES = 56 * 1024 * 1024


class Wire:
    def __init__(self, send, recv):
        self.send, self.recv, self.copies = send, recv, []

    def put(self, source, target, **where):
        place = len(self.copies)
        copy = pltpu.make_async_remote_copy(
            src_ref=source,
            dst_ref=target,
            send_sem=self.send.at[place],
            recv_sem=self.recv.at[place],
            device_id=where,
            device_id_type=MESH,
        )
        copy.start()
        self.copies.append(copy)
        return copy

    def finish(self):
        for copy in self.copies:
            copy.wait_send()


def greet(peers):
    barrier = pltpu.get_barrier_semaphore()
    for peer in peers:
        pl.semaphore_signal(barrier, inc=1, device_id=peer, device_id_type=MESH)
    pl.semaphore_wait(barrier, len(peers))


def in_order(*streams):
    for stream in streams:
        next(stream, None)


def place():
    s, c = lax.axis_index("seq"), lax.axis_index("chan")
    return s // NZ, s % NZ, c


def gather_chan(wire, shard, full, c, rows):
    x, core = c // 2, c % 2
    mate = c + 1 - 2 * core
    right = lax.rem(x + 1, NX) * 2 + core
    left = lax.rem(x + NX - 1, NX) * 2 + core
    across = lax.rem(x + 2, NX) * 2 + core
    lo, hi = pl.ds(0, rows // 2), pl.ds(rows // 2, rows // 2)
    to_right_lo = wire.put(shard.at[lo], full.at[c, lo], chan=right)
    to_left_hi = wire.put(shard.at[hi], full.at[c, hi], chan=left)
    yield
    to_right_hi = wire.put(shard.at[hi], full.at[c, hi], chan=right)
    to_left_lo = wire.put(shard.at[lo], full.at[c, lo], chan=left)
    to_mate = [wire.put(shard, full.at[c], chan=mate)]
    yield
    to_right_lo.wait_recv()
    on_right = wire.put(full.at[left, lo], full.at[left, lo], chan=right)
    to_left_hi.wait_recv()
    on_left = wire.put(full.at[right, hi], full.at[right, hi], chan=left)
    yield
    to_right_hi.wait_recv()
    to_mate.append(wire.put(full.at[left], full.at[left], chan=mate))
    to_left_lo.wait_recv()
    to_mate.append(wire.put(full.at[right], full.at[right], chan=mate))
    yield
    on_right.wait_recv()
    to_mate.append(wire.put(full.at[across, lo], full.at[across, lo], chan=mate))
    on_left.wait_recv()
    to_mate.append(wire.put(full.at[across, hi], full.at[across, hi], chan=mate))
    yield
    for copy in to_mate:
        copy.wait_recv()


def ring_z(wire, first, block, halves, y, z):
    up, down = y * NZ + lax.rem(z + 1, NZ), y * NZ + lax.rem(z + NZ - 1, NZ)
    plus = wire.put(first, block(z), seq=up)
    minus = wire.put(first, block(z), seq=down)
    for step in range(1, NZ // 2):
        last = step == NZ // 2 - 1
        yield
        behind, ahead = lax.rem(z + NZ - step, NZ), lax.rem(z + step, NZ)
        plus.wait_recv()
        moved = halves(behind)[0] if last else block(behind)
        plus = wire.put(moved, moved, seq=up)
        minus.wait_recv()
        moved = halves(ahead)[1] if last else block(ahead)
        minus = wire.put(moved, moved, seq=down)
    yield
    plus.wait_recv()
    minus.wait_recv()


def exchange_y(wire, shard, full, y, z, rows):
    puts = [
        wire.put(shard.at[rows], full.at[y, z, rows], seq=lax.rem(y + d, NY) * NZ + z)
        for d in (1, 3, 2)
    ]
    yield
    for copy in puts:
        copy.wait_recv()


def ring_z_columns(wire, full, y, z, rows):
    yield from ring_z(
        wire,
        full.at[:, z, rows],
        lambda at: full.at[:, at, rows],
        lambda at: (full.at[pl.ds(0, 2), at, rows], full.at[pl.ds(2, 2), at, rows]),
        y,
        z,
    )


def gather_z_then_y(wire, shard, full, y, z, rows):
    above, below = lax.rem(y + 1, NY), lax.rem(y + NY - 1, NY)
    y_up, y_down = above * NZ + z, below * NZ + z
    z_up, z_down = y * NZ + lax.rem(z + 1, NZ), y * NZ + lax.rem(z + NZ - 1, NZ)
    waiting, rest = [], []

    def spread(source, at, upward):
        block = full.at[y, at, rows]
        up, down = wire.put(source, block, seq=y_up), wire.put(source, block, seq=y_down)
        waiting.append((up, down, at, upward))

    def pass_on(count):
        for up, down, at, upward in waiting[:count]:
            if upward:
                up.wait_recv()
                block = full.at[below, at, rows]
                rest.extend([down, wire.put(block, block, seq=y_up)])
            else:
                down.wait_recv()
                block = full.at[above, at, rows]
                rest.extend([up, wire.put(block, block, seq=y_down)])
        del waiting[:count]

    own = full.at[y, z, rows]
    plus, minus = wire.put(shard.at[rows], own, seq=z_up), wire.put(shard.at[rows], own, seq=z_down)
    spread(shard.at[rows], z, True)
    for step in range(1, NZ // 2 + 1):
        yield
        before = len(waiting)
        behind = lax.rem(z + NZ - step, NZ)
        plus.wait_recv()
        block = full.at[y, behind, rows]
        if step < NZ // 2:
            plus = wire.put(block, block, seq=z_up)
        spread(block, behind, step < NZ // 2)
        if step < NZ // 2:
            ahead = lax.rem(z + step, NZ)
            minus.wait_recv()
            block = full.at[y, ahead, rows]
            if step < NZ // 2 - 1:
                minus = wire.put(block, block, seq=z_down)
            spread(block, ahead, False)
        pass_on(before)
    yield
    pass_on(len(waiting))
    yield
    for copy in rest:
        copy.wait_recv()


def gather_mix(wire, w_out, w_head, out, bufs, y, z, c):
    part, got_c, mine, line, picked = bufs
    rows = w_out.shape[0]
    part[...] = jnp.zeros_like(part)
    part[:, pl.ds(0, rows)] = lax.dot_general(
        w_head[...],
        w_out[...],
        (((1,), (1,)), ((), ())),
        preferred_element_type=jnp.float32,
    )
    puts = [
        wire.put(part, got_c.at[d - 1], chan=lax.rem(c + d, NCHAN)) for d in range(1, NCHAN)
    ]
    yield
    acc = part[...]
    for d in range(1, NCHAN):
        puts[d - 1].wait_recv()
        acc = acc + got_c[d - 1]
    mine[...] = acc
    line[z] = acc
    puts = [
        wire.put(mine, line.at[z], seq=y * NZ + lax.rem(z + d, NZ)) for d in range(1, NZ)
    ]
    yield
    for copy in puts:
        copy.wait_recv()
    kept = pl.ds((c % 2) * (NZ // 2), NZ // 2)
    puts = [
        wire.put(line.at[kept], picked.at[y], seq=lax.rem(y + d, NY) * NZ + z)
        for d in range(1, NY)
    ]
    picked[y] = line[kept]
    yield
    for copy in puts:
        copy.wait_recv()
    for at in range(NZ // 2):
        out[:, pl.ds(at * rows, rows)] = picked[c // 2, at][:, :rows]


def gather_kernel(
    resid, w_gate, w_x, w_out, w_head, full_resid, full_weights, mix, weights, *scratch
):
    *mix_bufs, send, recv, local = scratch
    y, z, c = place()
    half = w_gate.shape[1]
    weights[:, pl.ds(0, half)] = w_gate[...]
    weights[:, pl.ds(half, half)] = w_x[...]
    greet(
        [{"chan": lax.rem(c + d, NCHAN)} for d in range(1, NCHAN)]
        + [{"seq": lax.rem(y + d, NY) * NZ + z} for d in range(1, NY)]
        + [{"seq": y * NZ + lax.rem(z + d, NZ)} for d in range(1, NZ)]
    )
    wire = Wire(send, recv)
    own_weights = pltpu.make_async_copy(weights, full_weights.at[y, z], local.at[0])
    own_resid = pltpu.make_async_copy(resid, full_resid.at[c], local.at[1])
    own_weights.start()
    own_resid.start()
    rows, first = weights.shape[0], 32
    one, rest = pl.ds(0, first), pl.ds(first, rows - first)
    lines = gather_z_then_y(wire, weights, full_weights, y, z, rest)
    own_y = exchange_y(wire, weights, full_weights, y, z, one)
    columns = ring_z_columns(wire, full_weights, y, z, one)
    chans = gather_chan(wire, resid, full_resid, c, resid.shape[0])
    mixes = gather_mix(wire, w_out, w_head, mix, mix_bufs, y, z, c)
    in_order(own_y, lines, chans, mixes, own_y)
    own_weights.wait()
    in_order(columns, lines, chans, mixes, lines, columns, mixes, lines, chans)
    in_order(columns, lines, mixes, columns, chans, columns, lines, lines, chans, chans)
    own_resid.wait()
    wire.finish()


def gather_all(resid, w_gate, w_x, w_out, w_head):
    anywhere = pl.BlockSpec(memory_space=pl.ANY)
    vmem = pl.BlockSpec(memory_space=pltpu.VMEM)
    f32 = jnp.float32
    copies = 96
    block = (VOCAB, 128)
    rows, half = w_gate.shape
    return pl.pallas_call(
        gather_kernel,
        name="gather_all",
        out_shape=(
            jax.ShapeDtypeStruct((NCHAN, *resid.shape), resid.dtype),
            jax.ShapeDtypeStruct((NY, NZ, rows, 2 * half), w_gate.dtype),
            jax.ShapeDtypeStruct((VOCAB, resid.shape[0]), f32),
        ),
        in_specs=[anywhere] + [vmem] * 4,
        out_specs=(anywhere, anywhere, vmem),
        scratch_shapes=[
            pltpu.VMEM((rows, 2 * half), w_gate.dtype),
            pltpu.VMEM(block, f32),
            pltpu.VMEM((NCHAN - 1, *block), f32),
            pltpu.VMEM(block, f32),
            pltpu.VMEM((NZ, *block), f32),
            pltpu.VMEM((NY, NZ // 2, *block), f32),
            pltpu.SemaphoreType.DMA((copies,)),
            pltpu.SemaphoreType.DMA((copies,)),
            pltpu.SemaphoreType.DMA((2,)),
        ],
        compiler_params=pltpu.CompilerParams(collective_id=0, has_side_effects=True),
        cost_estimate=pl.CostEstimate(flops=10**10, bytes_accessed=10**8, transcendentals=0),
    )(resid, w_gate, w_x, w_out, w_head)


EXACT = lax.Precision.HIGHEST
LANES = 128
EDGE = 16
SUMS = 40
FACTS = 24


def middle_kernel(
    gate,
    xs,
    resid,
    head_t,
    mix_t,
    params,
    targets,
    w_out,
    dgate,
    dx,
    small,
    gained,
    facts,
    full_w_out,
    padded,
    prods,
    to_gate,
    to_conv,
    sums,
    parts,
    mine,
    before,
    after,
    acc_rows,
    acc_heads,
    send,
    recv,
    w_send,
    w_recv,
    local,
):
    f32, bf16 = jnp.float32, jnp.bfloat16
    tokens = gate.shape[0]
    y, z, c = place()
    s = y * NZ + z
    last_seq = NY * NZ - 1
    later, sooner = lax.rem(s + 1, NY * NZ), lax.rem(s + last_seq, NY * NZ)
    greet(
        [{"chan": lax.rem(c + d, NCHAN)} for d in range(1, NCHAN)]
        + [{"seq": later}, {"seq": sooner}]
        + [{"seq": lax.rem(y + d, NY) * NZ + z} for d in range(1, NY)]
        + [{"seq": y * NZ + lax.rem(z + d, NZ)} for d in (1, NZ - 1)]
    )
    wire = Wire(w_send, w_recv)
    whole = pl.ds(0, w_out.shape[0])
    own_w_out = pltpu.make_async_copy(w_out, full_w_out.at[y, z], local.at[0])
    own_w_out.start()

    def copy_of(source, target, at, where):
        return pltpu.make_async_remote_copy(
            src_ref=source,
            dst_ref=target,
            send_sem=send.at[at],
            recv_sem=recv.at[at],
            device_id=where,
            device_id_type=MESH,
        )

    edge = copy_of(xs.at[pl.ds(tokens - EDGE, EDGE)], before, 2 * NCHAN, {"seq": later})
    edge.start()
    own_y = exchange_y(wire, w_out, full_w_out, y, z, whole)
    columns = ring_z_columns(wire, full_w_out, y, z, whole)
    in_order(own_y)
    taps = [params[k : k + 1, :] for k in range(KERNEL)]
    bias, skip, gain = params[4:5, :], params[5:6, :], params[6:7, :]
    mix = mix_t[...]
    padded[pl.ds(EDGE, tokens), :] = xs[...].astype(f32)

    def window(tile):
        start = pl.multiple_of(tile * LANES, LANES)
        return pl.ds(start, LANES), padded[pl.ds(start, LANES + EDGE), :]

    def shifted(win, k):
        first = EDGE - (KERNEL - 1) + k
        return win[first : first + LANES]

    def share(step):
        peer = lax.rem(c + 1 + step, NCHAN)
        return copy_of(sums.at[peer], parts.at[step], step, {"chan": peer})

    def forward(tile):
        rows, win = window(tile)
        conv = bias + taps[0] * shifted(win, 0)
        for k in range(1, KERNEL):
            conv = conv + taps[k] * shifted(win, k)
        sig_conv = jax.nn.sigmoid(conv)
        active = conv * sig_conv
        gate_pre = gate[rows, :].astype(f32)
        sig_gate = jax.nn.sigmoid(gate_pre)
        silu_gate = gate_pre * sig_gate
        prod = active * silu_gate
        prods[rows, :] = prod
        to_gate[rows, :] = skip * active * slope(gate_pre, sig_gate)
        to_conv[rows, :] = skip * silu_gate * slope(conv, sig_conv)
        gated = prod * skip
        with_gain = gated * gain
        gained[:, rows] = with_gain.T.astype(bf16)
        by_lanes = (((1,), (1,)), ((), ()))
        sums[tile, pl.ds(0, VOCAB)] = lax.dot_general(
            head_t[...],
            resid[:, rows],
            (((1,), (0,)), ((), ())),
            preferred_element_type=f32,
        )
        sums[tile, pl.ds(VOCAB, VOCAB)] = lax.dot_general(
            mix, with_gain, by_lanes, precision=EXACT, preferred_element_type=f32
        )
        sums[tile, pl.ds(2 * VOCAB, 8)] = lax.dot_general(
            jnp.ones((8, gated.shape[1]), f32),
            gated * gated,
            by_lanes,
            precision=EXACT,
            preferred_element_type=f32,
        )

    edge.wait_recv()
    own_w_out.wait()
    in_order(own_y, columns)
    padded[pl.ds(0, EDGE), :] = before[...].astype(f32) * (s > 0).astype(f32)

    def forward_step(step, carry):
        forward(lax.rem(c + 1 + step, NCHAN))
        share(step).start()
        return carry

    lax.fori_loop(0, NCHAN - 1, forward_step, 0)
    forward(c)
    in_order(columns)
    total = sums[c]
    for step in range(NCHAN - 1):
        share(step).wait_recv()
        total = total + parts[step]
    inverse = lax.rsqrt(total[2 * VOCAB : 2 * VOCAB + 1] / INNER + 1e-05)
    gained_head = total[VOCAB : 2 * VOCAB]
    raised = jnp.exp(total[:VOCAB] + inverse * gained_head)
    probs = raised / jnp.sum(raised, axis=0, keepdims=True)
    words = lax.broadcasted_iota(jnp.int32, (VOCAB, LANES), 0)
    onehot = (words == targets[c]).astype(f32)
    weight = 4.0 / float(tokens * NY * NZ) ** 0.5
    dlogit = (probs - onehot) * weight
    dot_gn = jnp.sum(dlogit * gained_head, axis=0, keepdims=True)
    mine[pl.ds(0, VOCAB), :] = dlogit
    mine[pl.ds(VOCAB, 8), :] = jnp.concatenate(
        [inverse, inverse * inverse * inverse * dot_gn / INNER, jnp.zeros((6, LANES), f32)],
        axis=0,
    )
    facts[c] = mine[...]

    def tell(d):
        return copy_of(
            mine, facts.at[c], NCHAN - 1 + d, {"chan": lax.rem(c + d, NCHAN)}
        )

    for d in range(1, NCHAN):
        tell(d).start()
    acc_rows[...] = jnp.zeros_like(acc_rows)
    acc_heads[...] = jnp.zeros_like(acc_heads)
    for d in range(1, NCHAN):
        tell(d).wait_recv()
    in_order(columns)
    second = (
        lax.broadcasted_iota(jnp.int32, (8, mix.shape[1]), 0) == 1
    ).astype(f32)

    def fold(value):
        return jnp.sum(value.reshape(LANES // 8, 8, value.shape[1]), axis=0)

    def backward(tile):
        rows, win = window(tile)
        fact = facts[tile]
        dlogit = fact[:VOCAB]
        scaled = dlogit * fact[VOCAB : VOCAB + 1]
        by_rows = (((0,), (0,)), ((), ()))
        dnormed = lax.dot_general(
            scaled, mix, by_rows, precision=EXACT, preferred_element_type=f32
        )
        pull = lax.dot_general(
            fact[VOCAB : VOCAB + 8], second, by_rows, precision=EXACT, preferred_element_type=f32
        )
        prod = prods[rows, :]
        dgated = gain * dnormed - skip * prod * pull
        dgate[rows, :] = (dgated * to_gate[rows, :]).astype(bf16)
        dconv = dgated * to_conv[rows, :]
        to_conv[rows, :] = dconv
        for k in range(KERNEL):
            acc_rows[k] += fold(dconv * shifted(win, k))
        acc_rows[KERNEL] += fold(dconv)
        acc_rows[KERNEL + 1] += fold(dgated * prod)
        acc_heads[0] += jnp.dot(scaled, prod, precision=EXACT, preferred_element_type=f32)
        acc_heads[1] += lax.dot_general(
            dlogit,
            resid[:, rows].astype(f32),
            (((1,), (1,)), ((), ())),
            precision=EXACT,
            preferred_element_type=f32,
        )

    backward(0)
    first_rows = copy_of(to_conv.at[pl.ds(0, 8)], after, 2 * NCHAN + 1, {"seq": sooner})
    first_rows.start()

    def backward_step(tile, carry):
        backward(tile)
        return carry

    lax.fori_loop(1, tokens // LANES, backward_step, 0)
    in_order(columns)
    by_channel = acc_heads[0]
    small[pl.ds(0, VOCAB), :] = by_channel * skip * gain
    small[pl.ds(VOCAB, VOCAB), :] = acc_heads[1]
    lines = [jnp.sum(acc_rows[k], axis=0, keepdims=True) for k in range(KERNEL + 2)]
    lines.insert(KERNEL + 1, skip * jnp.sum(mix * by_channel, axis=0, keepdims=True))
    lines.append(jnp.zeros_like(skip))
    small[pl.ds(2 * VOCAB, 8), :] = jnp.concatenate(lines, axis=0)
    first_rows.wait_recv()
    to_conv[pl.ds(tokens, 8), :] = after[...] * (s < last_seq).astype(f32)

    def spread_step(tile, carry):
        start = pl.multiple_of(tile * LANES, LANES)
        win = to_conv[pl.ds(start, LANES + 8), :]
        acc = taps[KERNEL - 1] * win[0:LANES]
        for k in range(KERNEL - 1):
            acc = acc + taps[k] * win[KERNEL - 1 - k : KERNEL - 1 - k + LANES]
        dx[pl.ds(start, LANES), :] = acc.astype(bf16)
        return carry

    lax.fori_loop(0, tokens // LANES, spread_step, 0)
    in_order(columns)
    wire.finish()
    edge.wait_send()
    first_rows.wait_send()
    for d in range(1, NCHAN):
        share(d - 1).wait_send()
        tell(d).wait_send()


def middle(gate, xs, resid, head_t, mix_t, params, targets, w_out):
    f32, bf16 = jnp.float32, jnp.bfloat16
    vmem = pl.BlockSpec(memory_space=pltpu.VMEM)
    anywhere = pl.BlockSpec(memory_space=pl.ANY)
    tokens, width = gate.shape
    copies = 2 * NCHAN + 2
    return pl.pallas_call(
        middle_kernel,
        name="middle",
        out_shape=(
            jax.ShapeDtypeStruct((tokens, width), bf16),
            jax.ShapeDtypeStruct((tokens, width), bf16),
            jax.ShapeDtypeStruct((SUMS, width), f32),
            jax.ShapeDtypeStruct((width, tokens), bf16),
            jax.ShapeDtypeStruct((NCHAN, FACTS, LANES), f32),
            jax.ShapeDtypeStruct((NY, NZ, *w_out.shape), bf16),
        ),
        in_specs=[vmem] * 7 + [anywhere],
        out_specs=(vmem,) * 5 + (anywhere,),
        scratch_shapes=[
            pltpu.VMEM((tokens + EDGE, width), f32),
            pltpu.VMEM((tokens, width), f32),
            pltpu.VMEM((tokens, width), f32),
            pltpu.VMEM((tokens + 8, width), f32),
            pltpu.VMEM((NCHAN, SUMS, LANES), f32),
            pltpu.VMEM((NCHAN - 1, SUMS, LANES), f32),
            pltpu.VMEM((FACTS, LANES), f32),
            pltpu.VMEM((EDGE, width), bf16),
            pltpu.VMEM((8, width), f32),
            pltpu.VMEM((KERNEL + 2, 8, width), f32),
            pltpu.VMEM((2, VOCAB, width), f32),
            pltpu.SemaphoreType.DMA((copies,)),
            pltpu.SemaphoreType.DMA((copies,)),
            pltpu.SemaphoreType.DMA((NY + NZ,)),
            pltpu.SemaphoreType.DMA((NY + NZ,)),
            pltpu.SemaphoreType.DMA((1,)),
        ],
        compiler_params=pltpu.CompilerParams(
            collective_id=1, has_side_effects=True, vmem_limit_bytes=VMEM_BYTES
        ),
        cost_estimate=pl.CostEstimate(flops=10**10, bytes_accessed=10**7, transcendentals=0),
    )(gate, xs, resid, head_t, mix_t, params, targets, w_out)


def scatter_seq(wire, grads, ready, bufs, outs, y, z, start, count):
    f32, bf16 = jnp.float32, jnp.bfloat16
    from_below, from_above, via_up, via_down, got_below, got_above, lines, got_z = bufs
    rows = pl.ds(start, count)
    lo, hi = pl.ds(0, NZ // 2), pl.ds(NZ // 2, NZ // 2)
    above, below, across = lax.rem(y + 1, NY), lax.rem(y + 3, NY), lax.rem(y + 2, NY)
    up, down = above * NZ + z, below * NZ + z
    ready(2 * across)
    half_up = wire.put(grads.at[across, lo, rows], from_below.at[:, rows], seq=up)
    ready(2 * across + 1)
    half_down = wire.put(grads.at[across, hi, rows], from_above.at[:, rows], seq=down)
    ready(2 * above + 1)
    moves = [wire.put(grads.at[above, hi, rows], got_below.at[hi, rows], seq=up)]
    ready(2 * below)
    moves.append(wire.put(grads.at[below, lo, rows], got_above.at[lo, rows], seq=down))
    ready(2 * above)
    ready(2 * below + 1)
    yield
    half_up.wait_recv()
    via_up[:, rows] = (
        grads[above, lo, rows].astype(f32) + from_below[:, rows].astype(f32)
    ).astype(bf16)
    moves.append(wire.put(via_up.at[:, rows], got_below.at[lo, rows], seq=up))
    half_down.wait_recv()
    via_down[:, rows] = (
        grads[below, hi, rows].astype(f32) + from_above[:, rows].astype(f32)
    ).astype(bf16)
    moves.append(wire.put(via_down.at[:, rows], got_above.at[hi, rows], seq=down))
    ready(2 * y)
    ready(2 * y + 1)
    yield
    for copy in moves[:2]:
        copy.wait_recv()
    yield
    for copy in moves[2:]:
        copy.wait_recv()
    lines[:, rows] = (
        grads[y, :, rows].astype(f32)
        + got_below[:, rows].astype(f32)
        + got_above[:, rows].astype(f32)
    ).astype(bf16)
    puts = []
    for d in range(1, NZ):
        peer = lax.rem(z + d, NZ)
        puts.append(wire.put(lines.at[peer, rows], got_z.at[d - 1, rows], seq=y * NZ + peer))
    yield
    acc = (
        grads[y, z, rows].astype(f32)
        + got_below[z, rows].astype(f32)
        + got_above[z, rows].astype(f32)
    )
    for d in range(1, NZ):
        puts[d - 1].wait_recv()
        acc = acc + got_z[d - 1, rows].astype(f32)
    half = acc.shape[1] // 2
    outs[0][rows] = acc[:, :half]
    outs[1][rows] = acc[:, half:]


def sum_small(wire, small, got_y, part, got_z, total, heads, y, z, c):
    puts = [
        wire.put(small, got_y.at[y], seq=lax.rem(y + d, NY) * NZ + z) for d in range(1, NY)
    ]
    got_y[y] = small[...]
    yield
    for copy in puts:
        copy.wait_recv()
    acc = got_y[0]
    for at in range(1, NY):
        acc = acc + got_y[at]
    part[...] = acc
    puts = [
        wire.put(part, got_z.at[z], seq=y * NZ + lax.rem(z + d, NZ)) for d in range(1, NZ)
    ]
    got_z[z] = acc
    yield
    for copy in puts:
        copy.wait_recv()
    acc = got_z[0]
    for at in range(1, NZ):
        acc = acc + got_z[at]
    total[...] = acc
    first = pl.ds(0, VOCAB)
    puts = [
        wire.put(total.at[first], heads.at[c], chan=lax.rem(c + d, NCHAN))
        for d in range(1, NCHAN)
    ]
    heads[c] = total[first]
    yield
    for copy in puts:
        copy.wait_recv()


def grads_kernel(
    features,
    dgate,
    dx,
    small,
    gained,
    w_out,
    resid,
    facts,
    head_t,
    grad_gate,
    grad_x,
    total,
    grad_out,
    grad_head,
    new_resid,
    *scratch,
):
    f32, bf16 = jnp.float32, jnp.bfloat16
    feats, both, grads, full_gained, out_cols, heads, *rest = scratch
    *bufs, small_y, small_part, small_z, send, recv, local = rest
    y, z, c = place()
    width = dgate.shape[1]
    order = [
        2 * lax.rem(y + 2, NY),
        2 * lax.rem(y + 2, NY) + 1,
        2 * lax.rem(y + 1, NY) + 1,
        2 * lax.rem(y + 3, NY),
        2 * lax.rem(y + 1, NY),
        2 * lax.rem(y + 3, NY) + 1,
        2 * y,
        2 * y + 1,
    ]
    loads = [
        pltpu.make_async_copy(features.at[at], feats.at[step], local.at[step])
        for step, at in enumerate(order)
    ]
    for load in loads:
        load.start()
    own = pltpu.make_async_copy(gained, full_gained.at[c], local.at[NCHAN])
    own.start()
    weights = pltpu.make_async_copy(w_out, out_cols, local.at[NCHAN + 1])
    weights.start()
    both[:, pl.ds(0, width)] = dgate[...]
    both[:, pl.ds(width, width)] = dx[...]
    greet(
        [{"chan": lax.rem(c + d, NCHAN)} for d in range(1, NCHAN)]
        + [{"seq": lax.rem(y + d, NY) * NZ + z} for d in range(1, NY)]
        + [{"seq": y * NZ + lax.rem(z + d, NZ)} for d in range(1, NZ)]
    )
    wire = Wire(send, recv)
    steps = iter(range(NCHAN))

    def ready(block):
        step = next(steps)
        loads[step].wait()
        product = jnp.dot(feats[step], both[...], preferred_element_type=f32)
        lines = product.reshape(NZ // 2, product.shape[0] // (NZ // 2), product.shape[1])
        first = lax.rem(block, 2) * (NZ // 2)
        grads[block // 2, pl.ds(first, NZ // 2)] = lines.astype(bf16)

    rows = grad_gate.shape[0]
    outs = (grad_gate, grad_x)
    smalls = sum_small(wire, small, small_y, small_part, small_z, total, heads, y, z, c)
    one = scatter_seq(wire, grads, ready, bufs, outs, y, z, 0, 48)
    two = scatter_seq(wire, grads, lambda block: None, bufs, outs, y, z, 48, rows - 48)
    chans = gather_chan(wire, gained, full_gained, c, gained.shape[0])
    in_order(smalls, chans, one, chans, smalls, one, chans, one, two, one, chans)
    in_order(two, smalls, two, two, chans, smalls, chans)
    own.wait()
    weights.wait()

    def project_back(step, carry):
        cols = pl.ds(pl.multiple_of(step * 256, 256), 256)
        acc = 0.0
        for at in range(NCHAN):
            acc = acc + lax.dot_general(
                out_cols[at], full_gained[at, :, cols], BY_ROWS, preferred_element_type=f32
            )
        for at in range(2):
            tile = 2 * step + at
            lanes = pl.ds(pl.multiple_of(tile * LANES, LANES), LANES)
            scale = facts[tile, VOCAB : VOCAB + 1]
            summed = resid[:, lanes].astype(f32) + scale * acc[:, at * LANES : (at + 1) * LANES]
            new_resid[:, lanes] = summed.astype(bf16)
        return carry

    lax.fori_loop(0, new_resid.shape[1] // 256, project_back, 0)
    acc = 0.0
    for at in range(NCHAN):
        head = heads[at]
        high = head.astype(bf16)
        low = (head - high.astype(f32)).astype(bf16)
        acc = acc + jnp.dot(
            jnp.concatenate([high, low], axis=0), out_cols[at], preferred_element_type=f32
        )
    grad_head[...] = total[pl.ds(VOCAB, VOCAB), :] + acc[:VOCAB] + acc[VOCAB:]
    s = y * NZ + z
    per_chan = width // rows
    mine = heads[s // per_chan]
    here = jnp.zeros((VOCAB, rows), f32)
    for at in range(per_chan):
        chosen = (lax.rem(s, per_chan) == at).astype(f32)
        here = here + chosen * mine[:, at * rows : (at + 1) * rows]
    grad_out[...] = lax.dot_general(
        here, head_t[...].astype(f32), BY_ROWS, precision=EXACT, preferred_element_type=f32
    )
    in_order(one, two)
    wire.finish()


def finish_grads(features, dgate, dx, small, gained, w_out, resid, facts, head_t):
    f32, bf16 = jnp.float32, jnp.bfloat16
    anywhere = pl.BlockSpec(memory_space=pl.ANY)
    vmem = pl.BlockSpec(memory_space=pltpu.VMEM)
    tokens, width = dgate.shape
    _, depth, _ = w_out.shape
    rows = INNER // (NY * NZ)
    copies = 80
    cols = 2 * width
    half = (NZ // 2, rows, cols)
    line = (NZ, rows, cols)
    block = jax.ShapeDtypeStruct((rows, width), f32)
    return pl.pallas_call(
        grads_kernel,
        name="finish_grads",
        out_shape=(
            block,
            block,
            jax.ShapeDtypeStruct(small.shape, f32),
            block,
            jax.ShapeDtypeStruct((VOCAB, width), f32),
            jax.ShapeDtypeStruct(resid.shape, bf16),
        ),
        in_specs=[anywhere, vmem, vmem, vmem, anywhere, anywhere, vmem, vmem, vmem],
        out_specs=(vmem,) * 6,
        scratch_shapes=[
            pltpu.VMEM(features.shape, bf16),
            pltpu.VMEM((tokens, cols), bf16),
            pltpu.VMEM((NY, NZ, rows, cols), bf16),
            pltpu.VMEM((NCHAN, *gained.shape), bf16),
            pltpu.VMEM(w_out.shape, bf16),
            pltpu.VMEM((NCHAN, VOCAB, width), f32),
        ]
        + [pltpu.VMEM(half, bf16)] * 4
        + [pltpu.VMEM(line, bf16)] * 3
        + [
            pltpu.VMEM((NZ - 1, rows, cols), bf16),
            pltpu.VMEM((NY, *small.shape), f32),
            pltpu.VMEM(small.shape, f32),
            pltpu.VMEM((NZ, *small.shape), f32),
            pltpu.SemaphoreType.DMA((copies,)),
            pltpu.SemaphoreType.DMA((copies,)),
            pltpu.SemaphoreType.DMA((NCHAN + 2,)),
        ],
        compiler_params=pltpu.CompilerParams(
            collective_id=2, has_side_effects=True, vmem_limit_bytes=VMEM_BYTES
        ),
        cost_estimate=pl.CostEstimate(flops=10**10, bytes_accessed=10**8, transcendentals=0),
    )(features, dgate, dx, small, gained, w_out, resid, facts, head_t)


BY_ROWS = (((0,), (0,)), ((), ()))


def sum_of_dots(left, right):
    acc = 0.0
    for at in range(left.shape[0]):
        acc = acc + lax.dot_general(
            left[at], right[at], BY_ROWS, preferred_element_type=jnp.float32
        )
    return acc


def project_kernel(left, right, gate, xs):
    acc = sum_of_dots(left, right)
    width = gate.shape[1]
    gate[...] = acc[:, :width].astype(gate.dtype)
    xs[...] = acc[:, width:].astype(xs.dtype)


def project(left, right):
    parts, depth, tokens = left.shape
    tile, width = 256, right.shape[2] // 2
    half = pl.BlockSpec((tile, width), lambda i: (i, 0))
    return pl.pallas_call(
        project_kernel,
        name="project",
        grid=(tokens // tile,),
        out_shape=(jax.ShapeDtypeStruct((tokens, width), jnp.bfloat16),) * 2,
        in_specs=[
            pl.BlockSpec((parts, depth, tile), lambda i: (0, 0, i)),
            pl.BlockSpec(right.shape, lambda i: (0, 0, 0), pipeline_mode=pl.Buffered(1)),
        ],
        out_specs=(half, half),
        compiler_params=pltpu.CompilerParams(vmem_limit_bytes=VMEM_BYTES),
    )(left, right)


def slope(value, sig):
    return sig * (1.0 + value * (1.0 - sig))


def per_device(
    targets, resid, w_gate_in, w_x_in, conv_weight, conv_bias, skip_d, norm_gain, w_out, w_head
):
    f32 = jnp.float32
    local_inner = w_gate_in.shape[1]
    head_t, resid_t = w_head.T, resid.T
    features, full, mix_t = gather_all(resid_t, w_gate_in, w_x_in, w_out, head_t)
    gate_pre, x_pre = project(features, full.reshape(NCHAN, local_inner, 2 * local_inner))
    params = jnp.concatenate(
        [
            conv_weight,
            conv_bias[None],
            jnp.repeat(skip_d, HEADDIM)[None],
            norm_gain[None],
            jnp.zeros((1, local_inner), f32),
        ],
        axis=0,
    )
    dgate, dx_pre, small, gained, facts, out_cols = middle(
        gate_pre,
        x_pre,
        resid_t,
        head_t,
        mix_t,
        params,
        targets.reshape(NCHAN, 1, LANES),
        w_out,
    )
    grad_gate_in, grad_x_in, total, grad_out, grad_head_t, new_resid_t = finish_grads(
        features,
        dgate,
        dx_pre,
        small,
        gained,
        out_cols.reshape(NCHAN, local_inner, local_inner),
        resid_t,
        facts,
        head_t,
    )
    at = 2 * VOCAB
    grad_conv_weight = total[at : at + KERNEL]
    grad_conv_bias = total[at + KERNEL]
    grad_gain = total[at + KERNEL + 1]
    grad_skip = total[at + KERNEL + 2].reshape(-1, HEADDIM).sum(axis=1)
    return (
        new_resid_t.T,
        grad_gate_in,
        grad_x_in,
        grad_out,
        grad_head_t.T,
        grad_conv_weight,
        grad_conv_bias,
        grad_skip,
        grad_gain,
    )


def solution(mesh):
    return jax.shard_map(
        per_device,
        mesh=mesh,
        in_specs=(
            P("seq"),
            P("seq", "chan"),
            P("seq", "chan"),
            P("seq", "chan"),
            P(None, "chan"),
            P("chan"),
            P("chan"),
            P("chan"),
            P("seq", "chan"),
            P("chan", None),
        ),
        out_specs=(
            P("seq", "chan"),
            P("seq", "chan"),
            P("seq", "chan"),
            P("seq", "chan"),
            P("chan", None),
            P(None, "chan"),
            P("chan"),
            P("chan"),
            P("chan"),
        ),
        check_vma=False,
    )
```

```python
import jax
import jax.numpy as jnp
from jax import lax
from jax.experimental import pallas as pl
from jax.experimental.pallas import tpu as pltpu
from jax.sharding import PartitionSpec as P

HEADDIM = 64
KERNEL = 4
VOCAB = 16
INNER = 2560
NX, NY, NZ = 4, 4, 8
NCHAN = 2 * NX
MESH = pl.DeviceIdType.MESH
VMEM_BYTES = 56 * 1024 * 1024


class Wire:
    def __init__(self, send, recv):
        self.send, self.recv, self.copies = send, recv, []

    def put(self, source, target, **where):
        place = len(self.copies)
        copy = pltpu.make_async_remote_copy(
            src_ref=source,
            dst_ref=target,
            send_sem=self.send.at[place],
            recv_sem=self.recv.at[place],
            device_id=where,
            device_id_type=MESH,
        )
        copy.start()
        self.copies.append(copy)
        return copy

    def finish(self):
        for copy in self.copies:
            copy.wait_send()


def greet(peers):
    barrier = pltpu.get_barrier_semaphore()
    for peer in peers:
        pl.semaphore_signal(barrier, inc=1, device_id=peer, device_id_type=MESH)
    pl.semaphore_wait(barrier, len(peers))


def in_order(*streams):
    for stream in streams:
        next(stream, None)


def place():
    s, c = lax.axis_index("seq"), lax.axis_index("chan")
    return s // NZ, s % NZ, c


def gather_chan(wire, shard, full, c, rows):
    x, core = c // 2, c % 2
    mate = c + 1 - 2 * core
    right = lax.rem(x + 1, NX) * 2 + core
    left = lax.rem(x + NX - 1, NX) * 2 + core
    across = lax.rem(x + 2, NX) * 2 + core
    lo, hi = pl.ds(0, rows // 2), pl.ds(rows // 2, rows // 2)
    to_right_lo = wire.put(shard.at[lo], full.at[c, lo], chan=right)
    to_left_hi = wire.put(shard.at[hi], full.at[c, hi], chan=left)
    yield
    to_right_hi = wire.put(shard.at[hi], full.at[c, hi], chan=right)
    to_left_lo = wire.put(shard.at[lo], full.at[c, lo], chan=left)
    to_mate = [wire.put(shard, full.at[c], chan=mate)]
    yield
    to_right_lo.wait_recv()
    on_right = wire.put(full.at[left, lo], full.at[left, lo], chan=right)
    to_left_hi.wait_recv()
    on_left = wire.put(full.at[right, hi], full.at[right, hi], chan=left)
    yield
    to_right_hi.wait_recv()
    to_mate.append(wire.put(full.at[left], full.at[left], chan=mate))
    to_left_lo.wait_recv()
    to_mate.append(wire.put(full.at[right], full.at[right], chan=mate))
    yield
    on_right.wait_recv()
    to_mate.append(wire.put(full.at[across, lo], full.at[across, lo], chan=mate))
    on_left.wait_recv()
    to_mate.append(wire.put(full.at[across, hi], full.at[across, hi], chan=mate))
    yield
    for copy in to_mate:
        copy.wait_recv()


def ring_z(wire, first, block, halves, y, z):
    up, down = y * NZ + lax.rem(z + 1, NZ), y * NZ + lax.rem(z + NZ - 1, NZ)
    plus = wire.put(first, block(z), seq=up)
    minus = wire.put(first, block(z), seq=down)
    for step in range(1, NZ // 2):
        last = step == NZ // 2 - 1
        yield
        behind, ahead = lax.rem(z + NZ - step, NZ), lax.rem(z + step, NZ)
        plus.wait_recv()
        moved = halves(behind)[0] if last else block(behind)
        plus = wire.put(moved, moved, seq=up)
        minus.wait_recv()
        moved = halves(ahead)[1] if last else block(ahead)
        minus = wire.put(moved, moved, seq=down)
    yield
    plus.wait_recv()
    minus.wait_recv()


def exchange_y(wire, shard, full, y, z, rows):
    puts = [
        wire.put(shard.at[rows], full.at[y, z, rows], seq=lax.rem(y + d, NY) * NZ + z)
        for d in (1, 3, 2)
    ]
    yield
    for copy in puts:
        copy.wait_recv()


def ring_z_columns(wire, full, y, z, rows):
    yield from ring_z(
        wire,
        full.at[:, z, rows],
        lambda at: full.at[:, at, rows],
        lambda at: (full.at[pl.ds(0, 2), at, rows], full.at[pl.ds(2, 2), at, rows]),
        y,
        z,
    )


def gather_z_then_y(wire, shard, full, y, z, rows):
    above, below = lax.rem(y + 1, NY), lax.rem(y + NY - 1, NY)
    y_up, y_down = above * NZ + z, below * NZ + z
    z_up, z_down = y * NZ + lax.rem(z + 1, NZ), y * NZ + lax.rem(z + NZ - 1, NZ)
    waiting, rest = [], []

    def spread(source, at, upward):
        block = full.at[y, at, rows]
        up, down = wire.put(source, block, seq=y_up), wire.put(source, block, seq=y_down)
        waiting.append((up, down, at, upward))

    def pass_on(count):
        for up, down, at, upward in waiting[:count]:
            if upward:
                up.wait_recv()
                block = full.at[below, at, rows]
                rest.extend([down, wire.put(block, block, seq=y_up)])
            else:
                down.wait_recv()
                block = full.at[above, at, rows]
                rest.extend([up, wire.put(block, block, seq=y_down)])
        del waiting[:count]

    own = full.at[y, z, rows]
    plus, minus = wire.put(shard.at[rows], own, seq=z_up), wire.put(shard.at[rows], own, seq=z_down)
    spread(shard.at[rows], z, True)
    for step in range(1, NZ // 2 + 1):
        yield
        before = len(waiting)
        behind = lax.rem(z + NZ - step, NZ)
        plus.wait_recv()
        block = full.at[y, behind, rows]
        if step < NZ // 2:
            plus = wire.put(block, block, seq=z_up)
        spread(block, behind, step < NZ // 2)
        if step < NZ // 2:
            ahead = lax.rem(z + step, NZ)
            minus.wait_recv()
            block = full.at[y, ahead, rows]
            if step < NZ // 2 - 1:
                minus = wire.put(block, block, seq=z_down)
            spread(block, ahead, False)
        pass_on(before)
    yield
    pass_on(len(waiting))
    yield
    for copy in rest:
        copy.wait_recv()


def gather_mix(wire, w_out, w_head, out, bufs, y, z, c):
    part, got_c, mine, line, picked = bufs
    rows = w_out.shape[0]
    part[...] = jnp.zeros_like(part)
    part[:, pl.ds(0, rows)] = lax.dot_general(
        w_head[...],
        w_out[...],
        (((1,), (1,)), ((), ())),
        preferred_element_type=jnp.float32,
    )
    puts = [
        wire.put(part, got_c.at[d - 1], chan=lax.rem(c + d, NCHAN)) for d in range(1, NCHAN)
    ]
    yield
    acc = part[...]
    for d in range(1, NCHAN):
        puts[d - 1].wait_recv()
        acc = acc + got_c[d - 1]
    mine[...] = acc
    line[z] = acc
    puts = [
        wire.put(mine, line.at[z], seq=y * NZ + lax.rem(z + d, NZ)) for d in range(1, NZ)
    ]
    yield
    for copy in puts:
        copy.wait_recv()
    kept = pl.ds((c % 2) * (NZ // 2), NZ // 2)
    puts = [
        wire.put(line.at[kept], picked.at[y], seq=lax.rem(y + d, NY) * NZ + z)
        for d in range(1, NY)
    ]
    picked[y] = line[kept]
    yield
    for copy in puts:
        copy.wait_recv()
    for at in range(NZ // 2):
        out[:, pl.ds(at * rows, rows)] = picked[c // 2, at][:, :rows]


def gather_kernel(
    resid,
    w_gate,
    w_x,
    w_out,
    w_head,
    features,
    gate,
    xs,
    out_lines,
    mix,
    full_resid,
    full_weights,
    acc,
    weights,
    *scratch,
):
    *mix_bufs, send, recv, local = scratch
    y, z, c = place()
    half = w_gate.shape[1]
    weights[:, pl.ds(0, half)] = w_gate[...]
    weights[:, pl.ds(half, half)] = w_x[...]
    greet(
        [{"chan": lax.rem(c + d, NCHAN)} for d in range(1, NCHAN)]
        + [{"seq": lax.rem(y + d, NY) * NZ + z} for d in range(1, NY)]
        + [{"seq": y * NZ + lax.rem(z + d, NZ)} for d in range(1, NZ)]
    )
    wire = Wire(send, recv)
    own_weights = pltpu.make_async_copy(weights, full_weights.at[y, z], local.at[0])
    own_resid = pltpu.make_async_copy(resid, full_resid.at[c], local.at[1])
    own_weights.start()
    own_resid.start()
    rows, first = weights.shape[0], 32
    one, rest = pl.ds(0, first), pl.ds(first, rows - first)
    lines = gather_z_then_y(wire, weights, full_weights, y, z, rest)
    own_y = exchange_y(wire, weights, full_weights, y, z, one)
    columns = ring_z_columns(wire, full_weights, y, z, one)
    chans = gather_chan(wire, resid, full_resid, c, resid.shape[0])
    mixes = gather_mix(wire, w_out, w_head, mix, mix_bufs, y, z, c)
    in_order(own_y, lines, chans, mixes, own_y)
    own_weights.wait()
    in_order(columns, lines, chans, mixes, lines, columns, mixes, lines, chans)
    out_lines[y] = w_out[...]
    out_puts = [
        wire.put(w_out, out_lines.at[y], seq=lax.rem(y + d, NY) * NZ + z) for d in (1, 3, 2)
    ]
    in_order(columns, lines, mixes, columns, chans, columns, lines, lines)
    own_resid.wait()
    tile = 256
    width = gate.shape[1]
    x, core = c // 2, c % 2

    def project(blocks, first, last):
        def step(at, carry):
            cols = pl.ds(pl.multiple_of(at * tile, tile), tile)
            total = 0.0 if first else acc[cols, :]
            for block in blocks:
                part = full_weights[block // 2, pl.ds((block % 2) * (NZ // 2), NZ // 2)]
                total = total + lax.dot_general(
                    full_resid[block, :, cols],
                    part.reshape(part.shape[0] * part.shape[1], part.shape[2]),
                    BY_ROWS,
                    preferred_element_type=jnp.float32,
                )
            if last:
                gate[cols, :] = total[:, :width].astype(gate.dtype)
                xs[cols, :] = total[:, width:].astype(xs.dtype)
            else:
                acc[cols, :] = total
            return carry

        lax.fori_loop(0, acc.shape[0] // tile, step, 0)

    mate = c + 1 - 2 * core
    left = lax.rem(x + NX - 1, NX) * 2 + core
    right = lax.rem(x + 1, NX) * 2 + core
    project([c, left, right], True, False)
    in_order(chans, chans)
    out = pltpu.make_async_copy(full_resid, features, local.at[1])
    out.start()
    across = lax.rem(x + 2, NX) * 2 + core
    flip = 1 - 2 * core
    project([mate, left + flip, right + flip, across, across + flip], False, True)
    for copy in out_puts:
        copy.wait_recv()
    out.wait()
    wire.finish()


def gather_all(resid, w_gate, w_x, w_out, w_head):
    anywhere = pl.BlockSpec(memory_space=pl.ANY)
    vmem = pl.BlockSpec(memory_space=pltpu.VMEM)
    f32 = jnp.float32
    copies = 96
    block = (VOCAB, 128)
    rows, half = w_gate.shape
    tokens = resid.shape[1]
    return pl.pallas_call(
        gather_kernel,
        name="gather_all",
        out_shape=(
            jax.ShapeDtypeStruct((NCHAN, *resid.shape), resid.dtype),
            jax.ShapeDtypeStruct((tokens, half), resid.dtype),
            jax.ShapeDtypeStruct((tokens, half), resid.dtype),
            jax.ShapeDtypeStruct((NY, *w_out.shape), w_out.dtype),
            jax.ShapeDtypeStruct((VOCAB, resid.shape[0]), f32),
        ),
        in_specs=[vmem] * 5,
        out_specs=(anywhere, vmem, vmem, vmem, vmem),
        scratch_shapes=[
            pltpu.VMEM((NCHAN, *resid.shape), resid.dtype),
            pltpu.VMEM((NY, NZ, rows, 2 * half), w_gate.dtype),
            pltpu.VMEM((tokens, 2 * half), f32),
            pltpu.VMEM((rows, 2 * half), w_gate.dtype),
            pltpu.VMEM(block, f32),
            pltpu.VMEM((NCHAN - 1, *block), f32),
            pltpu.VMEM(block, f32),
            pltpu.VMEM((NZ, *block), f32),
            pltpu.VMEM((NY, NZ // 2, *block), f32),
            pltpu.SemaphoreType.DMA((copies,)),
            pltpu.SemaphoreType.DMA((copies,)),
            pltpu.SemaphoreType.DMA((2,)),
        ],
        compiler_params=pltpu.CompilerParams(
            collective_id=0, has_side_effects=True, vmem_limit_bytes=VMEM_BYTES
        ),
        cost_estimate=pl.CostEstimate(flops=10**10, bytes_accessed=10**8, transcendentals=0),
    )(resid, w_gate, w_x, w_out, w_head)


EXACT = lax.Precision.HIGHEST
LANES = 128
EDGE = 16
SUMS = 40
FACTS = 24


def middle_kernel(
    gate,
    xs,
    resid,
    head_t,
    mix_t,
    conv_weight,
    conv_bias,
    norm_gain,
    skip_d,
    targets,
    out_lines,
    dgate,
    dx,
    small,
    gained,
    facts,
    full_w_out,
    padded,
    prods,
    to_gate,
    to_conv,
    sums,
    parts,
    mine,
    before,
    after,
    acc_rows,
    acc_heads,
    send,
    recv,
    w_send,
    w_recv,
    local,
):
    f32, bf16 = jnp.float32, jnp.bfloat16
    tokens = gate.shape[0]
    y, z, c = place()
    s = y * NZ + z
    last_seq = NY * NZ - 1
    later, sooner = lax.rem(s + 1, NY * NZ), lax.rem(s + last_seq, NY * NZ)
    greet(
        [{"chan": lax.rem(c + d, NCHAN)} for d in range(1, NCHAN)]
        + [{"seq": later}, {"seq": sooner}]
        + [{"seq": y * NZ + lax.rem(z + d, NZ)} for d in (1, NZ - 1)]
    )
    wire = Wire(w_send, w_recv)
    own_lines = pltpu.make_async_copy(out_lines, full_w_out.at[:, z], local.at[0])
    own_lines.start()
    columns = ring_z(
        wire,
        out_lines,
        lambda at: full_w_out.at[:, at],
        lambda at: (full_w_out.at[pl.ds(0, 2), at], full_w_out.at[pl.ds(2, 2), at]),
        y,
        z,
    )

    def copy_of(source, target, at, where):
        return pltpu.make_async_remote_copy(
            src_ref=source,
            dst_ref=target,
            send_sem=send.at[at],
            recv_sem=recv.at[at],
            device_id=where,
            device_id_type=MESH,
        )

    edge = copy_of(xs.at[pl.ds(tokens - EDGE, EDGE)], before, 2 * NCHAN, {"seq": later})
    edge.start()
    in_order(columns)
    taps = [conv_weight[k : k + 1, :] for k in range(KERNEL)]
    bias, gain = conv_bias[...], norm_gain[...]
    head = lax.broadcasted_iota(jnp.int32, bias.shape, 1) // HEADDIM
    skip = jnp.zeros(bias.shape, f32)
    for at in range(skip_d.shape[0]):
        skip = jnp.where(head == at, skip_d[at], skip)
    mix = mix_t[...]
    padded[pl.ds(EDGE, tokens), :] = xs[...].astype(f32)

    def window(tile):
        start = pl.multiple_of(tile * LANES, LANES)
        return pl.ds(start, LANES), padded[pl.ds(start, LANES + EDGE), :]

    def shifted(win, k):
        first = EDGE - (KERNEL - 1) + k
        return win[first : first + LANES]

    def share(step):
        peer = lax.rem(c + 1 + step, NCHAN)
        return copy_of(sums.at[peer], parts.at[step], step, {"chan": peer})

    def forward(tile):
        rows, win = window(tile)
        conv = bias + taps[0] * shifted(win, 0)
        for k in range(1, KERNEL):
            conv = conv + taps[k] * shifted(win, k)
        sig_conv = jax.nn.sigmoid(conv)
        active = conv * sig_conv
        gate_pre = gate[rows, :].astype(f32)
        sig_gate = jax.nn.sigmoid(gate_pre)
        silu_gate = gate_pre * sig_gate
        prod = active * silu_gate
        prods[rows, :] = prod
        to_gate[rows, :] = skip * active * slope(gate_pre, sig_gate)
        to_conv[rows, :] = skip * silu_gate * slope(conv, sig_conv)
        gated = prod * skip
        with_gain = gated * gain
        gained[:, rows] = with_gain.T.astype(bf16)
        by_lanes = (((1,), (1,)), ((), ()))
        sums[tile, pl.ds(0, VOCAB)] = lax.dot_general(
            head_t[...],
            resid[:, rows],
            (((1,), (0,)), ((), ())),
            preferred_element_type=f32,
        )
        sums[tile, pl.ds(VOCAB, VOCAB)] = lax.dot_general(
            mix, with_gain, by_lanes, precision=EXACT, preferred_element_type=f32
        )
        sums[tile, pl.ds(2 * VOCAB, 8)] = lax.dot_general(
            jnp.ones((8, gated.shape[1]), f32),
            gated * gated,
            by_lanes,
            precision=EXACT,
            preferred_element_type=f32,
        )

    edge.wait_recv()
    padded[pl.ds(0, EDGE), :] = before[...].astype(f32) * (s > 0).astype(f32)

    def forward_step(step, carry):
        forward(lax.rem(c + 1 + step, NCHAN))
        share(step).start()
        return carry

    lax.fori_loop(0, NCHAN - 1, forward_step, 0)
    forward(c)
    in_order(columns)
    total = sums[c]
    for step in range(NCHAN - 1):
        share(step).wait_recv()
        total = total + parts[step]
    inverse = lax.rsqrt(total[2 * VOCAB : 2 * VOCAB + 1] / INNER + 1e-05)
    gained_head = total[VOCAB : 2 * VOCAB]
    raised = jnp.exp(total[:VOCAB] + inverse * gained_head)
    probs = raised / jnp.sum(raised, axis=0, keepdims=True)
    words = lax.broadcasted_iota(jnp.int32, (VOCAB, LANES), 0)
    onehot = (words == targets[c]).astype(f32)
    weight = 4.0 / float(tokens * NY * NZ) ** 0.5
    dlogit = (probs - onehot) * weight
    dot_gn = jnp.sum(dlogit * gained_head, axis=0, keepdims=True)
    mine[pl.ds(0, VOCAB), :] = dlogit
    mine[pl.ds(VOCAB, 8), :] = jnp.concatenate(
        [inverse, inverse * inverse * inverse * dot_gn / INNER, jnp.zeros((6, LANES), f32)],
        axis=0,
    )
    facts[c] = mine[...]

    def tell(d):
        return copy_of(
            mine, facts.at[c], NCHAN - 1 + d, {"chan": lax.rem(c + d, NCHAN)}
        )

    for d in range(1, NCHAN):
        tell(d).start()
    acc_rows[...] = jnp.zeros_like(acc_rows)
    acc_heads[...] = jnp.zeros_like(acc_heads)
    for d in range(1, NCHAN):
        tell(d).wait_recv()
    in_order(columns)
    second = (
        lax.broadcasted_iota(jnp.int32, (8, mix.shape[1]), 0) == 1
    ).astype(f32)

    def fold(value):
        return jnp.sum(value.reshape(LANES // 8, 8, value.shape[1]), axis=0)

    def backward(tile):
        rows, win = window(tile)
        fact = facts[tile]
        dlogit = fact[:VOCAB]
        scaled = dlogit * fact[VOCAB : VOCAB + 1]
        by_rows = (((0,), (0,)), ((), ()))
        dnormed = lax.dot_general(
            scaled, mix, by_rows, precision=EXACT, preferred_element_type=f32
        )
        pull = lax.dot_general(
            fact[VOCAB : VOCAB + 8], second, by_rows, precision=EXACT, preferred_element_type=f32
        )
        prod = prods[rows, :]
        dgated = gain * dnormed - skip * prod * pull
        dgate[rows, :] = (dgated * to_gate[rows, :]).astype(bf16)
        dconv = dgated * to_conv[rows, :]
        to_conv[rows, :] = dconv
        for k in range(KERNEL):
            acc_rows[k] += fold(dconv * shifted(win, k))
        acc_rows[KERNEL] += fold(dconv)
        acc_rows[KERNEL + 1] += fold(dgated * prod)
        acc_heads[0] += jnp.dot(scaled, prod, precision=EXACT, preferred_element_type=f32)
        acc_heads[1] += lax.dot_general(
            dlogit,
            resid[:, rows].astype(f32),
            (((1,), (1,)), ((), ())),
            precision=EXACT,
            preferred_element_type=f32,
        )

    backward(0)
    first_rows = copy_of(to_conv.at[pl.ds(0, 8)], after, 2 * NCHAN + 1, {"seq": sooner})
    first_rows.start()

    def backward_step(tile, carry):
        backward(tile)
        return carry

    lax.fori_loop(1, tokens // LANES, backward_step, 0)
    in_order(columns)
    by_channel = acc_heads[0]
    small[pl.ds(0, VOCAB), :] = by_channel * skip * gain
    small[pl.ds(VOCAB, VOCAB), :] = acc_heads[1]
    lines = [jnp.sum(acc_rows[k], axis=0, keepdims=True) for k in range(KERNEL + 2)]
    lines.insert(KERNEL + 1, skip * jnp.sum(mix * by_channel, axis=0, keepdims=True))
    lines.append(jnp.zeros_like(skip))
    small[pl.ds(2 * VOCAB, 8), :] = jnp.concatenate(lines, axis=0)
    first_rows.wait_recv()
    to_conv[pl.ds(tokens, 8), :] = after[...] * (s < last_seq).astype(f32)

    def spread_step(tile, carry):
        start = pl.multiple_of(tile * LANES, LANES)
        win = to_conv[pl.ds(start, LANES + 8), :]
        acc = taps[KERNEL - 1] * win[0:LANES]
        for k in range(KERNEL - 1):
            acc = acc + taps[k] * win[KERNEL - 1 - k : KERNEL - 1 - k + LANES]
        dx[pl.ds(start, LANES), :] = acc.astype(bf16)
        return carry

    lax.fori_loop(0, tokens // LANES, spread_step, 0)
    in_order(columns)
    wire.finish()
    own_lines.wait()
    edge.wait_send()
    first_rows.wait_send()
    for d in range(1, NCHAN):
        share(d - 1).wait_send()
        tell(d).wait_send()


def middle(gate, xs, *others):
    f32, bf16 = jnp.float32, jnp.bfloat16
    vmem = pl.BlockSpec(memory_space=pltpu.VMEM)
    anywhere = pl.BlockSpec(memory_space=pl.ANY)
    tokens, width = gate.shape
    copies = 2 * NCHAN + 2
    return pl.pallas_call(
        middle_kernel,
        name="middle",
        out_shape=(
            jax.ShapeDtypeStruct((tokens, width), bf16),
            jax.ShapeDtypeStruct((tokens, width), bf16),
            jax.ShapeDtypeStruct((SUMS, width), f32),
            jax.ShapeDtypeStruct((width, tokens), bf16),
            jax.ShapeDtypeStruct((NCHAN, FACTS, LANES), f32),
            jax.ShapeDtypeStruct((NY, NZ, *others[-1].shape[1:]), bf16),
        ),
        in_specs=[vmem] * 8 + [pl.BlockSpec(memory_space=pltpu.SMEM), vmem, anywhere],
        out_specs=(vmem,) * 5 + (anywhere,),
        scratch_shapes=[
            pltpu.VMEM((tokens + EDGE, width), f32),
            pltpu.VMEM((tokens, width), f32),
            pltpu.VMEM((tokens, width), f32),
            pltpu.VMEM((tokens + 8, width), f32),
            pltpu.VMEM((NCHAN, SUMS, LANES), f32),
            pltpu.VMEM((NCHAN - 1, SUMS, LANES), f32),
            pltpu.VMEM((FACTS, LANES), f32),
            pltpu.VMEM((EDGE, width), bf16),
            pltpu.VMEM((8, width), f32),
            pltpu.VMEM((KERNEL + 2, 8, width), f32),
            pltpu.VMEM((2, VOCAB, width), f32),
            pltpu.SemaphoreType.DMA((copies,)),
            pltpu.SemaphoreType.DMA((copies,)),
            pltpu.SemaphoreType.DMA((NZ,)),
            pltpu.SemaphoreType.DMA((NZ,)),
            pltpu.SemaphoreType.DMA((1,)),
        ],
        compiler_params=pltpu.CompilerParams(
            collective_id=1, has_side_effects=True, vmem_limit_bytes=VMEM_BYTES
        ),
        cost_estimate=pl.CostEstimate(flops=10**10, bytes_accessed=10**7, transcendentals=0),
    )(gate, xs, *others)


def scatter_seq(wire, grads, ready, bufs, outs, y, z, start, count):
    f32, bf16 = jnp.float32, jnp.bfloat16
    from_below, from_above, via_up, via_down, got_below, got_above, lines, got_z = bufs
    rows = pl.ds(start, count)
    lo, hi = pl.ds(0, NZ // 2), pl.ds(NZ // 2, NZ // 2)
    above, below, across = lax.rem(y + 1, NY), lax.rem(y + 3, NY), lax.rem(y + 2, NY)
    up, down = above * NZ + z, below * NZ + z
    ready(2 * across)
    half_up = wire.put(grads.at[across, lo, rows], from_below.at[:, rows], seq=up)
    ready(2 * across + 1)
    half_down = wire.put(grads.at[across, hi, rows], from_above.at[:, rows], seq=down)
    ready(2 * above + 1)
    moves = [wire.put(grads.at[above, hi, rows], got_below.at[hi, rows], seq=up)]
    ready(2 * below)
    moves.append(wire.put(grads.at[below, lo, rows], got_above.at[lo, rows], seq=down))
    ready(2 * above)
    ready(2 * below + 1)
    yield
    half_up.wait_recv()
    via_up[:, rows] = (
        grads[above, lo, rows].astype(f32) + from_below[:, rows].astype(f32)
    ).astype(bf16)
    moves.append(wire.put(via_up.at[:, rows], got_below.at[lo, rows], seq=up))
    half_down.wait_recv()
    via_down[:, rows] = (
        grads[below, hi, rows].astype(f32) + from_above[:, rows].astype(f32)
    ).astype(bf16)
    moves.append(wire.put(via_down.at[:, rows], got_above.at[hi, rows], seq=down))
    ready(2 * y)
    ready(2 * y + 1)
    yield
    for copy in moves[:2]:
        copy.wait_recv()
    yield
    for copy in moves[2:]:
        copy.wait_recv()
    lines[:, rows] = (
        grads[y, :, rows].astype(f32)
        + got_below[:, rows].astype(f32)
        + got_above[:, rows].astype(f32)
    ).astype(bf16)
    puts = []
    for d in (4, 3, 5, 2, 6, 1, 7):
        peer = lax.rem(z + d, NZ)
        puts.append(wire.put(lines.at[peer, rows], got_z.at[d - 1, rows], seq=y * NZ + peer))
    yield
    acc = (
        grads[y, z, rows].astype(f32)
        + got_below[z, rows].astype(f32)
        + got_above[z, rows].astype(f32)
    )
    for copy in puts:
        copy.wait_recv()
    for d in range(1, NZ):
        acc = acc + got_z[d - 1, rows].astype(f32)
    half = acc.shape[1] // 2
    outs[0][rows] = acc[:, :half]
    outs[1][rows] = acc[:, half:]


def sum_small(wire, small, got_y, part, got_z, total, heads, y, z, c):
    puts = [
        wire.put(small, got_y.at[y], seq=lax.rem(y + d, NY) * NZ + z) for d in range(1, NY)
    ]
    got_y[y] = small[...]
    yield
    for copy in puts:
        copy.wait_recv()
    acc = got_y[0]
    for at in range(1, NY):
        acc = acc + got_y[at]
    part[...] = acc
    puts = [
        wire.put(part, got_z.at[z], seq=y * NZ + lax.rem(z + d, NZ)) for d in range(1, NZ)
    ]
    got_z[z] = acc
    yield
    for copy in puts:
        copy.wait_recv()
    acc = got_z[0]
    for at in range(1, NZ):
        acc = acc + got_z[at]
    total[...] = acc
    first = pl.ds(0, VOCAB)
    puts = [
        wire.put(total.at[first], heads.at[c], chan=lax.rem(c + d, NCHAN))
        for d in range(1, NCHAN)
    ]
    heads[c] = total[first]
    yield
    for copy in puts:
        copy.wait_recv()


def grads_kernel(
    features,
    dgate,
    dx,
    small,
    gained,
    w_out,
    resid,
    facts,
    head_t,
    grad_gate,
    grad_x,
    total,
    grad_out,
    grad_head,
    new_resid,
    *scratch,
):
    f32, bf16 = jnp.float32, jnp.bfloat16
    feats, both, grads, full_gained, out_cols, heads, *rest = scratch
    *bufs, small_y, small_part, small_z, send, recv, local = rest
    y, z, c = place()
    width = dgate.shape[1]
    order = [
        2 * lax.rem(y + 2, NY),
        2 * lax.rem(y + 2, NY) + 1,
        2 * lax.rem(y + 1, NY) + 1,
        2 * lax.rem(y + 3, NY),
        2 * lax.rem(y + 1, NY),
        2 * lax.rem(y + 3, NY) + 1,
        2 * y,
        2 * y + 1,
    ]
    loads = [
        pltpu.make_async_copy(features.at[at], feats.at[step], local.at[step])
        for step, at in enumerate(order)
    ]
    for load in loads:
        load.start()
    own = pltpu.make_async_copy(gained, full_gained.at[c], local.at[NCHAN])
    own.start()
    weights = pltpu.make_async_copy(w_out, out_cols, local.at[NCHAN + 1])
    weights.start()
    both[:, pl.ds(0, width)] = dgate[...]
    both[:, pl.ds(width, width)] = dx[...]
    greet(
        [{"chan": lax.rem(c + d, NCHAN)} for d in range(1, NCHAN)]
        + [{"seq": lax.rem(y + d, NY) * NZ + z} for d in range(1, NY)]
        + [{"seq": y * NZ + lax.rem(z + d, NZ)} for d in range(1, NZ)]
    )
    wire = Wire(send, recv)
    steps = iter(range(NCHAN))

    def ready(block):
        step = next(steps)
        loads[step].wait()
        product = jnp.dot(feats[step], both[...], preferred_element_type=f32)
        lines = product.reshape(NZ // 2, product.shape[0] // (NZ // 2), product.shape[1])
        first = lax.rem(block, 2) * (NZ // 2)
        grads[block // 2, pl.ds(first, NZ // 2)] = lines.astype(bf16)

    rows = grad_gate.shape[0]
    outs = (grad_gate, grad_x)
    smalls = sum_small(wire, small, small_y, small_part, small_z, total, heads, y, z, c)
    one = scatter_seq(wire, grads, ready, bufs, outs, y, z, 0, 32)
    two = scatter_seq(wire, grads, lambda block: None, bufs, outs, y, z, 32, 32)
    three = scatter_seq(wire, grads, lambda block: None, bufs, outs, y, z, 64, rows - 64)
    chans = gather_chan(wire, gained, full_gained, c, gained.shape[0])
    in_order(smalls, chans, one, chans, smalls, one, chans, one, two, one, chans, two, smalls)
    in_order(two, three, two, three, chans, three, three, smalls, chans)
    own.wait()
    weights.wait()

    def project_back(step, carry):
        cols = pl.ds(pl.multiple_of(step * 256, 256), 256)
        acc = 0.0
        for at in range(NCHAN):
            acc = acc + lax.dot_general(
                out_cols[at], full_gained[at, :, cols], BY_ROWS, preferred_element_type=f32
            )
        for at in range(2):
            tile = 2 * step + at
            lanes = pl.ds(pl.multiple_of(tile * LANES, LANES), LANES)
            scale = facts[tile, VOCAB : VOCAB + 1]
            summed = resid[:, lanes].astype(f32) + scale * acc[:, at * LANES : (at + 1) * LANES]
            new_resid[:, lanes] = summed.astype(bf16)
        return carry

    lax.fori_loop(0, new_resid.shape[1] // 256, project_back, 0)
    acc = 0.0
    for at in range(NCHAN):
        head = heads[at]
        high = head.astype(bf16)
        low = (head - high.astype(f32)).astype(bf16)
        acc = acc + jnp.dot(
            jnp.concatenate([high, low], axis=0),
            out_cols[at],
            preferred_element_type=f32,
        )
    grad_head[...] = total[pl.ds(VOCAB, VOCAB), :] + acc[:VOCAB] + acc[VOCAB:]
    s = y * NZ + z
    per_chan = width // rows
    mine = heads[s // per_chan]
    here = jnp.zeros((VOCAB, rows), f32)
    for at in range(per_chan):
        chosen = (lax.rem(s, per_chan) == at).astype(f32)
        here = here + chosen * mine[:, at * rows : (at + 1) * rows]
    grad_out[...] = lax.dot_general(
        here, head_t[...].astype(f32), BY_ROWS, precision=EXACT, preferred_element_type=f32
    )
    in_order(one, two, three)
    wire.finish()


def finish_grads(features, dgate, dx, small, gained, w_out, resid, facts, head_t):
    f32, bf16 = jnp.float32, jnp.bfloat16
    anywhere = pl.BlockSpec(memory_space=pl.ANY)
    vmem = pl.BlockSpec(memory_space=pltpu.VMEM)
    tokens, width = dgate.shape
    rows = INNER // (NY * NZ)
    copies = 80
    cols = 2 * width
    half = (NZ // 2, rows, cols)
    line = (NZ, rows, cols)
    block = jax.ShapeDtypeStruct((rows, width), f32)
    return pl.pallas_call(
        grads_kernel,
        name="finish_grads",
        out_shape=(
            block,
            block,
            jax.ShapeDtypeStruct(small.shape, f32),
            block,
            jax.ShapeDtypeStruct((VOCAB, width), f32),
            jax.ShapeDtypeStruct(resid.shape, bf16),
        ),
        in_specs=[anywhere, vmem, vmem, vmem, anywhere, anywhere, vmem, vmem, vmem],
        out_specs=(vmem,) * 6,
        scratch_shapes=[
            pltpu.VMEM(features.shape, bf16),
            pltpu.VMEM((tokens, cols), bf16),
            pltpu.VMEM((NY, NZ, rows, cols), bf16),
            pltpu.VMEM((NCHAN, *gained.shape), bf16),
            pltpu.VMEM(w_out.shape, bf16),
            pltpu.VMEM((NCHAN, VOCAB, width), f32),
        ]
        + [pltpu.VMEM(half, bf16)] * 4
        + [pltpu.VMEM(line, bf16)] * 3
        + [
            pltpu.VMEM((NZ - 1, rows, cols), bf16),
            pltpu.VMEM((NY, *small.shape), f32),
            pltpu.VMEM(small.shape, f32),
            pltpu.VMEM((NZ, *small.shape), f32),
            pltpu.SemaphoreType.DMA((copies,)),
            pltpu.SemaphoreType.DMA((copies,)),
            pltpu.SemaphoreType.DMA((NCHAN + 2,)),
        ],
        compiler_params=pltpu.CompilerParams(
            collective_id=2, has_side_effects=True, vmem_limit_bytes=VMEM_BYTES
        ),
        cost_estimate=pl.CostEstimate(flops=10**10, bytes_accessed=10**8, transcendentals=0),
    )(features, dgate, dx, small, gained, w_out, resid, facts, head_t)


BY_ROWS = (((0,), (0,)), ((), ()))


def hand_out_kernel(total, *refs):
    count = len(refs) // 2
    for at in range(count):
        refs[at + count][...] = refs[at][...]
    refs[-1][...] = total[pl.ds(2 * VOCAB, KERNEL), :]


def hand_out(total, *arrays):
    vmem = pl.BlockSpec(memory_space=pltpu.VMEM)
    shapes = [jax.ShapeDtypeStruct(array.shape, array.dtype) for array in arrays]
    shapes.append(jax.ShapeDtypeStruct((KERNEL, total.shape[1]), total.dtype))
    return pl.pallas_call(
        hand_out_kernel,
        name="hand_out",
        out_shape=tuple(shapes),
        in_specs=[vmem] * (len(arrays) + 1),
        out_specs=(vmem,) * len(shapes),
        compiler_params=pltpu.CompilerParams(vmem_limit_bytes=VMEM_BYTES),
    )(total, *arrays)


def slope(value, sig):
    return sig * (1.0 + value * (1.0 - sig))


def per_device(
    targets, resid, w_gate_in, w_x_in, conv_weight, conv_bias, skip_d, norm_gain, w_out, w_head
):
    f32 = jnp.float32
    local_inner = w_gate_in.shape[1]
    head_t, resid_t = w_head.T, resid.T
    features, gate_pre, x_pre, out_lines, mix_t = gather_all(
        resid_t, w_gate_in, w_x_in, w_out, head_t
    )
    dgate, dx_pre, small, gained, facts, out_cols = middle(
        gate_pre,
        x_pre,
        resid_t,
        head_t,
        mix_t,
        conv_weight,
        conv_bias[None],
        norm_gain[None],
        skip_d,
        targets.reshape(NCHAN, 1, LANES),
        out_lines,
    )
    grad_gate_in, grad_x_in, total, *others = finish_grads(
        features,
        dgate,
        dx_pre,
        small,
        gained,
        out_cols.reshape(NCHAN, local_inner, local_inner),
        resid_t,
        facts,
        head_t,
    )
    grad_gate_in, grad_x_in, grad_out, grad_head_t, new_resid_t, grad_conv_weight = hand_out(
        total, grad_gate_in, grad_x_in, *others
    )
    at = 2 * VOCAB
    grad_conv_bias = total[at + KERNEL]
    grad_gain = total[at + KERNEL + 1]
    grad_skip = total[at + KERNEL + 2].reshape(-1, HEADDIM).sum(axis=1)
    return (
        new_resid_t.T,
        grad_gate_in,
        grad_x_in,
        grad_out,
        grad_head_t.T,
        grad_conv_weight,
        grad_conv_bias,
        grad_skip,
        grad_gain,
    )


def solution(mesh):
    return jax.shard_map(
        per_device,
        mesh=mesh,
        in_specs=(
            P("seq"),
            P("seq", "chan"),
            P("seq", "chan"),
            P("seq", "chan"),
            P(None, "chan"),
            P("chan"),
            P("chan"),
            P("chan"),
            P("seq", "chan"),
            P("chan", None),
        ),
        out_specs=(
            P("seq", "chan"),
            P("seq", "chan"),
            P("seq", "chan"),
            P("seq", "chan"),
            P("chan", None),
            P(None, "chan"),
            P("chan"),
            P("chan"),
            P("chan"),
        ),
        check_vma=False,
    )
```

```python
import jax
import jax.numpy as jnp
from jax import lax
from jax.experimental import pallas as pl
from jax.experimental.pallas import tpu as pltpu
from jax.sharding import PartitionSpec as P

HEADDIM = 64
KERNEL = 4
VOCAB = 16
INNER = 2560
NX, NY, NZ = 4, 4, 8
NCHAN = 2 * NX
MESH = pl.DeviceIdType.MESH
VMEM_BYTES = 56 * 1024 * 1024


class Wire:
    def __init__(self, send, recv):
        self.send, self.recv, self.copies = send, recv, []

    def put(self, source, target, **where):
        place = len(self.copies)
        copy = pltpu.make_async_remote_copy(
            src_ref=source,
            dst_ref=target,
            send_sem=self.send.at[place],
            recv_sem=self.recv.at[place],
            device_id=where,
            device_id_type=MESH,
        )
        copy.start()
        self.copies.append(copy)
        return copy

    def finish(self):
        for copy in self.copies:
            copy.wait_send()


def greet(peers):
    barrier = pltpu.get_barrier_semaphore()
    for peer in peers:
        pl.semaphore_signal(barrier, inc=1, device_id=peer, device_id_type=MESH)
    return lambda: pl.semaphore_wait(barrier, len(peers))


def in_order(*streams):
    for stream in streams:
        next(stream, None)


def place():
    s, c = lax.axis_index("seq"), lax.axis_index("chan")
    return s // NZ, s % NZ, c


def gather_chan(wire, shard, full, c, rows):
    x, core = c // 2, c % 2
    mate = c + 1 - 2 * core
    right = lax.rem(x + 1, NX) * 2 + core
    left = lax.rem(x + NX - 1, NX) * 2 + core
    across = lax.rem(x + 2, NX) * 2 + core
    lo, hi = pl.ds(0, rows // 2), pl.ds(rows // 2, rows // 2)
    to_right_lo = wire.put(shard.at[lo], full.at[c, lo], chan=right)
    to_left_hi = wire.put(shard.at[hi], full.at[c, hi], chan=left)
    yield
    to_right_hi = wire.put(shard.at[hi], full.at[c, hi], chan=right)
    to_left_lo = wire.put(shard.at[lo], full.at[c, lo], chan=left)
    to_mate = [wire.put(shard, full.at[c], chan=mate)]
    yield
    to_right_lo.wait_recv()
    on_right = wire.put(full.at[left, lo], full.at[left, lo], chan=right)
    to_left_hi.wait_recv()
    on_left = wire.put(full.at[right, hi], full.at[right, hi], chan=left)
    yield
    to_right_hi.wait_recv()
    to_mate.append(wire.put(full.at[left], full.at[left], chan=mate))
    to_left_lo.wait_recv()
    to_mate.append(wire.put(full.at[right], full.at[right], chan=mate))
    yield
    on_right.wait_recv()
    to_mate.append(wire.put(full.at[across, lo], full.at[across, lo], chan=mate))
    on_left.wait_recv()
    to_mate.append(wire.put(full.at[across, hi], full.at[across, hi], chan=mate))
    yield
    for copy in to_mate:
        copy.wait_recv()


def ring_z(wire, first, block, halves, y, z):
    up, down = y * NZ + lax.rem(z + 1, NZ), y * NZ + lax.rem(z + NZ - 1, NZ)
    plus = wire.put(first, block(z), seq=up)
    minus = wire.put(first, block(z), seq=down)
    for step in range(1, NZ // 2):
        last = step == NZ // 2 - 1
        yield
        behind, ahead = lax.rem(z + NZ - step, NZ), lax.rem(z + step, NZ)
        plus.wait_recv()
        moved = halves(behind)[0] if last else block(behind)
        plus = wire.put(moved, moved, seq=up)
        minus.wait_recv()
        moved = halves(ahead)[1] if last else block(ahead)
        minus = wire.put(moved, moved, seq=down)
    yield
    plus.wait_recv()
    minus.wait_recv()


def exchange_y(wire, shard, full, y, z, rows):
    puts = [
        wire.put(shard.at[rows], full.at[y, z, rows], seq=lax.rem(y + d, NY) * NZ + z)
        for d in (1, 3, 2)
    ]
    yield
    for copy in puts:
        copy.wait_recv()


def ring_z_columns(wire, full, y, z, rows):
    yield from ring_z(
        wire,
        full.at[:, z, rows],
        lambda at: full.at[:, at, rows],
        lambda at: (full.at[pl.ds(0, 2), at, rows], full.at[pl.ds(2, 2), at, rows]),
        y,
        z,
    )


def gather_z_then_y(wire, shard, full, y, z, rows):
    above, below = lax.rem(y + 1, NY), lax.rem(y + NY - 1, NY)
    y_up, y_down = above * NZ + z, below * NZ + z
    z_up, z_down = y * NZ + lax.rem(z + 1, NZ), y * NZ + lax.rem(z + NZ - 1, NZ)
    waiting, rest = [], []

    def spread(source, at, upward):
        block = full.at[y, at, rows]
        up, down = wire.put(source, block, seq=y_up), wire.put(source, block, seq=y_down)
        waiting.append((up, down, at, upward))

    def pass_on(count):
        for up, down, at, upward in waiting[:count]:
            if upward:
                up.wait_recv()
                block = full.at[below, at, rows]
                rest.extend([down, wire.put(block, block, seq=y_up)])
            else:
                down.wait_recv()
                block = full.at[above, at, rows]
                rest.extend([up, wire.put(block, block, seq=y_down)])
        del waiting[:count]

    own = full.at[y, z, rows]
    plus, minus = wire.put(shard.at[rows], own, seq=z_up), wire.put(shard.at[rows], own, seq=z_down)
    spread(shard.at[rows], z, True)
    for step in range(1, NZ // 2 + 1):
        yield
        before = len(waiting)
        behind = lax.rem(z + NZ - step, NZ)
        plus.wait_recv()
        block = full.at[y, behind, rows]
        if step < NZ // 2:
            plus = wire.put(block, block, seq=z_up)
        spread(block, behind, step < NZ // 2)
        if step < NZ // 2:
            ahead = lax.rem(z + step, NZ)
            minus.wait_recv()
            block = full.at[y, ahead, rows]
            if step < NZ // 2 - 1:
                minus = wire.put(block, block, seq=z_down)
            spread(block, ahead, False)
        pass_on(before)
    yield
    pass_on(len(waiting))
    yield
    for copy in rest:
        copy.wait_recv()


def gather_mix(wire, w_out, w_head, out, bufs, y, z, c):
    part, got_c, mine, line, picked = bufs
    rows = w_out.shape[0]
    part[...] = jnp.zeros_like(part)
    part[:, pl.ds(0, rows)] = lax.dot_general(
        w_head[...],
        w_out[...],
        (((1,), (1,)), ((), ())),
        preferred_element_type=jnp.float32,
    )
    puts = [
        wire.put(part, got_c.at[d - 1], chan=lax.rem(c + d, NCHAN)) for d in range(1, NCHAN)
    ]
    yield
    acc = part[...]
    for d in range(1, NCHAN):
        puts[d - 1].wait_recv()
        acc = acc + got_c[d - 1]
    mine[...] = acc
    line[z] = acc
    puts = [
        wire.put(mine, line.at[z], seq=y * NZ + lax.rem(z + d, NZ)) for d in range(1, NZ)
    ]
    yield
    for copy in puts:
        copy.wait_recv()
    kept = pl.ds((c % 2) * (NZ // 2), NZ // 2)
    puts = [
        wire.put(line.at[kept], picked.at[y], seq=lax.rem(y + d, NY) * NZ + z)
        for d in range(1, NY)
    ]
    picked[y] = line[kept]
    yield
    for copy in puts:
        copy.wait_recv()
    for at in range(NZ // 2):
        out[:, pl.ds(at * rows, rows)] = picked[c // 2, at][:, :rows]


def gather_kernel(
    resid,
    w_gate,
    w_x,
    w_out,
    w_head,
    features,
    gate,
    xs,
    out_lines,
    mix,
    full_resid,
    full_weights,
    acc,
    weights,
    *scratch,
):
    *mix_bufs, send, recv, local = scratch
    y, z, c = place()
    half = w_gate.shape[1]
    meet = greet(
        [{"chan": lax.rem(c + d, NCHAN)} for d in range(1, NCHAN)]
        + [{"seq": lax.rem(y + d, NY) * NZ + z} for d in range(1, NY)]
        + [{"seq": y * NZ + lax.rem(z + d, NZ)} for d in range(1, NZ)]
    )
    weights[:, pl.ds(0, half)] = w_gate[...]
    weights[:, pl.ds(half, half)] = w_x[...]
    wire = Wire(send, recv)
    own_weights = pltpu.make_async_copy(weights, full_weights.at[y, z], local.at[0])
    own_resid = pltpu.make_async_copy(resid, full_resid.at[c], local.at[1])
    own_weights.start()
    own_resid.start()
    meet()
    rows, first = weights.shape[0], 32
    one, rest = pl.ds(0, first), pl.ds(first, rows - first)
    lines = gather_z_then_y(wire, weights, full_weights, y, z, rest)
    own_y = exchange_y(wire, weights, full_weights, y, z, one)
    columns = ring_z_columns(wire, full_weights, y, z, one)
    chans = gather_chan(wire, resid, full_resid, c, resid.shape[0])
    mixes = gather_mix(wire, w_out, w_head, mix, mix_bufs, y, z, c)
    in_order(own_y, lines, chans, mixes, own_y)
    own_weights.wait()
    in_order(columns, lines, chans, mixes, lines, columns, mixes, lines, chans)
    out_lines[0, y] = w_out[...]
    out_puts = [
        wire.put(w_out, out_lines.at[0, y], seq=lax.rem(y + d, NY) * NZ + z) for d in (1, 3, 2)
    ]
    in_order(columns, lines, mixes, columns, chans, columns, lines, lines)
    own_resid.wait()
    tile = 256
    width = gate.shape[1]
    x, core = c // 2, c % 2

    def project(blocks, first, last):
        def step(at, carry):
            cols = pl.ds(pl.multiple_of(at * tile, tile), tile)
            total = 0.0 if first else acc[cols, :]
            for block in blocks:
                part = full_weights[block // 2, pl.ds((block % 2) * (NZ // 2), NZ // 2)]
                total = total + lax.dot_general(
                    full_resid[block, :, cols],
                    part.reshape(part.shape[0] * part.shape[1], part.shape[2]),
                    BY_ROWS,
                    preferred_element_type=jnp.float32,
                )
            if last:
                gate[cols, :] = total[:, :width].astype(gate.dtype)
                xs[cols, :] = total[:, width:].astype(xs.dtype)
            else:
                acc[cols, :] = total
            return carry

        lax.fori_loop(0, acc.shape[0] // tile, step, 0)

    mate = c + 1 - 2 * core
    left = lax.rem(x + NX - 1, NX) * 2 + core
    right = lax.rem(x + 1, NX) * 2 + core
    for copy in out_puts:
        copy.wait_recv()
    out_puts = [
        wire.put(out_lines.at[0], out_lines.at[1], seq=y * NZ + lax.rem(z + 1, NZ)),
        wire.put(out_lines.at[0], out_lines.at[2], seq=y * NZ + lax.rem(z + NZ - 1, NZ)),
    ]
    project([c, left, right], True, False)
    in_order(chans, chans)
    out = pltpu.make_async_copy(full_resid, features, local.at[1])
    out.start()
    across = lax.rem(x + 2, NX) * 2 + core
    flip = 1 - 2 * core
    project([mate, left + flip, right + flip, across, across + flip], False, True)
    for copy in out_puts:
        copy.wait_recv()
    out.wait()
    wire.finish()


def gather_all(resid, w_gate, w_x, w_out, w_head):
    anywhere = pl.BlockSpec(memory_space=pl.ANY)
    vmem = pl.BlockSpec(memory_space=pltpu.VMEM)
    f32 = jnp.float32
    copies = 96
    block = (VOCAB, 128)
    rows, half = w_gate.shape
    tokens = resid.shape[1]
    return pl.pallas_call(
        gather_kernel,
        name="gather_all",
        out_shape=(
            jax.ShapeDtypeStruct((NCHAN, *resid.shape), resid.dtype),
            jax.ShapeDtypeStruct((tokens, half), resid.dtype),
            jax.ShapeDtypeStruct((tokens, half), resid.dtype),
            jax.ShapeDtypeStruct((3, NY, *w_out.shape), w_out.dtype),
            jax.ShapeDtypeStruct((VOCAB, resid.shape[0]), f32),
        ),
        in_specs=[vmem] * 5,
        out_specs=(anywhere, vmem, vmem, vmem, vmem),
        scratch_shapes=[
            pltpu.VMEM((NCHAN, *resid.shape), resid.dtype),
            pltpu.VMEM((NY, NZ, rows, 2 * half), w_gate.dtype),
            pltpu.VMEM((tokens, 2 * half), f32),
            pltpu.VMEM((rows, 2 * half), w_gate.dtype),
            pltpu.VMEM(block, f32),
            pltpu.VMEM((NCHAN - 1, *block), f32),
            pltpu.VMEM(block, f32),
            pltpu.VMEM((NZ, *block), f32),
            pltpu.VMEM((NY, NZ // 2, *block), f32),
            pltpu.SemaphoreType.DMA((copies,)),
            pltpu.SemaphoreType.DMA((copies,)),
            pltpu.SemaphoreType.DMA((2,)),
        ],
        compiler_params=pltpu.CompilerParams(
            collective_id=0, has_side_effects=True, vmem_limit_bytes=VMEM_BYTES
        ),
        cost_estimate=pl.CostEstimate(flops=10**10, bytes_accessed=10**8, transcendentals=0),
    )(resid, w_gate, w_x, w_out, w_head)


EXACT = lax.Precision.HIGHEST
LANES = 128
EDGE = 16
SUMS = 40
FACTS = 24


def ring_on(wire, lines, full, y, z):
    up, down = y * NZ + lax.rem(z + 1, NZ), y * NZ + lax.rem(z + NZ - 1, NZ)
    plus = wire.put(lines.at[1], full.at[:, lax.rem(z + NZ - 1, NZ)], seq=up)
    minus = wire.put(lines.at[2], full.at[:, lax.rem(z + 1, NZ)], seq=down)
    for step in range(2, NZ // 2):
        yield
        last = step == NZ // 2 - 1
        behind, ahead = lax.rem(z + NZ - step, NZ), lax.rem(z + step, NZ)
        plus.wait_recv()
        moved = full.at[pl.ds(0, NY // 2) if last else slice(None), behind]
        plus = wire.put(moved, moved, seq=up)
        minus.wait_recv()
        moved = full.at[pl.ds(NY // 2, NY // 2) if last else slice(None), ahead]
        minus = wire.put(moved, moved, seq=down)
    yield
    plus.wait_recv()
    minus.wait_recv()


def middle_kernel(
    gate,
    xs,
    resid,
    head_t,
    mix_t,
    conv_weight,
    conv_bias,
    norm_gain,
    skip_d,
    targets,
    out_lines,
    dgate,
    dx,
    small,
    gained,
    facts,
    full_w_out,
    padded,
    prods,
    to_gate,
    to_conv,
    sums,
    parts,
    mine,
    before,
    after,
    acc_rows,
    acc_heads,
    send,
    recv,
    w_send,
    w_recv,
    local,
):
    f32, bf16 = jnp.float32, jnp.bfloat16
    tokens = gate.shape[0]
    y, z, c = place()
    s = y * NZ + z
    last_seq = NY * NZ - 1
    later, sooner = lax.rem(s + 1, NY * NZ), lax.rem(s + last_seq, NY * NZ)
    meet = greet(
        [{"chan": lax.rem(c + d, NCHAN)} for d in range(1, NCHAN)]
        + [{"seq": later}, {"seq": sooner}]
        + [{"seq": y * NZ + lax.rem(z + d, NZ)} for d in (1, NZ - 1)]
    )
    wire = Wire(w_send, w_recv)
    near = (z, lax.rem(z + NZ - 1, NZ), lax.rem(z + 1, NZ))
    own_lines = [
        pltpu.make_async_copy(out_lines.at[at], full_w_out.at[:, near[at]], local.at[at])
        for at in range(3)
    ]
    for copy in own_lines:
        copy.start()
    columns = ring_on(wire, out_lines, full_w_out, y, z)

    def copy_of(source, target, at, where):
        return pltpu.make_async_remote_copy(
            src_ref=source,
            dst_ref=target,
            send_sem=send.at[at],
            recv_sem=recv.at[at],
            device_id=where,
            device_id_type=MESH,
        )

    edge = copy_of(xs.at[pl.ds(tokens - EDGE, EDGE)], before, 2 * NCHAN, {"seq": later})
    taps = [conv_weight[k : k + 1, :] for k in range(KERNEL)]
    bias, gain = conv_bias[...], norm_gain[...]
    head = lax.broadcasted_iota(jnp.int32, bias.shape, 1) // HEADDIM
    skip = jnp.zeros(bias.shape, f32)
    for at in range(skip_d.shape[0]):
        skip = jnp.where(head == at, skip_d[at], skip)
    mix = mix_t[...]
    padded[pl.ds(EDGE, tokens), :] = xs[...].astype(f32)
    meet()
    edge.start()
    in_order(columns)

    def window(tile):
        start = pl.multiple_of(tile * LANES, LANES)
        return pl.ds(start, LANES), padded[pl.ds(start, LANES + EDGE), :]

    def shifted(win, k):
        first = EDGE - (KERNEL - 1) + k
        return win[first : first + LANES]

    def share(step):
        peer = lax.rem(c + 1 + step, NCHAN)
        return copy_of(sums.at[peer], parts.at[step], step, {"chan": peer})

    def forward(tile):
        rows, win = window(tile)
        conv = bias + taps[0] * shifted(win, 0)
        for k in range(1, KERNEL):
            conv = conv + taps[k] * shifted(win, k)
        sig_conv = jax.nn.sigmoid(conv)
        active = conv * sig_conv
        gate_pre = gate[rows, :].astype(f32)
        sig_gate = jax.nn.sigmoid(gate_pre)
        silu_gate = gate_pre * sig_gate
        prod = active * silu_gate
        prods[rows, :] = prod
        to_gate[rows, :] = skip * active * slope(gate_pre, sig_gate)
        to_conv[rows, :] = skip * silu_gate * slope(conv, sig_conv)
        gated = prod * skip
        with_gain = gated * gain
        gained[:, rows] = with_gain.T.astype(bf16)
        by_lanes = (((1,), (1,)), ((), ()))
        sums[tile, pl.ds(0, VOCAB)] = lax.dot_general(
            head_t[...],
            resid[:, rows],
            (((1,), (0,)), ((), ())),
            preferred_element_type=f32,
        )
        sums[tile, pl.ds(VOCAB, VOCAB)] = lax.dot_general(
            mix, with_gain, by_lanes, precision=EXACT, preferred_element_type=f32
        )
        sums[tile, pl.ds(2 * VOCAB, 8)] = lax.dot_general(
            jnp.ones((8, gated.shape[1]), f32),
            gated * gated,
            by_lanes,
            precision=EXACT,
            preferred_element_type=f32,
        )

    edge.wait_recv()
    padded[pl.ds(0, EDGE), :] = before[...].astype(f32) * (s > 0).astype(f32)

    def forward_step(step, carry):
        forward(lax.rem(c + 1 + step, NCHAN))
        share(step).start()
        return carry

    lax.fori_loop(0, NCHAN - 1, forward_step, 0)
    forward(c)
    in_order(columns)
    total = sums[c]
    for step in range(NCHAN - 1):
        share(step).wait_recv()
        total = total + parts[step]
    inverse = lax.rsqrt(total[2 * VOCAB : 2 * VOCAB + 1] / INNER + 1e-05)
    gained_head = total[VOCAB : 2 * VOCAB]
    raised = jnp.exp(total[:VOCAB] + inverse * gained_head)
    probs = raised / jnp.sum(raised, axis=0, keepdims=True)
    words = lax.broadcasted_iota(jnp.int32, (VOCAB, LANES), 0)
    onehot = (words == targets[c]).astype(f32)
    weight = 4.0 / float(tokens * NY * NZ) ** 0.5
    dlogit = (probs - onehot) * weight
    dot_gn = jnp.sum(dlogit * gained_head, axis=0, keepdims=True)
    mine[pl.ds(0, VOCAB), :] = dlogit
    mine[pl.ds(VOCAB, 8), :] = jnp.concatenate(
        [inverse, inverse * inverse * inverse * dot_gn / INNER, jnp.zeros((6, LANES), f32)],
        axis=0,
    )
    facts[c] = mine[...]

    def tell(d):
        return copy_of(
            mine, facts.at[c], NCHAN - 1 + d, {"chan": lax.rem(c + d, NCHAN)}
        )

    for d in range(1, NCHAN):
        tell(d).start()
    acc_rows[...] = jnp.zeros_like(acc_rows)
    acc_heads[...] = jnp.zeros_like(acc_heads)
    for d in range(1, NCHAN):
        tell(d).wait_recv()
    in_order(columns)
    second = (
        lax.broadcasted_iota(jnp.int32, (8, mix.shape[1]), 0) == 1
    ).astype(f32)

    def fold(value):
        return jnp.sum(value.reshape(LANES // 8, 8, value.shape[1]), axis=0)

    def backward(tile):
        rows, win = window(tile)
        fact = facts[tile]
        dlogit = fact[:VOCAB]
        scaled = dlogit * fact[VOCAB : VOCAB + 1]
        by_rows = (((0,), (0,)), ((), ()))
        dnormed = lax.dot_general(
            scaled, mix, by_rows, precision=EXACT, preferred_element_type=f32
        )
        pull = lax.dot_general(
            fact[VOCAB : VOCAB + 8], second, by_rows, precision=EXACT, preferred_element_type=f32
        )
        prod = prods[rows, :]
        dgated = gain * dnormed - skip * prod * pull
        dgate[rows, :] = (dgated * to_gate[rows, :]).astype(bf16)
        dconv = dgated * to_conv[rows, :]
        to_conv[rows, :] = dconv
        for k in range(KERNEL):
            acc_rows[k] += fold(dconv * shifted(win, k))
        acc_rows[KERNEL] += fold(dconv)
        acc_rows[KERNEL + 1] += fold(dgated * prod)
        acc_heads[0] += jnp.dot(scaled, prod, precision=EXACT, preferred_element_type=f32)
        acc_heads[1] += lax.dot_general(
            dlogit,
            resid[:, rows].astype(f32),
            (((1,), (1,)), ((), ())),
            precision=EXACT,
            preferred_element_type=f32,
        )

    backward(0)
    first_rows = copy_of(to_conv.at[pl.ds(0, 8)], after, 2 * NCHAN + 1, {"seq": sooner})
    first_rows.start()

    def backward_step(tile, carry):
        backward(tile)
        return carry

    lax.fori_loop(1, tokens // LANES, backward_step, 0)
    by_channel = acc_heads[0]
    small[pl.ds(0, VOCAB), :] = by_channel * skip * gain
    small[pl.ds(VOCAB, VOCAB), :] = acc_heads[1]
    lines = [jnp.sum(acc_rows[k], axis=0, keepdims=True) for k in range(KERNEL + 2)]
    lines.insert(KERNEL + 1, skip * jnp.sum(mix * by_channel, axis=0, keepdims=True))
    lines.append(jnp.zeros_like(skip))
    small[pl.ds(2 * VOCAB, 8), :] = jnp.concatenate(lines, axis=0)
    first_rows.wait_recv()
    to_conv[pl.ds(tokens, 8), :] = after[...] * (s < last_seq).astype(f32)

    def spread_step(tile, carry):
        start = pl.multiple_of(tile * LANES, LANES)
        win = to_conv[pl.ds(start, LANES + 8), :]
        acc = taps[KERNEL - 1] * win[0:LANES]
        for k in range(KERNEL - 1):
            acc = acc + taps[k] * win[KERNEL - 1 - k : KERNEL - 1 - k + LANES]
        dx[pl.ds(start, LANES), :] = acc.astype(bf16)
        return carry

    lax.fori_loop(0, tokens // LANES, spread_step, 0)
    in_order(columns)
    wire.finish()
    for copy in own_lines:
        copy.wait()
    edge.wait_send()
    first_rows.wait_send()
    for d in range(1, NCHAN):
        share(d - 1).wait_send()
        tell(d).wait_send()


def middle(gate, xs, *others):
    f32, bf16 = jnp.float32, jnp.bfloat16
    vmem = pl.BlockSpec(memory_space=pltpu.VMEM)
    anywhere = pl.BlockSpec(memory_space=pl.ANY)
    tokens, width = gate.shape
    copies = 2 * NCHAN + 2
    return pl.pallas_call(
        middle_kernel,
        name="middle",
        out_shape=(
            jax.ShapeDtypeStruct((tokens, width), bf16),
            jax.ShapeDtypeStruct((tokens, width), bf16),
            jax.ShapeDtypeStruct((SUMS, width), f32),
            jax.ShapeDtypeStruct((width, tokens), bf16),
            jax.ShapeDtypeStruct((NCHAN, FACTS, LANES), f32),
            jax.ShapeDtypeStruct((NY, NZ, *others[-1].shape[2:]), bf16),
        ),
        in_specs=[vmem] * 8 + [pl.BlockSpec(memory_space=pltpu.SMEM), vmem, anywhere],
        out_specs=(vmem,) * 5 + (anywhere,),
        scratch_shapes=[
            pltpu.VMEM((tokens + EDGE, width), f32),
            pltpu.VMEM((tokens, width), f32),
            pltpu.VMEM((tokens, width), f32),
            pltpu.VMEM((tokens + 8, width), f32),
            pltpu.VMEM((NCHAN, SUMS, LANES), f32),
            pltpu.VMEM((NCHAN - 1, SUMS, LANES), f32),
            pltpu.VMEM((FACTS, LANES), f32),
            pltpu.VMEM((EDGE, width), bf16),
            pltpu.VMEM((8, width), f32),
            pltpu.VMEM((KERNEL + 2, 8, width), f32),
            pltpu.VMEM((2, VOCAB, width), f32),
            pltpu.SemaphoreType.DMA((copies,)),
            pltpu.SemaphoreType.DMA((copies,)),
            pltpu.SemaphoreType.DMA((NZ,)),
            pltpu.SemaphoreType.DMA((NZ,)),
            pltpu.SemaphoreType.DMA((3,)),
        ],
        compiler_params=pltpu.CompilerParams(
            collective_id=1, has_side_effects=True, vmem_limit_bytes=VMEM_BYTES
        ),
        cost_estimate=pl.CostEstimate(flops=10**10, bytes_accessed=10**7, transcendentals=0),
    )(gate, xs, *others)


def scatter_seq(wire, grads, ready, bufs, outs, y, z, start, count):
    f32, bf16 = jnp.float32, jnp.bfloat16
    from_below, from_above, via_up, via_down, got_below, got_above, lines, got_z = bufs
    rows = pl.ds(start, count)
    lo, hi = pl.ds(0, NZ // 2), pl.ds(NZ // 2, NZ // 2)
    above, below, across = lax.rem(y + 1, NY), lax.rem(y + 3, NY), lax.rem(y + 2, NY)
    up, down = above * NZ + z, below * NZ + z
    ready(2 * across)
    half_up = wire.put(grads.at[across, lo, rows], from_below.at[:, rows], seq=up)
    ready(2 * across + 1)
    half_down = wire.put(grads.at[across, hi, rows], from_above.at[:, rows], seq=down)
    ready(2 * above + 1)
    moves = [wire.put(grads.at[above, hi, rows], got_below.at[hi, rows], seq=up)]
    ready(2 * below)
    moves.append(wire.put(grads.at[below, lo, rows], got_above.at[lo, rows], seq=down))
    ready(2 * above)
    ready(2 * below + 1)
    yield
    half_up.wait_recv()
    via_up[:, rows] = (
        grads[above, lo, rows].astype(f32) + from_below[:, rows].astype(f32)
    ).astype(bf16)
    moves.append(wire.put(via_up.at[:, rows], got_below.at[lo, rows], seq=up))
    half_down.wait_recv()
    via_down[:, rows] = (
        grads[below, hi, rows].astype(f32) + from_above[:, rows].astype(f32)
    ).astype(bf16)
    moves.append(wire.put(via_down.at[:, rows], got_above.at[hi, rows], seq=down))
    ready(2 * y)
    ready(2 * y + 1)
    yield
    for copy in moves[:2]:
        copy.wait_recv()
    yield
    for copy in moves[2:]:
        copy.wait_recv()
    lines[:, rows] = (
        grads[y, :, rows].astype(f32)
        + got_below[:, rows].astype(f32)
        + got_above[:, rows].astype(f32)
    ).astype(bf16)
    puts = []
    for d in (4, 3, 5, 2, 6, 1, 7):
        peer = lax.rem(z + d, NZ)
        puts.append(wire.put(lines.at[peer, rows], got_z.at[d - 1, rows], seq=y * NZ + peer))
    yield
    acc = (
        grads[y, z, rows].astype(f32)
        + got_below[z, rows].astype(f32)
        + got_above[z, rows].astype(f32)
    )
    for copy in puts:
        copy.wait_recv()
    for d in range(1, NZ):
        acc = acc + got_z[d - 1, rows].astype(f32)
    half = acc.shape[1] // 2
    outs[0][rows] = acc[:, :half]
    outs[1][rows] = acc[:, half:]


def sum_small(wire, small, got_y, part, got_z, total, heads, y, z, c):
    puts = [
        wire.put(small, got_y.at[y], seq=lax.rem(y + d, NY) * NZ + z) for d in range(1, NY)
    ]
    got_y[y] = small[...]
    yield
    for copy in puts:
        copy.wait_recv()
    acc = got_y[0]
    for at in range(1, NY):
        acc = acc + got_y[at]
    part[...] = acc
    puts = [
        wire.put(part, got_z.at[z], seq=y * NZ + lax.rem(z + d, NZ)) for d in range(1, NZ)
    ]
    got_z[z] = acc
    yield
    for copy in puts:
        copy.wait_recv()
    acc = got_z[0]
    for at in range(1, NZ):
        acc = acc + got_z[at]
    total[...] = acc
    first = pl.ds(0, VOCAB)
    puts = [
        wire.put(total.at[first], heads.at[c], chan=lax.rem(c + d, NCHAN))
        for d in range(1, NCHAN)
    ]
    heads[c] = total[first]
    yield
    for copy in puts:
        copy.wait_recv()


def grads_kernel(
    features,
    dgate,
    dx,
    small,
    gained,
    w_out,
    resid,
    facts,
    head_t,
    grad_gate,
    grad_x,
    total,
    grad_out,
    grad_head,
    new_resid,
    *scratch,
):
    f32, bf16 = jnp.float32, jnp.bfloat16
    feats, both, grads, full_gained, out_cols, heads, *rest = scratch
    *bufs, small_y, small_part, small_z, send, recv, local = rest
    y, z, c = place()
    width = dgate.shape[1]
    meet = greet(
        [{"chan": lax.rem(c + d, NCHAN)} for d in range(1, NCHAN)]
        + [{"seq": lax.rem(y + d, NY) * NZ + z} for d in range(1, NY)]
        + [{"seq": y * NZ + lax.rem(z + d, NZ)} for d in range(1, NZ)]
    )
    order = [
        2 * lax.rem(y + 2, NY),
        2 * lax.rem(y + 2, NY) + 1,
        2 * lax.rem(y + 1, NY) + 1,
        2 * lax.rem(y + 3, NY),
        2 * lax.rem(y + 1, NY),
        2 * lax.rem(y + 3, NY) + 1,
        2 * y,
        2 * y + 1,
    ]
    loads = [
        pltpu.make_async_copy(features.at[at], feats.at[step], local.at[step])
        for step, at in enumerate(order)
    ]
    for load in loads:
        load.start()
    own = pltpu.make_async_copy(gained, full_gained.at[c], local.at[NCHAN])
    own.start()
    weights = pltpu.make_async_copy(w_out, out_cols, local.at[NCHAN + 1])
    weights.start()
    both[:, pl.ds(0, width)] = dgate[...]
    both[:, pl.ds(width, width)] = dx[...]
    wire = Wire(send, recv)
    steps = []

    def compute(step):
        loads[step].wait()
        product = jnp.dot(feats[step], both[...], preferred_element_type=f32)
        lines = product.reshape(NZ // 2, product.shape[0] // (NZ // 2), product.shape[1])
        block = order[step]
        first = lax.rem(block, 2) * (NZ // 2)
        grads[block // 2, pl.ds(first, NZ // 2)] = lines.astype(bf16)

    def ready(block):
        steps.append(block)
        if len(steps) > 2:
            compute(len(steps) - 1)

    compute(0)
    compute(1)
    meet()
    rows = grad_gate.shape[0]
    outs = (grad_gate, grad_x)
    smalls = sum_small(wire, small, small_y, small_part, small_z, total, heads, y, z, c)
    one = scatter_seq(wire, grads, ready, bufs, outs, y, z, 0, 32)
    two = scatter_seq(wire, grads, lambda block: None, bufs, outs, y, z, 32, 32)
    three = scatter_seq(wire, grads, lambda block: None, bufs, outs, y, z, 64, rows - 64)
    chans = gather_chan(wire, gained, full_gained, c, gained.shape[0])
    in_order(smalls, chans, one, chans, smalls, one, chans, one, two, one, chans, two, smalls)
    in_order(two, three, two, three, chans, three, three, smalls, chans)
    own.wait()
    weights.wait()

    def project_back(step, carry):
        cols = pl.ds(pl.multiple_of(step * 256, 256), 256)
        acc = 0.0
        for at in range(NCHAN):
            acc = acc + lax.dot_general(
                out_cols[at], full_gained[at, :, cols], BY_ROWS, preferred_element_type=f32
            )
        for at in range(2):
            tile = 2 * step + at
            lanes = pl.ds(pl.multiple_of(tile * LANES, LANES), LANES)
            scale = facts[tile, VOCAB : VOCAB + 1]
            summed = resid[:, lanes].astype(f32) + scale * acc[:, at * LANES : (at + 1) * LANES]
            new_resid[:, lanes] = summed.astype(bf16)
        return carry

    lax.fori_loop(0, new_resid.shape[1] // 256, project_back, 0)
    acc = 0.0
    for at in range(NCHAN):
        head = heads[at]
        high = head.astype(bf16)
        low = (head - high.astype(f32)).astype(bf16)
        acc = acc + jnp.dot(
            jnp.concatenate([high, low], axis=0),
            out_cols[at],
            preferred_element_type=f32,
        )
    grad_head[...] = total[pl.ds(VOCAB, VOCAB), :] + acc[:VOCAB] + acc[VOCAB:]
    s = y * NZ + z
    per_chan = width // rows
    mine = heads[s // per_chan]
    here = jnp.zeros((VOCAB, rows), f32)
    for at in range(per_chan):
        chosen = (lax.rem(s, per_chan) == at).astype(f32)
        here = here + chosen * mine[:, at * rows : (at + 1) * rows]
    grad_out[...] = lax.dot_general(
        here, head_t[...].astype(f32), BY_ROWS, precision=EXACT, preferred_element_type=f32
    )
    in_order(one, two, three)
    wire.finish()


def finish_grads(features, dgate, dx, small, gained, w_out, resid, facts, head_t):
    f32, bf16 = jnp.float32, jnp.bfloat16
    anywhere = pl.BlockSpec(memory_space=pl.ANY)
    vmem = pl.BlockSpec(memory_space=pltpu.VMEM)
    tokens, width = dgate.shape
    rows = INNER // (NY * NZ)
    copies = 80
    cols = 2 * width
    half = (NZ // 2, rows, cols)
    line = (NZ, rows, cols)
    block = jax.ShapeDtypeStruct((rows, width), f32)
    return pl.pallas_call(
        grads_kernel,
        name="finish_grads",
        out_shape=(
            block,
            block,
            jax.ShapeDtypeStruct(small.shape, f32),
            block,
            jax.ShapeDtypeStruct((VOCAB, width), f32),
            jax.ShapeDtypeStruct(resid.shape, bf16),
        ),
        in_specs=[anywhere, vmem, vmem, vmem, anywhere, anywhere, vmem, vmem, vmem],
        out_specs=(vmem,) * 6,
        scratch_shapes=[
            pltpu.VMEM(features.shape, bf16),
            pltpu.VMEM((tokens, cols), bf16),
            pltpu.VMEM((NY, NZ, rows, cols), bf16),
            pltpu.VMEM((NCHAN, *gained.shape), bf16),
            pltpu.VMEM(w_out.shape, bf16),
            pltpu.VMEM((NCHAN, VOCAB, width), f32),
        ]
        + [pltpu.VMEM(half, bf16)] * 4
        + [pltpu.VMEM(line, bf16)] * 3
        + [
            pltpu.VMEM((NZ - 1, rows, cols), bf16),
            pltpu.VMEM((NY, *small.shape), f32),
            pltpu.VMEM(small.shape, f32),
            pltpu.VMEM((NZ, *small.shape), f32),
            pltpu.SemaphoreType.DMA((copies,)),
            pltpu.SemaphoreType.DMA((copies,)),
            pltpu.SemaphoreType.DMA((NCHAN + 2,)),
        ],
        compiler_params=pltpu.CompilerParams(
            collective_id=2, has_side_effects=True, vmem_limit_bytes=VMEM_BYTES
        ),
        cost_estimate=pl.CostEstimate(flops=10**10, bytes_accessed=10**8, transcendentals=0),
    )(features, dgate, dx, small, gained, w_out, resid, facts, head_t)


BY_ROWS = (((0,), (0,)), ((), ()))


def hand_out_kernel(total, *refs):
    count = len(refs) // 2
    for at in range(count):
        refs[at + count][...] = refs[at][...]
    refs[-1][...] = total[pl.ds(2 * VOCAB, KERNEL), :]


def hand_out(total, *arrays):
    vmem = pl.BlockSpec(memory_space=pltpu.VMEM)
    shapes = [jax.ShapeDtypeStruct(array.shape, array.dtype) for array in arrays]
    shapes.append(jax.ShapeDtypeStruct((KERNEL, total.shape[1]), total.dtype))
    return pl.pallas_call(
        hand_out_kernel,
        name="hand_out",
        out_shape=tuple(shapes),
        in_specs=[vmem] * (len(arrays) + 1),
        out_specs=(vmem,) * len(shapes),
        compiler_params=pltpu.CompilerParams(vmem_limit_bytes=VMEM_BYTES),
    )(total, *arrays)


def slope(value, sig):
    return sig * (1.0 + value * (1.0 - sig))


def per_device(
    targets, resid, w_gate_in, w_x_in, conv_weight, conv_bias, skip_d, norm_gain, w_out, w_head
):
    f32 = jnp.float32
    local_inner = w_gate_in.shape[1]
    head_t, resid_t = w_head.T, resid.T
    features, gate_pre, x_pre, out_lines, mix_t = gather_all(
        resid_t, w_gate_in, w_x_in, w_out, head_t
    )
    dgate, dx_pre, small, gained, facts, out_cols = middle(
        gate_pre,
        x_pre,
        resid_t,
        head_t,
        mix_t,
        conv_weight,
        conv_bias[None],
        norm_gain[None],
        skip_d,
        targets.reshape(NCHAN, 1, LANES),
        out_lines,
    )
    grad_gate_in, grad_x_in, total, *others = finish_grads(
        features,
        dgate,
        dx_pre,
        small,
        gained,
        out_cols.reshape(NCHAN, local_inner, local_inner),
        resid_t,
        facts,
        head_t,
    )
    grad_gate_in, grad_x_in, grad_out, grad_head_t, new_resid_t, grad_conv_weight = hand_out(
        total, grad_gate_in, grad_x_in, *others
    )
    at = 2 * VOCAB
    grad_conv_bias = total[at + KERNEL]
    grad_gain = total[at + KERNEL + 1]
    grad_skip = total[at + KERNEL + 2].reshape(-1, HEADDIM).sum(axis=1)
    return (
        new_resid_t.T,
        grad_gate_in,
        grad_x_in,
        grad_out,
        grad_head_t.T,
        grad_conv_weight,
        grad_conv_bias,
        grad_skip,
        grad_gain,
    )


def solution(mesh):
    return jax.shard_map(
        per_device,
        mesh=mesh,
        in_specs=(
            P("seq"),
            P("seq", "chan"),
            P("seq", "chan"),
            P("seq", "chan"),
            P(None, "chan"),
            P("chan"),
            P("chan"),
            P("chan"),
            P("seq", "chan"),
            P("chan", None),
        ),
        out_specs=(
            P("seq", "chan"),
            P("seq", "chan"),
            P("seq", "chan"),
            P("seq", "chan"),
            P("chan", None),
            P(None, "chan"),
            P("chan"),
            P("chan"),
            P("chan"),
        ),
        check_vma=False,
    )
```

```python
import jax
import jax.numpy as jnp
from jax import lax
from jax.experimental import pallas as pl
from jax.experimental.pallas import tpu as pltpu
from jax.sharding import PartitionSpec as P

HEADDIM = 64
KERNEL = 4
VOCAB = 16
INNER = 2560
NX, NY, NZ = 4, 4, 8
NCHAN = 2 * NX
MESH = pl.DeviceIdType.MESH
VMEM_BYTES = 56 * 1024 * 1024


class Wire:
    def __init__(self, send, recv):
        self.send, self.recv, self.copies = send, recv, []

    def put(self, source, target, **where):
        place = len(self.copies)
        copy = pltpu.make_async_remote_copy(
            src_ref=source,
            dst_ref=target,
            send_sem=self.send.at[place],
            recv_sem=self.recv.at[place],
            device_id=where,
            device_id_type=MESH,
        )
        copy.start()
        self.copies.append(copy)
        return copy

    def finish(self):
        for copy in self.copies:
            copy.wait_send()


def greet(peers):
    barrier = pltpu.get_barrier_semaphore()
    for peer in peers:
        pl.semaphore_signal(barrier, inc=1, device_id=peer, device_id_type=MESH)
    return lambda: pl.semaphore_wait(barrier, len(peers))


def in_order(*streams):
    for stream in streams:
        next(stream, None)


def place():
    s, c = lax.axis_index("seq"), lax.axis_index("chan")
    return s // NZ, s % NZ, c


def gather_chan(wire, shard, full, c, rows):
    x, core = c // 2, c % 2
    mate = c + 1 - 2 * core
    right = lax.rem(x + 1, NX) * 2 + core
    left = lax.rem(x + NX - 1, NX) * 2 + core
    across = lax.rem(x + 2, NX) * 2 + core
    lo, hi = pl.ds(0, rows // 2), pl.ds(rows // 2, rows // 2)
    to_right_lo = wire.put(shard.at[lo], full.at[c, lo], chan=right)
    to_left_hi = wire.put(shard.at[hi], full.at[c, hi], chan=left)
    yield
    to_right_hi = wire.put(shard.at[hi], full.at[c, hi], chan=right)
    to_left_lo = wire.put(shard.at[lo], full.at[c, lo], chan=left)
    to_mate = [wire.put(shard, full.at[c], chan=mate)]
    yield
    to_right_lo.wait_recv()
    on_right = wire.put(full.at[left, lo], full.at[left, lo], chan=right)
    to_left_hi.wait_recv()
    on_left = wire.put(full.at[right, hi], full.at[right, hi], chan=left)
    yield
    to_right_hi.wait_recv()
    to_mate.append(wire.put(full.at[left], full.at[left], chan=mate))
    to_left_lo.wait_recv()
    to_mate.append(wire.put(full.at[right], full.at[right], chan=mate))
    yield
    on_right.wait_recv()
    to_mate.append(wire.put(full.at[across, lo], full.at[across, lo], chan=mate))
    on_left.wait_recv()
    to_mate.append(wire.put(full.at[across, hi], full.at[across, hi], chan=mate))
    yield
    for copy in to_mate:
        copy.wait_recv()


def ring_z(wire, first, block, halves, y, z):
    up, down = y * NZ + lax.rem(z + 1, NZ), y * NZ + lax.rem(z + NZ - 1, NZ)
    plus = wire.put(first, block(z), seq=up)
    minus = wire.put(first, block(z), seq=down)
    for step in range(1, NZ // 2):
        last = step == NZ // 2 - 1
        yield
        behind, ahead = lax.rem(z + NZ - step, NZ), lax.rem(z + step, NZ)
        plus.wait_recv()
        moved = halves(behind)[0] if last else block(behind)
        plus = wire.put(moved, moved, seq=up)
        minus.wait_recv()
        moved = halves(ahead)[1] if last else block(ahead)
        minus = wire.put(moved, moved, seq=down)
    yield
    plus.wait_recv()
    minus.wait_recv()


def exchange_y(wire, shard, full, y, z, rows):
    puts = [
        wire.put(shard.at[rows], full.at[y, z, rows], seq=lax.rem(y + d, NY) * NZ + z)
        for d in (1, 3, 2)
    ]
    yield
    for copy in puts:
        copy.wait_recv()


def ring_z_columns(wire, full, y, z, rows):
    yield from ring_z(
        wire,
        full.at[:, z, rows],
        lambda at: full.at[:, at, rows],
        lambda at: (full.at[pl.ds(0, 2), at, rows], full.at[pl.ds(2, 2), at, rows]),
        y,
        z,
    )


def gather_z_then_y(wire, shard, full, y, z, rows):
    above, below = lax.rem(y + 1, NY), lax.rem(y + NY - 1, NY)
    y_up, y_down = above * NZ + z, below * NZ + z
    z_up, z_down = y * NZ + lax.rem(z + 1, NZ), y * NZ + lax.rem(z + NZ - 1, NZ)
    waiting, rest = [], []

    def spread(source, at, upward):
        block = full.at[y, at, rows]
        up, down = wire.put(source, block, seq=y_up), wire.put(source, block, seq=y_down)
        waiting.append((up, down, at, upward))

    def pass_on(count):
        for up, down, at, upward in waiting[:count]:
            if upward:
                up.wait_recv()
                block = full.at[below, at, rows]
                rest.extend([down, wire.put(block, block, seq=y_up)])
            else:
                down.wait_recv()
                block = full.at[above, at, rows]
                rest.extend([up, wire.put(block, block, seq=y_down)])
        del waiting[:count]

    own = full.at[y, z, rows]
    plus, minus = wire.put(shard.at[rows], own, seq=z_up), wire.put(shard.at[rows], own, seq=z_down)
    spread(shard.at[rows], z, True)
    for step in range(1, NZ // 2 + 1):
        yield
        before = len(waiting)
        behind = lax.rem(z + NZ - step, NZ)
        plus.wait_recv()
        block = full.at[y, behind, rows]
        if step < NZ // 2:
            plus = wire.put(block, block, seq=z_up)
        spread(block, behind, step < NZ // 2)
        if step < NZ // 2:
            ahead = lax.rem(z + step, NZ)
            minus.wait_recv()
            block = full.at[y, ahead, rows]
            if step < NZ // 2 - 1:
                minus = wire.put(block, block, seq=z_down)
            spread(block, ahead, False)
        pass_on(before)
    yield
    pass_on(len(waiting))
    yield
    for copy in rest:
        copy.wait_recv()


def gather_mix(wire, w_out, w_head, out, bufs, y, z, c):
    part, got_c, mine, line, picked = bufs
    rows = w_out.shape[0]
    part[...] = jnp.zeros_like(part)
    part[:, pl.ds(0, rows)] = lax.dot_general(
        w_head[...],
        w_out[...],
        (((1,), (1,)), ((), ())),
        preferred_element_type=jnp.float32,
    )
    puts = [
        wire.put(part, got_c.at[d - 1], chan=lax.rem(c + d, NCHAN)) for d in range(1, NCHAN)
    ]
    yield
    acc = part[...]
    for d in range(1, NCHAN):
        puts[d - 1].wait_recv()
        acc = acc + got_c[d - 1]
    mine[...] = acc
    line[z] = acc
    puts = [
        wire.put(mine, line.at[z], seq=y * NZ + lax.rem(z + d, NZ)) for d in range(1, NZ)
    ]
    yield
    for copy in puts:
        copy.wait_recv()
    kept = pl.ds((c % 2) * (NZ // 2), NZ // 2)
    puts = [
        wire.put(line.at[kept], picked.at[y], seq=lax.rem(y + d, NY) * NZ + z)
        for d in range(1, NY)
    ]
    picked[y] = line[kept]
    yield
    for copy in puts:
        copy.wait_recv()
    for at in range(NZ // 2):
        out[:, pl.ds(at * rows, rows)] = picked[c // 2, at][:, :rows]


def gather_kernel(
    resid,
    w_gate,
    w_x,
    w_out,
    w_head,
    features,
    gate,
    xs,
    out_lines,
    mix,
    full_resid,
    full_weights,
    acc,
    weights,
    *scratch,
):
    *mix_bufs, send, recv, local = scratch
    y, z, c = place()
    half = w_gate.shape[1]
    meet = greet(
        [{"chan": lax.rem(c + d, NCHAN)} for d in range(1, NCHAN)]
        + [{"seq": lax.rem(y + d, NY) * NZ + z} for d in range(1, NY)]
        + [{"seq": y * NZ + lax.rem(z + d, NZ)} for d in range(1, NZ)]
    )
    weights[:, pl.ds(0, half)] = w_gate[...]
    weights[:, pl.ds(half, half)] = w_x[...]
    wire = Wire(send, recv)
    own_weights = pltpu.make_async_copy(weights, full_weights.at[y, z], local.at[0])
    own_resid = pltpu.make_async_copy(resid, full_resid.at[c], local.at[1])
    own_weights.start()
    own_resid.start()
    meet()
    rows, first = weights.shape[0], 32
    one, rest = pl.ds(0, first), pl.ds(first, rows - first)
    lines = gather_z_then_y(wire, weights, full_weights, y, z, rest)
    own_y = exchange_y(wire, weights, full_weights, y, z, one)
    columns = ring_z_columns(wire, full_weights, y, z, one)
    chans = gather_chan(wire, resid, full_resid, c, resid.shape[0])
    mixes = gather_mix(wire, w_out, w_head, mix, mix_bufs, y, z, c)
    in_order(own_y, lines, chans, mixes, own_y)
    own_weights.wait()
    in_order(columns, lines, chans, mixes, lines, columns, mixes, lines, chans)
    out_lines[0, y] = w_out[...]
    out_puts = [
        wire.put(w_out, out_lines.at[0, y], seq=lax.rem(y + d, NY) * NZ + z) for d in (1, 3, 2)
    ]
    in_order(columns, lines, mixes, columns, chans, columns, lines, lines)
    own_resid.wait()
    tile = 256
    width = gate.shape[1]
    x, core = c // 2, c % 2

    def project(blocks, first, last):
        def step(at, carry):
            cols = pl.ds(pl.multiple_of(at * tile, tile), tile)
            total = 0.0 if first else acc[cols, :]
            for block in blocks:
                part = full_weights[block // 2, pl.ds((block % 2) * (NZ // 2), NZ // 2)]
                total = total + lax.dot_general(
                    full_resid[block, :, cols],
                    part.reshape(part.shape[0] * part.shape[1], part.shape[2]),
                    BY_ROWS,
                    preferred_element_type=jnp.float32,
                )
            if last:
                gate[cols, :] = total[:, :width].astype(gate.dtype)
                xs[cols, :] = total[:, width:].astype(xs.dtype)
            else:
                acc[cols, :] = total
            return carry

        lax.fori_loop(0, acc.shape[0] // tile, step, 0)

    mate = c + 1 - 2 * core
    left = lax.rem(x + NX - 1, NX) * 2 + core
    right = lax.rem(x + 1, NX) * 2 + core
    for copy in out_puts:
        copy.wait_recv()
    out_puts = [
        wire.put(out_lines.at[0], out_lines.at[1], seq=y * NZ + lax.rem(z + 1, NZ)),
        wire.put(out_lines.at[0], out_lines.at[2], seq=y * NZ + lax.rem(z + NZ - 1, NZ)),
    ]
    project([c, left, right], True, False)
    in_order(chans, chans)
    out = pltpu.make_async_copy(full_resid, features, local.at[1])
    out.start()
    across = lax.rem(x + 2, NX) * 2 + core
    flip = 1 - 2 * core
    project([mate, left + flip, right + flip, across, across + flip], False, True)
    for copy in out_puts:
        copy.wait_recv()
    out.wait()
    wire.finish()


def gather_all(resid, w_gate, w_x, w_out, w_head):
    anywhere = pl.BlockSpec(memory_space=pl.ANY)
    vmem = pl.BlockSpec(memory_space=pltpu.VMEM)
    f32 = jnp.float32
    copies = 96
    block = (VOCAB, 128)
    rows, half = w_gate.shape
    tokens = resid.shape[1]
    return pl.pallas_call(
        gather_kernel,
        name="gather_all",
        out_shape=(
            jax.ShapeDtypeStruct((NCHAN, *resid.shape), resid.dtype),
            jax.ShapeDtypeStruct((tokens, half), resid.dtype),
            jax.ShapeDtypeStruct((tokens, half), resid.dtype),
            jax.ShapeDtypeStruct((3, NY, *w_out.shape), w_out.dtype),
            jax.ShapeDtypeStruct((VOCAB, resid.shape[0]), f32),
        ),
        in_specs=[vmem] * 5,
        out_specs=(anywhere, vmem, vmem, vmem, vmem),
        scratch_shapes=[
            pltpu.VMEM((NCHAN, *resid.shape), resid.dtype),
            pltpu.VMEM((NY, NZ, rows, 2 * half), w_gate.dtype),
            pltpu.VMEM((tokens, 2 * half), f32),
            pltpu.VMEM((rows, 2 * half), w_gate.dtype),
            pltpu.VMEM(block, f32),
            pltpu.VMEM((NCHAN - 1, *block), f32),
            pltpu.VMEM(block, f32),
            pltpu.VMEM((NZ, *block), f32),
            pltpu.VMEM((NY, NZ // 2, *block), f32),
            pltpu.SemaphoreType.DMA((copies,)),
            pltpu.SemaphoreType.DMA((copies,)),
            pltpu.SemaphoreType.DMA((2,)),
        ],
        compiler_params=pltpu.CompilerParams(
            collective_id=0, has_side_effects=True, vmem_limit_bytes=VMEM_BYTES
        ),
        cost_estimate=pl.CostEstimate(flops=10**10, bytes_accessed=10**8, transcendentals=0),
    )(resid, w_gate, w_x, w_out, w_head)


EXACT = lax.Precision.HIGHEST
LANES = 128
EDGE = 16
SUMS = 40
FACTS = 24


def ring_on(wire, lines, full, y, z):
    up, down = y * NZ + lax.rem(z + 1, NZ), y * NZ + lax.rem(z + NZ - 1, NZ)
    plus = wire.put(lines.at[1], full.at[:, lax.rem(z + NZ - 1, NZ)], seq=up)
    minus = wire.put(lines.at[2], full.at[:, lax.rem(z + 1, NZ)], seq=down)
    for step in range(2, NZ // 2):
        yield
        last = step == NZ // 2 - 1
        behind, ahead = lax.rem(z + NZ - step, NZ), lax.rem(z + step, NZ)
        plus.wait_recv()
        moved = full.at[pl.ds(0, NY // 2) if last else slice(None), behind]
        plus = wire.put(moved, moved, seq=up)
        minus.wait_recv()
        moved = full.at[pl.ds(NY // 2, NY // 2) if last else slice(None), ahead]
        minus = wire.put(moved, moved, seq=down)
    yield
    plus.wait_recv()
    minus.wait_recv()


def middle_kernel(
    gate,
    xs,
    resid,
    head_t,
    mix_t,
    conv_weight,
    conv_bias,
    norm_gain,
    skip_d,
    targets,
    out_lines,
    dgate,
    dx,
    small,
    gained,
    facts,
    full_w_out,
    padded,
    prods,
    to_gate,
    to_conv,
    sums,
    parts,
    mine,
    before,
    after,
    acc_rows,
    acc_heads,
    send,
    recv,
    w_send,
    w_recv,
    local,
):
    f32, bf16 = jnp.float32, jnp.bfloat16
    tokens = gate.shape[0]
    y, z, c = place()
    s = y * NZ + z
    last_seq = NY * NZ - 1
    later, sooner = lax.rem(s + 1, NY * NZ), lax.rem(s + last_seq, NY * NZ)
    meet = greet(
        [{"chan": lax.rem(c + d, NCHAN)} for d in range(1, NCHAN)]
        + [{"seq": later}, {"seq": sooner}]
        + [{"seq": y * NZ + lax.rem(z + d, NZ)} for d in (1, NZ - 1)]
    )
    wire = Wire(w_send, w_recv)
    near = (z, lax.rem(z + NZ - 1, NZ), lax.rem(z + 1, NZ))
    own_lines = [
        pltpu.make_async_copy(out_lines.at[at], full_w_out.at[:, near[at]], local.at[at])
        for at in range(3)
    ]
    for copy in own_lines:
        copy.start()
    columns = ring_on(wire, out_lines, full_w_out, y, z)

    def copy_of(source, target, at, where):
        return pltpu.make_async_remote_copy(
            src_ref=source,
            dst_ref=target,
            send_sem=send.at[at],
            recv_sem=recv.at[at],
            device_id=where,
            device_id_type=MESH,
        )

    edge = copy_of(xs.at[pl.ds(tokens - EDGE, EDGE)], before, 2 * NCHAN, {"seq": later})
    taps = [conv_weight[k : k + 1, :] for k in range(KERNEL)]
    bias, gain = conv_bias[...], norm_gain[...]
    head = lax.broadcasted_iota(jnp.int32, bias.shape, 1) // HEADDIM
    skip = jnp.zeros(bias.shape, f32)
    for at in range(skip_d.shape[0]):
        skip = jnp.where(head == at, skip_d[at], skip)
    mix = mix_t[...]
    padded[pl.ds(EDGE, tokens), :] = xs[...].astype(f32)
    meet()
    edge.start()
    in_order(columns)

    def window(tile):
        start = pl.multiple_of(tile * LANES, LANES)
        return pl.ds(start, LANES), padded[pl.ds(start, LANES + EDGE), :]

    def shifted(win, k):
        first = EDGE - (KERNEL - 1) + k
        return win[first : first + LANES]

    def share(step):
        peer = lax.rem(c + 1 + step, NCHAN)
        return copy_of(sums.at[peer], parts.at[step], step, {"chan": peer})

    def forward(tile):
        rows, win = window(tile)
        conv = bias + taps[0] * shifted(win, 0)
        for k in range(1, KERNEL):
            conv = conv + taps[k] * shifted(win, k)
        sig_conv = jax.nn.sigmoid(conv)
        active = conv * sig_conv
        gate_pre = gate[rows, :].astype(f32)
        sig_gate = jax.nn.sigmoid(gate_pre)
        silu_gate = gate_pre * sig_gate
        prod = active * silu_gate
        prods[rows, :] = prod
        to_gate[rows, :] = skip * active * slope(gate_pre, sig_gate)
        to_conv[rows, :] = skip * silu_gate * slope(conv, sig_conv)
        gated = prod * skip
        with_gain = gated * gain
        gained[:, rows] = with_gain.T.astype(bf16)
        by_lanes = (((1,), (1,)), ((), ()))
        sums[tile, pl.ds(0, VOCAB)] = lax.dot_general(
            head_t[...],
            resid[:, rows],
            (((1,), (0,)), ((), ())),
            preferred_element_type=f32,
        )
        sums[tile, pl.ds(VOCAB, VOCAB)] = lax.dot_general(
            mix, with_gain, by_lanes, precision=EXACT, preferred_element_type=f32
        )
        sums[tile, pl.ds(2 * VOCAB, 8)] = lax.dot_general(
            jnp.ones((8, gated.shape[1]), f32),
            gated * gated,
            by_lanes,
            precision=EXACT,
            preferred_element_type=f32,
        )

    edge.wait_recv()
    padded[pl.ds(0, EDGE), :] = before[...].astype(f32) * (s > 0).astype(f32)

    def forward_step(step, carry):
        forward(lax.rem(c + 1 + step, NCHAN))
        share(step).start()
        return carry

    lax.fori_loop(0, NCHAN - 1, forward_step, 0)
    forward(c)
    in_order(columns)
    total = sums[c]
    for step in range(NCHAN - 1):
        share(step).wait_recv()
        total = total + parts[step]
    inverse = lax.rsqrt(total[2 * VOCAB : 2 * VOCAB + 1] / INNER + 1e-05)
    gained_head = total[VOCAB : 2 * VOCAB]
    raised = jnp.exp(total[:VOCAB] + inverse * gained_head)
    probs = raised / jnp.sum(raised, axis=0, keepdims=True)
    words = lax.broadcasted_iota(jnp.int32, (VOCAB, LANES), 0)
    onehot = (words == targets[c]).astype(f32)
    weight = 4.0 / float(tokens * NY * NZ) ** 0.5
    dlogit = (probs - onehot) * weight
    dot_gn = jnp.sum(dlogit * gained_head, axis=0, keepdims=True)
    mine[pl.ds(0, VOCAB), :] = dlogit
    mine[pl.ds(VOCAB, 8), :] = jnp.concatenate(
        [inverse, inverse * inverse * inverse * dot_gn / INNER, jnp.zeros((6, LANES), f32)],
        axis=0,
    )
    facts[c] = mine[...]

    def tell(d):
        return copy_of(
            mine, facts.at[c], NCHAN - 1 + d, {"chan": lax.rem(c + d, NCHAN)}
        )

    for d in range(1, NCHAN):
        tell(d).start()
    acc_rows[...] = jnp.zeros_like(acc_rows)
    acc_heads[...] = jnp.zeros_like(acc_heads)
    for d in range(1, NCHAN):
        tell(d).wait_recv()
    in_order(columns)
    second = (
        lax.broadcasted_iota(jnp.int32, (8, mix.shape[1]), 0) == 1
    ).astype(f32)

    def fold(value):
        return jnp.sum(value.reshape(LANES // 8, 8, value.shape[1]), axis=0)

    def backward(tile):
        rows, win = window(tile)
        fact = facts[tile]
        dlogit = fact[:VOCAB]
        scaled = dlogit * fact[VOCAB : VOCAB + 1]
        by_rows = (((0,), (0,)), ((), ()))
        dnormed = lax.dot_general(
            scaled, mix, by_rows, precision=EXACT, preferred_element_type=f32
        )
        pull = lax.dot_general(
            fact[VOCAB : VOCAB + 8], second, by_rows, precision=EXACT, preferred_element_type=f32
        )
        prod = prods[rows, :]
        dgated = gain * dnormed - skip * prod * pull
        dgate[rows, :] = (dgated * to_gate[rows, :]).astype(bf16)
        dconv = dgated * to_conv[rows, :]
        to_conv[rows, :] = dconv
        for k in range(KERNEL):
            acc_rows[k] += fold(dconv * shifted(win, k))
        acc_rows[KERNEL] += fold(dconv)
        acc_rows[KERNEL + 1] += fold(dgated * prod)
        acc_heads[0] += jnp.dot(scaled, prod, precision=EXACT, preferred_element_type=f32)
        acc_heads[1] += lax.dot_general(
            dlogit,
            resid[:, rows].astype(f32),
            (((1,), (1,)), ((), ())),
            precision=EXACT,
            preferred_element_type=f32,
        )

    backward(0)
    first_rows = copy_of(to_conv.at[pl.ds(0, 8)], after, 2 * NCHAN + 1, {"seq": sooner})
    first_rows.start()

    def backward_step(tile, carry):
        backward(tile)
        return carry

    lax.fori_loop(1, tokens // LANES, backward_step, 0)
    by_channel = acc_heads[0]
    small[pl.ds(0, VOCAB), :] = by_channel * skip * gain
    small[pl.ds(VOCAB, VOCAB), :] = acc_heads[1]
    lines = [jnp.sum(acc_rows[k], axis=0, keepdims=True) for k in range(KERNEL + 2)]
    lines.insert(KERNEL + 1, skip * jnp.sum(mix * by_channel, axis=0, keepdims=True))
    lines.append(jnp.zeros_like(skip))
    small[pl.ds(2 * VOCAB, 8), :] = jnp.concatenate(lines, axis=0)
    first_rows.wait_recv()
    to_conv[pl.ds(tokens, 8), :] = after[...] * (s < last_seq).astype(f32)

    def spread_step(tile, carry):
        start = pl.multiple_of(tile * LANES, LANES)
        win = to_conv[pl.ds(start, LANES + 8), :]
        acc = taps[KERNEL - 1] * win[0:LANES]
        for k in range(KERNEL - 1):
            acc = acc + taps[k] * win[KERNEL - 1 - k : KERNEL - 1 - k + LANES]
        dx[pl.ds(start, LANES), :] = acc.astype(bf16)
        return carry

    lax.fori_loop(0, tokens // LANES, spread_step, 0)
    in_order(columns)
    wire.finish()
    for copy in own_lines:
        copy.wait()
    edge.wait_send()
    first_rows.wait_send()
    for d in range(1, NCHAN):
        share(d - 1).wait_send()
        tell(d).wait_send()


def middle(gate, xs, *others):
    f32, bf16 = jnp.float32, jnp.bfloat16
    vmem = pl.BlockSpec(memory_space=pltpu.VMEM)
    anywhere = pl.BlockSpec(memory_space=pl.ANY)
    tokens, width = gate.shape
    copies = 2 * NCHAN + 2
    return pl.pallas_call(
        middle_kernel,
        name="middle",
        out_shape=(
            jax.ShapeDtypeStruct((tokens, width), bf16),
            jax.ShapeDtypeStruct((tokens, width), bf16),
            jax.ShapeDtypeStruct((SUMS, width), f32),
            jax.ShapeDtypeStruct((width, tokens), bf16),
            jax.ShapeDtypeStruct((NCHAN, FACTS, LANES), f32),
            jax.ShapeDtypeStruct((NY, NZ, *others[-1].shape[2:]), bf16),
        ),
        in_specs=[vmem] * 8 + [pl.BlockSpec(memory_space=pltpu.SMEM), vmem, anywhere],
        out_specs=(vmem,) * 5 + (anywhere,),
        scratch_shapes=[
            pltpu.VMEM((tokens + EDGE, width), f32),
            pltpu.VMEM((tokens, width), f32),
            pltpu.VMEM((tokens, width), f32),
            pltpu.VMEM((tokens + 8, width), f32),
            pltpu.VMEM((NCHAN, SUMS, LANES), f32),
            pltpu.VMEM((NCHAN - 1, SUMS, LANES), f32),
            pltpu.VMEM((FACTS, LANES), f32),
            pltpu.VMEM((EDGE, width), bf16),
            pltpu.VMEM((8, width), f32),
            pltpu.VMEM((KERNEL + 2, 8, width), f32),
            pltpu.VMEM((2, VOCAB, width), f32),
            pltpu.SemaphoreType.DMA((copies,)),
            pltpu.SemaphoreType.DMA((copies,)),
            pltpu.SemaphoreType.DMA((NZ,)),
            pltpu.SemaphoreType.DMA((NZ,)),
            pltpu.SemaphoreType.DMA((3,)),
        ],
        compiler_params=pltpu.CompilerParams(
            collective_id=1, has_side_effects=True, vmem_limit_bytes=VMEM_BYTES
        ),
        cost_estimate=pl.CostEstimate(flops=10**10, bytes_accessed=10**7, transcendentals=0),
    )(gate, xs, *others)


def scatter_seq(wire, grads, ready, bufs, outs, y, z, start, count):
    f32, bf16 = jnp.float32, jnp.bfloat16
    from_below, from_above, via_up, via_down, got_below, got_above, lines, got_z = bufs
    rows = pl.ds(start, count)
    lo, hi = pl.ds(0, NZ // 2), pl.ds(NZ // 2, NZ // 2)
    above, below, across = lax.rem(y + 1, NY), lax.rem(y + 3, NY), lax.rem(y + 2, NY)
    up, down = above * NZ + z, below * NZ + z
    ready(2 * across)
    half_up = wire.put(grads.at[across, lo, rows], from_below.at[:, rows], seq=up)
    ready(2 * across + 1)
    half_down = wire.put(grads.at[across, hi, rows], from_above.at[:, rows], seq=down)
    ready(2 * above + 1)
    moves = [wire.put(grads.at[above, hi, rows], got_below.at[hi, rows], seq=up)]
    ready(2 * below)
    moves.append(wire.put(grads.at[below, lo, rows], got_above.at[lo, rows], seq=down))
    ready(2 * above)
    ready(2 * below + 1)
    yield
    half_up.wait_recv()
    via_up[:, rows] = (
        grads[above, lo, rows].astype(f32) + from_below[:, rows].astype(f32)
    ).astype(bf16)
    moves.append(wire.put(via_up.at[:, rows], got_below.at[lo, rows], seq=up))
    half_down.wait_recv()
    via_down[:, rows] = (
        grads[below, hi, rows].astype(f32) + from_above[:, rows].astype(f32)
    ).astype(bf16)
    moves.append(wire.put(via_down.at[:, rows], got_above.at[hi, rows], seq=down))
    ready(2 * y)
    ready(2 * y + 1)
    yield
    for copy in moves[:2]:
        copy.wait_recv()
    yield
    for copy in moves[2:]:
        copy.wait_recv()
    lines[:, rows] = (
        grads[y, :, rows].astype(f32)
        + got_below[:, rows].astype(f32)
        + got_above[:, rows].astype(f32)
    ).astype(bf16)
    puts = []
    for d in (4, 3, 5, 2, 6, 1, 7):
        peer = lax.rem(z + d, NZ)
        puts.append(wire.put(lines.at[peer, rows], got_z.at[d - 1, rows], seq=y * NZ + peer))
    yield
    acc = (
        grads[y, z, rows].astype(f32)
        + got_below[z, rows].astype(f32)
        + got_above[z, rows].astype(f32)
    )
    for copy in puts:
        copy.wait_recv()
    for d in range(1, NZ):
        acc = acc + got_z[d - 1, rows].astype(f32)
    half = acc.shape[1] // 2
    outs[0][rows] = acc[:, :half]
    outs[1][rows] = acc[:, half:]


def sum_small(wire, small, got_y, part, got_z, mine, sums, total, heads, y, z, c):
    puts = [
        wire.put(small, got_y.at[y], seq=lax.rem(y + d, NY) * NZ + z) for d in range(1, NY)
    ]
    got_y[y] = small[...]
    yield
    for copy in puts:
        copy.wait_recv()
    acc = got_y[0]
    for at in range(1, NY):
        acc = acc + got_y[at]
    used = small.shape[0] // 8
    for at in range(NZ):
        lines = acc[8 * at : 8 * at + 8] if at < used else jnp.zeros_like(acc[:8])
        part[at] = lines
    puts = []
    for d in range(1, NZ):
        peer = lax.rem(z + d, NZ)
        puts.append(wire.put(part.at[peer], got_z.at[z], seq=y * NZ + peer))
    got_z[z] = part[z]
    yield
    for copy in puts:
        copy.wait_recv()
    acc = got_z[0]
    for at in range(1, NZ):
        acc = acc + got_z[at]
    mine[...] = acc
    puts = [
        wire.put(mine, sums.at[z], seq=y * NZ + lax.rem(z + d, NZ)) for d in range(1, NZ)
    ]
    sums[z] = acc
    yield
    for copy in puts:
        copy.wait_recv()
    for at in range(used):
        total[pl.ds(8 * at, 8), :] = sums[at]
    first = pl.ds(0, VOCAB)
    puts = [
        wire.put(total.at[first], heads.at[c], chan=lax.rem(c + d, NCHAN))
        for d in range(1, NCHAN)
    ]
    heads[c] = total[first]
    yield
    for copy in puts:
        copy.wait_recv()


def grads_kernel(
    features,
    dgate,
    dx,
    small,
    gained,
    w_out,
    resid,
    facts,
    head_t,
    grad_gate,
    grad_x,
    total,
    grad_out,
    grad_head,
    new_resid,
    *scratch,
):
    f32, bf16 = jnp.float32, jnp.bfloat16
    feats, both, grads, full_gained, out_cols, heads, back, *rest = scratch
    *bufs, small_y, small_part, small_z, small_mine, small_sums, send, recv, local = rest
    y, z, c = place()
    width = dgate.shape[1]
    meet = greet(
        [{"chan": lax.rem(c + d, NCHAN)} for d in range(1, NCHAN)]
        + [{"seq": lax.rem(y + d, NY) * NZ + z} for d in range(1, NY)]
        + [{"seq": y * NZ + lax.rem(z + d, NZ)} for d in range(1, NZ)]
    )
    order = [
        2 * lax.rem(y + 2, NY),
        2 * lax.rem(y + 2, NY) + 1,
        2 * lax.rem(y + 1, NY) + 1,
        2 * lax.rem(y + 3, NY),
        2 * lax.rem(y + 1, NY),
        2 * lax.rem(y + 3, NY) + 1,
        2 * y,
        2 * y + 1,
    ]
    loads = [
        pltpu.make_async_copy(features.at[at], feats.at[step], local.at[step])
        for step, at in enumerate(order)
    ]
    for load in loads:
        load.start()
    own = pltpu.make_async_copy(gained, full_gained.at[c], local.at[NCHAN])
    own.start()
    weights = pltpu.make_async_copy(w_out, out_cols, local.at[NCHAN + 1])
    weights.start()
    both[:, pl.ds(0, width)] = dgate[...]
    both[:, pl.ds(width, width)] = dx[...]
    wire = Wire(send, recv)
    steps = []

    def compute(step):
        loads[step].wait()
        product = jnp.dot(feats[step], both[...], preferred_element_type=f32)
        lines = product.reshape(NZ // 2, product.shape[0] // (NZ // 2), product.shape[1])
        block = order[step]
        first = lax.rem(block, 2) * (NZ // 2)
        grads[block // 2, pl.ds(first, NZ // 2)] = lines.astype(bf16)

    def ready(block):
        steps.append(block)
        if len(steps) > 2:
            compute(len(steps) - 1)

    compute(0)
    compute(1)
    meet()
    rows = grad_gate.shape[0]
    outs = (grad_gate, grad_x)
    small_bufs = (small_y, small_part, small_z, small_mine, small_sums)
    smalls = sum_small(wire, small, *small_bufs, total, heads, y, z, c)
    one = scatter_seq(wire, grads, ready, bufs, outs, y, z, 0, 32)
    two = scatter_seq(wire, grads, lambda block: None, bufs, outs, y, z, 32, 32)
    three = scatter_seq(wire, grads, lambda block: None, bufs, outs, y, z, 64, rows - 64)
    chans = gather_chan(wire, gained, full_gained, c, gained.shape[0])
    in_order(smalls, chans, one, chans, smalls, one, chans, smalls, one, two, one, chans, two)
    in_order(smalls, two, three, two, chans)
    own.wait()
    weights.wait()
    x, core = c // 2, c % 2
    near = [2 * lax.rem(x + d, NX) + core for d in range(NX)]

    def project_back(blocks, last):
        def step(at, carry):
            cols = pl.ds(pl.multiple_of(at * 256, 256), 256)
            acc = back[:, cols] if last else 0.0
            for block in blocks:
                acc = acc + lax.dot_general(
                    out_cols[block],
                    full_gained[block, :, cols],
                    BY_ROWS,
                    preferred_element_type=f32,
                )
            if not last:
                back[:, cols] = acc
                return carry
            for part in range(2):
                tile = 2 * at + part
                lanes = pl.ds(pl.multiple_of(tile * LANES, LANES), LANES)
                scale = facts[tile, VOCAB : VOCAB + 1]
                scaled = scale * acc[:, part * LANES : (part + 1) * LANES]
                new_resid[:, lanes] = (resid[:, lanes].astype(f32) + scaled).astype(bf16)
            return carry

        lax.fori_loop(0, new_resid.shape[1] // 256, step, 0)

    project_back(near, False)
    in_order(three, three, three, smalls, chans)
    project_back([block + 1 - 2 * core for block in near], True)
    acc = 0.0
    for at in range(NCHAN):
        head = heads[at]
        high = head.astype(bf16)
        low = (head - high.astype(f32)).astype(bf16)
        acc = acc + jnp.dot(
            jnp.concatenate([high, low], axis=0),
            out_cols[at],
            preferred_element_type=f32,
        )
    grad_head[...] = total[pl.ds(VOCAB, VOCAB), :] + acc[:VOCAB] + acc[VOCAB:]
    s = y * NZ + z
    per_chan = width // rows
    mine = heads[s // per_chan]
    here = jnp.zeros((VOCAB, rows), f32)
    for at in range(per_chan):
        chosen = (lax.rem(s, per_chan) == at).astype(f32)
        here = here + chosen * mine[:, at * rows : (at + 1) * rows]
    grad_out[...] = lax.dot_general(
        here, head_t[...].astype(f32), BY_ROWS, precision=EXACT, preferred_element_type=f32
    )
    in_order(one, two, three)
    wire.finish()


def finish_grads(features, dgate, dx, small, gained, w_out, resid, facts, head_t):
    f32, bf16 = jnp.float32, jnp.bfloat16
    anywhere = pl.BlockSpec(memory_space=pl.ANY)
    vmem = pl.BlockSpec(memory_space=pltpu.VMEM)
    tokens, width = dgate.shape
    rows = INNER // (NY * NZ)
    copies = 80
    cols = 2 * width
    half = (NZ // 2, rows, cols)
    line = (NZ, rows, cols)
    block = jax.ShapeDtypeStruct((rows, width), f32)
    return pl.pallas_call(
        grads_kernel,
        name="finish_grads",
        out_shape=(
            block,
            block,
            jax.ShapeDtypeStruct(small.shape, f32),
            block,
            jax.ShapeDtypeStruct((VOCAB, width), f32),
            jax.ShapeDtypeStruct(resid.shape, bf16),
        ),
        in_specs=[anywhere, vmem, vmem, vmem, anywhere, anywhere, vmem, vmem, vmem],
        out_specs=(vmem,) * 6,
        scratch_shapes=[
            pltpu.VMEM(features.shape, bf16),
            pltpu.VMEM((tokens, cols), bf16),
            pltpu.VMEM((NY, NZ, rows, cols), bf16),
            pltpu.VMEM((NCHAN, *gained.shape), bf16),
            pltpu.VMEM(w_out.shape, bf16),
            pltpu.VMEM((NCHAN, VOCAB, width), f32),
            pltpu.VMEM(resid.shape, f32),
        ]
        + [pltpu.VMEM(half, bf16)] * 4
        + [pltpu.VMEM(line, bf16)] * 3
        + [
            pltpu.VMEM((NZ - 1, rows, cols), bf16),
            pltpu.VMEM((NY, *small.shape), f32),
            pltpu.VMEM((NZ, 8, width), f32),
            pltpu.VMEM((NZ, 8, width), f32),
            pltpu.VMEM((8, width), f32),
            pltpu.VMEM((NZ, 8, width), f32),
            pltpu.SemaphoreType.DMA((copies,)),
            pltpu.SemaphoreType.DMA((copies,)),
            pltpu.SemaphoreType.DMA((NCHAN + 2,)),
        ],
        compiler_params=pltpu.CompilerParams(
            collective_id=2, has_side_effects=True, vmem_limit_bytes=VMEM_BYTES
        ),
        cost_estimate=pl.CostEstimate(flops=10**10, bytes_accessed=10**8, transcendentals=0),
    )(features, dgate, dx, small, gained, w_out, resid, facts, head_t)


BY_ROWS = (((0,), (0,)), ((), ()))


def hand_out_kernel(total, *refs):
    count = len(refs) // 2
    for at in range(count):
        refs[at + count][...] = refs[at][...]
    refs[-1][...] = total[pl.ds(2 * VOCAB, KERNEL), :]


def hand_out(total, *arrays):
    vmem = pl.BlockSpec(memory_space=pltpu.VMEM)
    shapes = [jax.ShapeDtypeStruct(array.shape, array.dtype) for array in arrays]
    shapes.append(jax.ShapeDtypeStruct((KERNEL, total.shape[1]), total.dtype))
    return pl.pallas_call(
        hand_out_kernel,
        name="hand_out",
        out_shape=tuple(shapes),
        in_specs=[vmem] * (len(arrays) + 1),
        out_specs=(vmem,) * len(shapes),
        compiler_params=pltpu.CompilerParams(vmem_limit_bytes=VMEM_BYTES),
    )(total, *arrays)


def slope(value, sig):
    return sig * (1.0 + value * (1.0 - sig))


def per_device(
    targets, resid, w_gate_in, w_x_in, conv_weight, conv_bias, skip_d, norm_gain, w_out, w_head
):
    f32 = jnp.float32
    local_inner = w_gate_in.shape[1]
    head_t, resid_t = w_head.T, resid.T
    features, gate_pre, x_pre, out_lines, mix_t = gather_all(
        resid_t, w_gate_in, w_x_in, w_out, head_t
    )
    dgate, dx_pre, small, gained, facts, out_cols = middle(
        gate_pre,
        x_pre,
        resid_t,
        head_t,
        mix_t,
        conv_weight,
        conv_bias[None],
        norm_gain[None],
        skip_d,
        targets.reshape(NCHAN, 1, LANES),
        out_lines,
    )
    grad_gate_in, grad_x_in, total, *others = finish_grads(
        features,
        dgate,
        dx_pre,
        small,
        gained,
        out_cols.reshape(NCHAN, local_inner, local_inner),
        resid_t,
        facts,
        head_t,
    )
    grad_gate_in, grad_x_in, grad_out, grad_head_t, new_resid_t, grad_conv_weight = hand_out(
        total, grad_gate_in, grad_x_in, *others
    )
    at = 2 * VOCAB
    grad_conv_bias = total[at + KERNEL]
    grad_gain = total[at + KERNEL + 1]
    grad_skip = total[at + KERNEL + 2].reshape(-1, HEADDIM).sum(axis=1)
    return (
        new_resid_t.T,
        grad_gate_in,
        grad_x_in,
        grad_out,
        grad_head_t.T,
        grad_conv_weight,
        grad_conv_bias,
        grad_skip,
        grad_gain,
    )


def solution(mesh):
    return jax.shard_map(
        per_device,
        mesh=mesh,
        in_specs=(
            P("seq"),
            P("seq", "chan"),
            P("seq", "chan"),
            P("seq", "chan"),
            P(None, "chan"),
            P("chan"),
            P("chan"),
            P("chan"),
            P("seq", "chan"),
            P("chan", None),
        ),
        out_specs=(
            P("seq", "chan"),
            P("seq", "chan"),
            P("seq", "chan"),
            P("seq", "chan"),
            P("chan", None),
            P(None, "chan"),
            P("chan"),
            P("chan"),
            P("chan"),
        ),
        check_vma=False,
    )
```
